32 devices in a mesh: wide: 8 (over z, x), narrow: 4 (over y, core).
Axes of the slice: x: 2, y: 2, z: 4, core: 2. Of those that a mesh axis runs over, the one named last changes fastest.
Arguments:
- block_source: bfloat16 [64, 576, 384], P(('wide', 'narrow')), may hold values from -6 to 6
- upstream_adjoint: bfloat16 [64, 576, 384], P(('wide', 'narrow')), may hold values from -6 to 6
- picture_patch_extents: int32 [64, 2], P(('wide', 'narrow')), may hold values from 18 to 24, as said below
- triple_matrix: float32 [384, 1152], replicated, may hold values from -0.3125 to 0.3125
- mixer_matrix: float32 [384, 384], replicated, may hold values from -1.25 to 1.25
- expand_matrix: float32 [384, 1536], replicated, may hold values from -0.3125 to 0.3125
- shrink_matrix: float32 [1536, 384], replicated, may hold values from -0.15625 to 0.15625
- affine_entries: float32 [40, 384], replicated, may hold values from -2 to 2
- sharpness: float32 [8], replicated, may hold values from 10 to 30
- triple_velocity: float32 [384, 1152], P(None, 'narrow'), may hold values from -100 to 100
- mixer_velocity: float32 [384, 384], P('narrow'), may hold values from -300 to 300
- expand_velocity: float32 [384, 1536], P(None, 'narrow'), may hold values from -500 to 500
- shrink_velocity: float32 [1536, 384], P('narrow'), may hold values from -500 to 500
- affine_velocity: float32 [40, 384], replicated, may hold values from -300 to 300
- sharpness_velocity: float32 [8], replicated, may hold values from -8 to 8
Outputs:
- block_out: bfloat16 [64, 576, 384], P(('wide', 'narrow'))
- incoming_adjoint: float32 [64, 576, 384], P(('wide', 'narrow'))
- triple_matrix_adjoint: float32 [384, 1152], P(None, 'narrow')
- mixer_matrix_adjoint: float32 [384, 384], P('narrow')
- expand_matrix_adjoint: float32 [384, 1536], P(None, 'narrow')
- shrink_matrix_adjoint: float32 [1536, 384], P('narrow')
- affine_entries_adjoint: float32 [40, 384], replicated
- sharpness_adjoint: float32 [8], replicated
- revised_triple_matrix: float32 [384, 1152], P(None, 'narrow')
- revised_mixer_matrix: float32 [384, 384], P('narrow')
- revised_expand_matrix: float32 [384, 1536], P(None, 'narrow')
- revised_shrink_matrix: float32 [1536, 384], P('narrow')
- renewed_triple_velocity: float32 [384, 1152], P(None, 'narrow')
- renewed_mixer_velocity: float32 [384, 384], P('narrow')
- renewed_expand_velocity: float32 [384, 1536], P(None, 'narrow')
- renewed_shrink_velocity: float32 [1536, 384], P('narrow')
- copy_qkv: bfloat16 [384, 1152], P(None, 'narrow')
- copy_proj: bfloat16 [384, 384], P('narrow')
- copy_fc1: bfloat16 [384, 1536], P(None, 'narrow')
- copy_fc2: bfloat16 [1536, 384], P('narrow')
- revised_affine_entries: float32 [40, 384], replicated
- renewed_affine_velocity: float32 [40, 384], replicated
- revised_sharpness: float32 [8], replicated
- renewed_sharpness_velocity: float32 [8], replicated
The draws below stay inside these ranges and needn't reach their ends.
Inputs may be any that keep to these rules, and one draw needn't show every extreme that they name: Image i holds real patches in the top-left picture_patch_extents[i, 0] x picture_patch_extents[i, 1] block of its 24 x 24 slots; some image fills all its slots in every draw.
All inputs are finite; a program needn't handle non-finite values.
Results may differ from the reference program's by a relative error of at most 0.006.
The reference program's roundings to bfloat16 on the way count: a program that leaves them out, or rounds other values in their place, can miss the bound.
Values sent between devices are 32-bit elements; how exact they have to be, the bound alone decides.
No kernel may reach another device: no remote copies, remote signals or barrier semaphores. Data moves between devices by JAX's collectives and lax.ppermute only.
A program may use at most 128 MiB of HBM per device.

```python
import math
from functools import partial
import jax
import jax.numpy as jnp
from jax import lax

D = 384
ATTN_GROUPS = 8
HEAD = 48
FF = 1536
GRID = 24
NS_STEPS = 5
SMALL_ROWS = 40
IMG_DEV = 2
SLOTS = 576
IMAGES = 64


def state_values(key, dims, spread):
    drawn = jnp.clip(jax.random.normal(key, dims, jnp.float32), -4.0, 4.0)
    return drawn * spread


def draw_picture_patch_extents(key, part):
    sides = jax.random.randint(key, (IMAGES, 2), 3 * GRID // 4, GRID + 1, jnp.int32)
    chosen = jax.random.randint(jax.random.fold_in(key, 7), (), 0, IMAGES, jnp.int32)
    filled = (jnp.arange(IMAGES, dtype=jnp.int32) == chosen)[:, None]
    return jnp.where(filled, GRID, sides)


def draw_affine_entries(key, part):
    row_index = jnp.arange(SMALL_ROWS, dtype=jnp.int32)[:, None]
    gain_rows = (row_index == 0) | (row_index == 7) | (row_index == 19) | (row_index == 32)
    scale_rows = (row_index == 6) | (row_index == 31) | (row_index == 39)
    kernel_rows = (row_index >= 9) & (row_index <= 17) | (row_index >= 21) & (row_index <= 29)
    normal_part = jnp.clip(jax.random.normal(jax.random.fold_in(key, 1), (SMALL_ROWS, D), jnp.float32), -4.0, 4.0)
    gain_draw = jax.random.uniform(jax.random.fold_in(key, 2), (SMALL_ROWS, D), jnp.float32, 0.6, 1.4)
    scale_draw = jax.random.uniform(jax.random.fold_in(key, 3), (SMALL_ROWS, D), jnp.float32, 0.5, 1.5)
    return jnp.where(gain_rows, gain_draw, jnp.where(scale_rows, scale_draw, jnp.where(kernel_rows, 0.35 * normal_part, 0.3 * normal_part)))


def draw_triple_velocity(key, part):
    return state_values(key, (D, 3 * D), 25.0)


def draw_mixer_velocity(key, part):
    return state_values(key, (D, D), 75.0)


def draw_expand_velocity(key, part):
    return state_values(key, (D, FF), 125.0)


def draw_shrink_velocity(key, part):
    return state_values(key, (FF, D), 125.0)


def draw_affine_velocity(key, part):
    return state_values(key, (SMALL_ROWS, D), 75.0)


def draw_sharpness_velocity(key, part):
    return state_values(key, (ATTN_GROUPS,), 2.0)


def levels(stream_key, extent, shards, low, top_value):
    loudness, own = 1.0, jax.random.fold_in(stream_key, 6)
    for dim, parts in shards:
        steps = jnp.exp(jax.random.uniform(jax.random.fold_in(own, dim), (parts,), jnp.float32, low / len(shards), top_value / len(shards)))
        loudness = loudness * jnp.repeat(steps, extent[dim] // parts).reshape([-1 if axis == dim else 1 for axis in range(len(extent))])
    return loudness


def normal_values(own_key, extent, deviation, reach, shards=(), held_as=jnp.bfloat16):
    factor_of = levels(own_key, extent, shards, -0.22, 0.18) if shards else 1.0
    values = jax.random.normal(own_key, extent, jnp.float32) * deviation * factor_of
    return jnp.minimum(jnp.maximum(values, -reach), reach).astype(held_as)


def setup_inputs(seed: int = 0) -> dict:
    splits = jax.random.split(jax.random.key(seed), 16)
    block_source = normal_values(splits[0], (IMAGES, SLOTS, D), 1.0, 6.0, ((0, 32),))
    upstream_adjoint = normal_values(splits[1], (IMAGES, SLOTS, D), 1.0, 6.0, ((0, 32),))
    picture_patch_extents = draw_picture_patch_extents(jax.random.fold_in(splits[15], 71), 0)
    triple_matrix = normal_values(splits[3], (D, 3 * D), D ** -0.5, 0.3125, (), jnp.float32)
    mixer_matrix = normal_values(splits[4], (D, D), (D // 16) ** -0.5, 1.25, (), jnp.float32)
    expand_matrix = normal_values(splits[5], (D, FF), D ** -0.5, 0.3125, (), jnp.float32)
    shrink_matrix = normal_values(splits[6], (FF, D), FF ** -0.5, 0.15625, (), jnp.float32)
    affine_entries = draw_affine_entries(jax.random.fold_in(splits[15], 71), 0)
    sharpness = jnp.clip(jnp.exp(jax.random.uniform(splits[8], (ATTN_GROUPS,), jnp.float32, math.log(10.0), math.log(30.0))), 10.0, 30.0)
    triple_velocity = draw_triple_velocity(jax.random.fold_in(splits[15], 71), 0)
    mixer_velocity = draw_mixer_velocity(jax.random.fold_in(splits[15], 71), 0)
    expand_velocity = draw_expand_velocity(jax.random.fold_in(splits[15], 71), 0)
    shrink_velocity = draw_shrink_velocity(jax.random.fold_in(splits[15], 71), 0)
    affine_velocity = draw_affine_velocity(jax.random.fold_in(splits[15], 71), 0)
    sharpness_velocity = draw_sharpness_velocity(jax.random.fold_in(splits[15], 71), 0)
    return dict(block_source=block_source, upstream_adjoint=upstream_adjoint, picture_patch_extents=picture_patch_extents, triple_matrix=triple_matrix, mixer_matrix=mixer_matrix, expand_matrix=expand_matrix, shrink_matrix=shrink_matrix, affine_entries=affine_entries, sharpness=sharpness, triple_velocity=triple_velocity, mixer_velocity=mixer_velocity, expand_velocity=expand_velocity, shrink_velocity=shrink_velocity, affine_velocity=affine_velocity, sharpness_velocity=sharpness_velocity)


@jax.custom_vjp
def low(v):
    return lax.optimization_barrier(v.astype(jnp.bfloat16)).astype(jnp.float32)

@jax.custom_vjp
def low_back(v):
    return v

def low_keep(v):
    return (low(v), None)

def low_pass(kept, grad):
    return (grad,)

def back_keep(v):
    return (v, None)

def back_low(kept, grad):
    return (low(grad),)
low.defvjp(low_keep, low_pass)
low_back.defvjp(back_keep, back_low)
highest = lax.Precision.HIGHEST
layer_eps = 1e-06
unit_eps = 1e-06
batch_eps = 1e-05
frob_eps = 1e-07
velocity_damping = 0.5
rate_matrix = 0.25
affine_step_size = 0.2
coef_first = 3.4445
coef_second = -4.775
coef_third = 2.0315

def layer_norm(source, gain_row, bias_row):
    centre = source - lax.optimization_barrier(jnp.mean(source, axis=-1, keepdims=True))
    return centre * lax.rsqrt(lax.optimization_barrier(jnp.mean(centre * centre, axis=-1, keepdims=True)) + layer_eps) * gain_row + bias_row

def gelu_exact(source):
    return 0.5 * source * (1.0 + lax.erf(source * 0.7071067811865476))

def depthwise(source, kernel):
    padded = jnp.pad(source, ((0, 0), (1, 1), (1, 1), (0, 0)))
    summed = jnp.zeros_like(source)
    for offset in range(9):
        summed = summed + padded[:, offset // 3:offset // 3 + GRID, offset % 3:offset % 3 + GRID, :] * kernel[offset]
    return summed

def unit_rows(source):
    return source * lax.rsqrt(lax.optimization_barrier(jnp.sum(source * source, axis=1, keepdims=True)) + unit_eps)

def valid_mask(picture_patch_extents):
    position = jnp.arange(SLOTS, dtype=jnp.int32)
    rows_ok = (position // GRID)[None, :] < picture_patch_extents[:, 0:1]
    cols_ok = (position % GRID)[None, :] < picture_patch_extents[:, 1:2]
    return (rows_ok & cols_ok).astype(jnp.float32)

def front_portion(model_entries_nested, incoming_patches, interior_patches):
    triple_matrix, mixer_matrix, affine_entries, sharpness = model_entries_nested
    inside_col = interior_patches[:, :, None]
    images = incoming_patches.shape[0]
    head_shape = (images, SLOTS, ATTN_GROUPS, HEAD)
    normed = low(layer_norm(incoming_patches, affine_entries[0], affine_entries[1]))
    joined = low_back(jnp.einsum('gsk,ke->gse', normed, triple_matrix, precision=highest) + affine_entries[2:5].reshape(-1))
    query_unit = unit_rows(joined[:, :, :D] * inside_col)
    key_unit = unit_rows(joined[:, :, D:2 * D] * inside_col)
    feature_crosscov = jnp.einsum('gshi,gshj->ghij', query_unit.reshape(head_shape), key_unit.reshape(head_shape), precision=highest)
    mix_patches = jax.nn.softmax(feature_crosscov * sharpness[None, :, None, None], axis=-1)
    mixing = jnp.einsum('ghij,gshj->gshi', mix_patches, joined[:, :, 2 * D:].reshape(head_shape), precision=highest).reshape(incoming_patches.shape)
    branch = low_back(jnp.einsum('gsk,ke->gse', low(mixing), mixer_matrix, precision=highest) + affine_entries[5])
    after_mix = incoming_patches + inside_col * affine_entries[6] * branch
    local_in = layer_norm(after_mix, affine_entries[7], affine_entries[8]) * inside_col
    conv_out = depthwise(local_in.reshape(images, GRID, GRID, D), affine_entries[9:18]).reshape(incoming_patches.shape) + affine_entries[18]
    return (after_mix, gelu_exact(conv_out))

def second_half(model_entries_nested, after_mix, activated, interior_patches, centre_mean, inverse_std):
    expand_matrix, shrink_matrix, affine_entries = model_entries_nested
    inside_col = interior_patches[:, :, None]
    images = after_mix.shape[0]
    normal_bn = ((activated - centre_mean) * inverse_std * affine_entries[19] + affine_entries[20]) * inside_col
    conv_out = depthwise(normal_bn.reshape(images, GRID, GRID, D), affine_entries[21:30]).reshape(after_mix.shape) + affine_entries[30]
    after_local = after_mix + inside_col * affine_entries[31] * conv_out
    normed = low(layer_norm(after_local, affine_entries[32], affine_entries[33]))
    hidden = low_back(jnp.einsum('gsk,kf->gsf', normed, expand_matrix, precision=highest) + affine_entries[34:38].reshape(-1))
    branch = low_back(jnp.einsum('gsf,fk->gsk', low(gelu_exact(hidden)), shrink_matrix, precision=highest) + affine_entries[38])
    return after_local + inside_col * affine_entries[39] * branch

def entire_evaluation(incoming_patches, triple_matrix, mixer_matrix, expand_matrix, shrink_matrix, affine_entries, sharpness, interior_patches):
    asker_lowprec = low(triple_matrix)
    attention_weights_lowprec = low(mixer_matrix)
    one_low = low(expand_matrix)
    two_low = low(shrink_matrix)
    groups = IMAGES // IMG_DEV
    grouped = incoming_patches.reshape(groups, IMG_DEV, SLOTS, D)
    mask_groups = interior_patches.reshape(groups, IMG_DEV, SLOTS)

    def section_one(bundled_optimizer_buffers):
        return front_portion((asker_lowprec, attention_weights_lowprec, affine_entries, sharpness), bundled_optimizer_buffers[0], bundled_optimizer_buffers[1])
    after_mix, activated = lax.map(jax.checkpoint(section_one), (grouped, mask_groups))
    genuine_patch_tally = jnp.sum(interior_patches)
    weight_in = mask_groups[..., None]
    centre_mean = lax.optimization_barrier(jnp.sum(activated * weight_in, axis=(0, 1, 2))) / genuine_patch_tally
    spread = (activated - centre_mean) * weight_in
    inverse_std = lax.rsqrt(lax.optimization_barrier(jnp.sum(spread * spread, axis=(0, 1, 2))) / genuine_patch_tally + batch_eps)

    def section_two(bundled_optimizer_buffers):
        return second_half((one_low, two_low, affine_entries), bundled_optimizer_buffers[0], bundled_optimizer_buffers[1], bundled_optimizer_buffers[2], centre_mean, inverse_std)
    result = lax.map(jax.checkpoint(section_two), (after_mix, activated, mask_groups))
    return result.reshape(IMAGES, SLOTS, D)

def orthogonal(matrix):
    is_tall = matrix.shape[0] >= matrix.shape[1]
    source = matrix / (jnp.sqrt(jnp.sum(matrix * matrix)) + frob_eps)
    for sweep_index in range(NS_STEPS):
        if is_tall:
            gram_now = jnp.dot(source.T, source, precision=highest)
            polynomial = coef_second * gram_now + coef_third * jnp.dot(gram_now, gram_now, precision=highest)
            source = coef_first * source + jnp.dot(source, polynomial, precision=highest)
        else:
            gram_now = jnp.dot(source, source.T, precision=highest)
            polynomial = coef_second * gram_now + coef_third * jnp.dot(gram_now, gram_now, precision=highest)
            source = coef_first * source + jnp.dot(polynomial, source, precision=highest)
    return source

def matrix_update(master, moment, gradient):
    new_state = velocity_damping * moment + gradient
    factor = math.sqrt(max(1.0, master.shape[0] / master.shape[1]))
    return (master - rate_matrix * factor * orthogonal(new_state), new_state)

def reference(block_source, upstream_adjoint, picture_patch_extents, triple_matrix, mixer_matrix, expand_matrix, shrink_matrix, affine_entries, sharpness, triple_velocity, mixer_velocity, expand_velocity, shrink_velocity, affine_velocity, sharpness_velocity):
    interior_patches = valid_mask(picture_patch_extents)
    genuine_patch_tally = jnp.sum(interior_patches)
    incoming_patches = block_source.astype(jnp.float32)
    block_target, adjoint_mapping = jax.vjp(partial(entire_evaluation, interior_patches=interior_patches), incoming_patches, triple_matrix, mixer_matrix, expand_matrix, shrink_matrix, affine_entries, sharpness)
    gradients = adjoint_mapping(upstream_adjoint.astype(jnp.float32))
    incoming_adjoint, triple_matrix_adjoint, mixer_matrix_adjoint, expand_matrix_adjoint, shrink_matrix_adjoint, affine_entries_adjoint, sharpness_adjoint = gradients
    revised_triple_matrix, renewed_triple_velocity = matrix_update(triple_matrix, triple_velocity, triple_matrix_adjoint)
    revised_mixer_matrix, renewed_mixer_velocity = matrix_update(mixer_matrix, mixer_velocity, mixer_matrix_adjoint)
    revised_expand_matrix, renewed_expand_velocity = matrix_update(expand_matrix, expand_velocity, expand_matrix_adjoint)
    revised_shrink_matrix, renewed_shrink_velocity = matrix_update(shrink_matrix, shrink_velocity, shrink_matrix_adjoint)
    renewed_affine_velocity = velocity_damping * affine_velocity + affine_entries_adjoint
    revised_affine_entries = affine_entries - affine_step_size * renewed_affine_velocity * lax.rsqrt(genuine_patch_tally)
    renewed_sharpness_velocity = velocity_damping * sharpness_velocity + sharpness_adjoint
    revised_sharpness = sharpness - affine_step_size * renewed_sharpness_velocity * lax.rsqrt(genuine_patch_tally)
    return (block_target.astype(jnp.bfloat16), incoming_adjoint, triple_matrix_adjoint, mixer_matrix_adjoint, expand_matrix_adjoint, shrink_matrix_adjoint, affine_entries_adjoint, sharpness_adjoint, revised_triple_matrix, revised_mixer_matrix, revised_expand_matrix, revised_shrink_matrix, renewed_triple_velocity, renewed_mixer_velocity, renewed_expand_velocity, renewed_shrink_velocity, revised_triple_matrix.astype(jnp.bfloat16), revised_mixer_matrix.astype(jnp.bfloat16), revised_expand_matrix.astype(jnp.bfloat16), revised_shrink_matrix.astype(jnp.bfloat16), revised_affine_entries, renewed_affine_velocity, revised_sharpness, renewed_sharpness_velocity)
```

```python
import math

import jax
import jax.numpy as jnp
from jax import lax
from jax.sharding import PartitionSpec as P

GRID = 24
NS_STEPS = 5


highest = lax.Precision.HIGHEST
layer_eps = 1e-06
unit_eps = 1e-06
batch_eps = 1e-05
frob_eps = 1e-07
velocity_damping = 0.5
rate_matrix = 0.25
affine_step_size = 0.2
coef_first = 3.4445
coef_second = -4.775
coef_third = 2.0315
root_half = 0.7071067811865476
inverse_root_tau = 0.3989422804014327


def layer_stats(source, gain_row, bias_row):
    centre = source - jnp.mean(source, axis=-1, keepdims=True)
    inverse = lax.rsqrt(jnp.mean(centre * centre, axis=-1, keepdims=True) + layer_eps)
    normal = centre * inverse
    return (normal * gain_row + bias_row, normal, inverse)


def layer_back(grad_norm, normal, inverse, gain_row):
    scaled = grad_norm * gain_row
    return inverse * (
        scaled
        - jnp.mean(scaled, axis=-1, keepdims=True)
        - normal * jnp.mean(scaled * normal, axis=-1, keepdims=True)
    )


def token_sum(source):
    return jnp.sum(source, axis=(0, 1))


def gelu_exact(source):
    return 0.5 * source * (1.0 + lax.erf(source * root_half))


def gelu_slope(source):
    return (
        0.5 * (1.0 + lax.erf(source * root_half))
        + source * jnp.exp(-0.5 * source * source) * inverse_root_tau
    )


def depthwise(source, kernel):
    grid_side = source.shape[1]
    padded = jnp.pad(source, ((0, 0), (1, 1), (1, 1), (0, 0)))
    summed = jnp.zeros_like(source)
    for offset in range(9):
        summed = (
            summed
            + padded[
                :, offset // 3 : offset // 3 + grid_side, offset % 3 : offset % 3 + grid_side, :
            ]
            * kernel[offset]
        )
    return summed


def kernel_grad(source, grad_conv):
    grid_side = source.shape[1]
    padded = jnp.pad(source, ((0, 0), (1, 1), (1, 1), (0, 0)))
    return jnp.stack(
        [
            jnp.sum(
                padded[
                    :, offset // 3 : offset // 3 + grid_side, offset % 3 : offset % 3 + grid_side, :
                ]
                * grad_conv,
                axis=(0, 1, 2),
            )
            for offset in range(9)
        ]
    )


def unit_back(grad_unit, unit_vals, inverse):
    return inverse * (grad_unit - unit_vals * jnp.sum(grad_unit * unit_vals, axis=1, keepdims=True))


def right_mul(left, right):
    return jnp.einsum("gsk,ke->gse", left, right, preferred_element_type=jnp.float32)


def right_mul_t(left, right):
    return jnp.einsum("gse,ke->gsk", left, right, preferred_element_type=jnp.float32)


def outer_sum(left, right):
    return jnp.einsum("gsk,gse->ke", left, right, preferred_element_type=jnp.float32)


def fold_bits(size):
    return [1 << place for place in range(size.bit_length() - 1)]


def swap(source, axis, bit):
    size = lax.axis_size(axis)
    return lax.ppermute(source, axis, [(member, member ^ bit) for member in range(size)])


def everyone(rows):
    devices = lax.axis_size("wide") * lax.axis_size("narrow")
    copies = jnp.broadcast_to(rows[None], (devices,) + rows.shape)
    return lax.all_to_all(copies, ("wide", "narrow"), 0, 0, tiled=True)


def pick(source, index):
    return lax.dynamic_index_in_dim(source, index, 0, keepdims=False)


def scatter_sum(bundle):
    narrow_pos = lax.axis_index("narrow")
    wide_pos = lax.axis_index("wide")
    held = bundle
    for bit in fold_bits(lax.axis_size("narrow")):
        mine = (narrow_pos // bit) % 2
        pairs = held.reshape((held.shape[0] // 2, 2) + held.shape[1:]).swapaxes(0, 1)
        held = pick(pairs, mine) + swap(pick(pairs, 1 - mine), "narrow", bit)
    held = held[0]
    for bit in fold_bits(lax.axis_size("wide")):
        mine = (wide_pos // bit) % 2
        halves = held.reshape((2, held.shape[0] // 2) + held.shape[1:])
        held = pick(halves, mine) + swap(pick(halves, 1 - mine), "wide", bit)
    return held


def gather_wide(share):
    wide_pos = lax.axis_index("wide")
    held = share
    for bit in reversed(fold_bits(lax.axis_size("wide"))):
        other = swap(held, "wide", bit)
        low = (wide_pos // bit) % 2 == 0
        held = jnp.concatenate([jnp.where(low, held, other), jnp.where(low, other, held)])
    return held


def gather_narrow(share):
    narrow_pos = lax.axis_index("narrow")
    held = share[None]
    for bit in reversed(fold_bits(lax.axis_size("narrow"))):
        other = swap(held, "narrow", bit)
        low = (narrow_pos // bit) % 2 == 0
        held = jnp.stack([jnp.where(low, held, other), jnp.where(low, other, held)], axis=1)
        held = held.reshape((-1,) + share.shape)
    return held


def dot3(left, right):
    return jnp.dot(left, right, precision=lax.Precision.HIGH)


def polynomial_of(gram):
    norm = jnp.sqrt(jnp.trace(gram)) + frob_eps
    now = gram / (norm * norm)
    identity = jnp.eye(gram.shape[0], dtype=jnp.float32)
    total = None
    for sweep_index in range(NS_STEPS):
        step = coef_first * identity + coef_second * now + coef_third * dot3(now, now)
        total = step / norm if total is None else dot3(step, total)
        if sweep_index < NS_STEPS - 1:
            now = dot3(dot3(step, now), step)
    return total


def orthogonal_pair(first, second, grams):
    narrow_pos = lax.axis_index("narrow")
    even = narrow_pos % 2 == 0
    mine = jnp.where(even, grams[0], grams[1]) + swap(
        jnp.where(even, grams[1], grams[0]), "narrow", 1
    )
    for bit in fold_bits(lax.axis_size("narrow"))[1:]:
        mine = mine + swap(mine, "narrow", bit)
    result = polynomial_of(mine)
    other = swap(result, "narrow", 1)
    return first(jnp.where(even, result, other)), second(jnp.where(even, other, result))


def on_device(
    block_source,
    upstream_adjoint,
    picture_patch_extents,
    triple_matrix,
    mixer_matrix,
    expand_matrix,
    shrink_matrix,
    affine_entries,
    sharpness,
    triple_velocity,
    mixer_velocity,
    expand_velocity,
    shrink_velocity,
    affine_velocity,
    sharpness_velocity,
):
    images, slot_count, model_width = block_source.shape
    group_index = sharpness.shape[0]
    head_size = model_width // group_index
    grid_side = GRID
    flat_shape = block_source.shape
    grid_shape = (images, grid_side, grid_side, model_width)
    head_shape = (images, slot_count, group_index, head_size)
    position = jnp.arange(slot_count, dtype=jnp.int32)
    rows_ok = (position // grid_side)[None, :] < picture_patch_extents[:, 0:1]
    cols_ok = (position % grid_side)[None, :] < picture_patch_extents[:, 1:2]
    interior_patches = (rows_ok & cols_ok).astype(jnp.float32)
    inside_col = interior_patches[:, :, None]
    asker_lowprec = triple_matrix.astype(jnp.bfloat16)
    attention_weights_lowprec = mixer_matrix.astype(jnp.bfloat16)
    one_low = expand_matrix.astype(jnp.bfloat16)
    two_low = shrink_matrix.astype(jnp.bfloat16)
    incoming_patches = block_source.astype(jnp.float32)
    norm_one, unit_one, inv_one = layer_stats(
        incoming_patches, affine_entries[0], affine_entries[1]
    )
    norm_one_low = norm_one.astype(jnp.bfloat16)
    joined = right_mul(norm_one_low, asker_lowprec) + affine_entries[2:5].reshape(-1)
    query_in = joined[:, :, :model_width] * inside_col
    key_in = joined[:, :, model_width : 2 * model_width] * inside_col
    value_heads = joined[:, :, 2 * model_width :].reshape(head_shape)
    query_inv = lax.rsqrt(jnp.sum(query_in * query_in, axis=1, keepdims=True) + unit_eps)
    key_inv = lax.rsqrt(jnp.sum(key_in * key_in, axis=1, keepdims=True) + unit_eps)
    query_unit = query_in * query_inv
    key_unit = key_in * key_inv
    query_heads = query_unit.reshape(head_shape)
    key_heads = key_unit.reshape(head_shape)
    feature_crosscov = jnp.einsum("gshi,gshj->ghij", query_heads, key_heads, precision=highest)
    mix_patches = jax.nn.softmax(feature_crosscov * sharpness[None, :, None, None], axis=-1)
    mixing_low = (
        jnp.einsum("ghij,gshj->gshi", mix_patches, value_heads, precision=highest)
        .reshape(flat_shape)
        .astype(jnp.bfloat16)
    )
    branch_one = right_mul(mixing_low, attention_weights_lowprec) + affine_entries[5]
    after_mix = incoming_patches + inside_col * affine_entries[6] * branch_one
    norm_two, unit_two, inv_two = layer_stats(after_mix, affine_entries[7], affine_entries[8])
    local_in = (norm_two * inside_col).reshape(grid_shape)
    conv_one = depthwise(local_in, affine_entries[9:18]).reshape(flat_shape) + affine_entries[18]
    activated = gelu_exact(conv_one)
    local_count = jnp.sum(interior_patches)
    local_sum = token_sum(activated * inside_col)
    local_mean = local_sum / local_count
    local_dev = (activated - local_mean) * inside_col
    first_rows = jnp.stack(
        [local_sum, token_sum(local_dev * local_dev), jnp.full_like(local_sum, local_count)]
    )
    first_all = everyone(first_rows)
    counts = first_all[:, 2]
    genuine_patch_tally = jnp.sum(counts[:, 0])
    centre_mean = jnp.sum(first_all[:, 0], axis=0) / genuine_patch_tally
    shifts = first_all[:, 0] / counts - centre_mean
    variance = (
        jnp.sum(first_all[:, 1] + counts * shifts * shifts, axis=0) / genuine_patch_tally
    )
    inverse_std = lax.rsqrt(variance + batch_eps)
    unit_bn = (activated - centre_mean) * inverse_std * inside_col
    normal_bn = (unit_bn * affine_entries[19] + affine_entries[20]) * inside_col
    normal_grid = normal_bn.reshape(grid_shape)
    conv_two = (
        depthwise(normal_grid, affine_entries[21:30]).reshape(flat_shape) + affine_entries[30]
    )
    after_local = after_mix + inside_col * affine_entries[31] * conv_two
    norm_three, unit_three, inv_three = layer_stats(
        after_local, affine_entries[32], affine_entries[33]
    )
    norm_three_low = norm_three.astype(jnp.bfloat16)
    hidden = right_mul(norm_three_low, one_low) + affine_entries[34:38].reshape(-1)
    hidden_low = gelu_exact(hidden).astype(jnp.bfloat16)
    branch_three = right_mul(hidden_low, two_low) + affine_entries[38]
    block_out = (after_local + inside_col * affine_entries[39] * branch_three).astype(jnp.bfloat16)
    grad_out = upstream_adjoint.astype(jnp.float32)
    grad_branch3 = (inside_col * affine_entries[39] * grad_out).astype(jnp.bfloat16)
    gamma_three = token_sum(inside_col * grad_out * branch_three)
    bias_fc2 = token_sum(grad_branch3.astype(jnp.float32))
    grad_w2 = outer_sum(hidden_low, grad_branch3)
    grad_hidden = (right_mul_t(grad_branch3, two_low) * gelu_slope(hidden)).astype(jnp.bfloat16)
    bias_fc1 = token_sum(grad_hidden.astype(jnp.float32)).reshape(4, model_width)
    grad_w1 = outer_sum(grad_hidden, norm_three_low)
    grad_norm3 = right_mul_t(grad_hidden, one_low)
    gain_three = token_sum(grad_norm3 * unit_three)
    shift_three = token_sum(grad_norm3)
    grad_local = grad_out + layer_back(grad_norm3, unit_three, inv_three, affine_entries[32])
    grad_conv2 = inside_col * affine_entries[31] * grad_local
    gamma_two = token_sum(inside_col * grad_local * conv_two)
    bias_conv2 = token_sum(grad_conv2)
    grad_conv2_grid = grad_conv2.reshape(grid_shape)
    kernel_two = kernel_grad(normal_grid, grad_conv2_grid)
    grad_bn = depthwise(grad_conv2_grid, affine_entries[29:20:-1]).reshape(flat_shape) * inside_col
    bn_grads = jnp.sum(
        everyone(jnp.stack([token_sum(grad_bn), token_sum(grad_bn * unit_bn)])), axis=0
    )
    bias_bn = bn_grads[0]
    gain_bn = bn_grads[1]
    grad_act = (
        inside_col
        * affine_entries[19]
        * inverse_std
        * (grad_bn - (bias_bn + unit_bn * gain_bn) / genuine_patch_tally)
    )
    grad_conv1 = grad_act * gelu_slope(conv_one)
    bias_conv1 = token_sum(grad_conv1)
    grad_conv1_grid = grad_conv1.reshape(grid_shape)
    kernel_one = kernel_grad(local_in, grad_conv1_grid)
    grad_norm2 = (
        depthwise(grad_conv1_grid, affine_entries[17:8:-1]).reshape(flat_shape) * inside_col
    )
    gain_two = token_sum(grad_norm2 * unit_two)
    shift_two = token_sum(grad_norm2)
    grad_mix = grad_local + layer_back(grad_norm2, unit_two, inv_two, affine_entries[7])
    grad_branch1 = (inside_col * affine_entries[6] * grad_mix).astype(jnp.bfloat16)
    gamma_one = token_sum(inside_col * grad_mix * branch_one)
    bias_proj = token_sum(grad_branch1.astype(jnp.float32))
    grad_wp = outer_sum(mixing_low, grad_branch1)
    grad_mixing = right_mul_t(grad_branch1, attention_weights_lowprec).reshape(head_shape)
    grad_attend = jnp.einsum("gshi,gshj->ghij", grad_mixing, value_heads, precision=highest)
    grad_value = jnp.einsum("ghij,gshi->gshj", mix_patches, grad_mixing, precision=highest).reshape(
        flat_shape
    )
    logits_adjoint = mix_patches * (
        grad_attend - jnp.sum(mix_patches * grad_attend, axis=-1, keepdims=True)
    )
    sharpness_adjoint = jnp.sum(logits_adjoint * feature_crosscov, axis=(0, 2, 3))
    crosscov_adjoint = logits_adjoint * sharpness[None, :, None, None]
    grad_qunit = jnp.einsum(
        "ghij,gshj->gshi", crosscov_adjoint, key_heads, precision=highest
    ).reshape(flat_shape)
    grad_kunit = jnp.einsum(
        "ghij,gshi->gshj", crosscov_adjoint, query_heads, precision=highest
    ).reshape(flat_shape)
    grad_query = unit_back(grad_qunit, query_unit, query_inv) * inside_col
    grad_key = unit_back(grad_kunit, key_unit, key_inv) * inside_col
    grad_joined = jnp.concatenate([grad_query, grad_key, grad_value], axis=-1).astype(jnp.bfloat16)
    bias_qkv = token_sum(grad_joined.astype(jnp.float32)).reshape(3, model_width)
    grad_wq = outer_sum(grad_joined, norm_one_low)
    grad_norm1 = right_mul_t(grad_joined, asker_lowprec)
    gain_one = token_sum(grad_norm1 * unit_one)
    shift_one = token_sum(grad_norm1)
    incoming_adjoint = grad_mix + layer_back(grad_norm1, unit_one, inv_one, affine_entries[0])
    zero_row = jnp.zeros((model_width,), jnp.float32)
    grad_vec = jnp.concatenate(
        [
            jnp.stack([gain_one, shift_one]),
            bias_qkv,
            jnp.stack([bias_proj, gamma_one, gain_two, shift_two]),
            kernel_one,
            jnp.stack([bias_conv1, zero_row, zero_row]),
            kernel_two,
            jnp.stack([bias_conv2, gamma_two, gain_three, shift_three]),
            bias_fc1,
            jnp.stack([bias_fc2, gamma_three]),
        ]
    )
    narrow_parts = lax.axis_size("narrow")
    narrow_pos = lax.axis_index("narrow")

    def own_part(full_matrix, along):
        part_size = full_matrix.shape[along] // narrow_parts
        return lax.dynamic_slice_in_dim(full_matrix, narrow_pos * part_size, part_size, along)

    def parts_of(full_matrix):
        return full_matrix.reshape((narrow_parts, -1) + full_matrix.shape[1:])

    fed_bundle = jnp.concatenate([parts_of(grad_w1), parts_of(grad_w2)], axis=1)
    fed_rows = grad_w1.shape[0] // narrow_parts
    fed_share = gather_wide(scatter_sum(fed_bundle))
    shard_w1 = fed_share[:fed_rows].T
    shard_w2 = fed_share[fed_rows:]

    vec_rows = jnp.zeros((narrow_parts * 64, model_width), jnp.float32)
    vec_rows = vec_rows.at[: grad_vec.shape[0]].set(grad_vec)
    vec_rows = vec_rows.at[grad_vec.shape[0], :group_index].set(sharpness_adjoint)
    att_bundle = jnp.concatenate(
        [parts_of(grad_wq), parts_of(grad_wp), parts_of(vec_rows)], axis=1
    )
    att_rows = grad_wq.shape[0] // narrow_parts
    mix_rows = grad_wp.shape[0] // narrow_parts
    att_share = gather_wide(scatter_sum(att_bundle))
    shard_wq = att_share[:att_rows].T
    shard_wp = att_share[att_rows : att_rows + mix_rows]
    vec_share = gather_narrow(att_share[att_rows + mix_rows :]).reshape(-1, model_width)
    vec_total = vec_share[: grad_vec.shape[0]]
    sharpness_sum = vec_share[grad_vec.shape[0], :group_index]
    shard_grads = (shard_wq, shard_wp, shard_w1, shard_w2)
    vec_full = jnp.concatenate([vec_total[:19], jnp.stack([gain_bn, bias_bn]), vec_total[21:]])
    moments = (triple_velocity, mixer_velocity, expand_velocity, shrink_velocity)
    states = [velocity_damping * moments[member] + shard_grads[member] for member in range(4)]
    fed_fields = orthogonal_pair(
        lambda poly: dot3(poly, states[2]),
        lambda poly: dot3(states[3], poly),
        (dot3(states[2], states[2].T), dot3(states[3].T, states[3])),
    )
    att_fields = orthogonal_pair(
        lambda poly: dot3(poly, states[0]),
        lambda poly: dot3(states[1], poly),
        (dot3(states[0], states[0].T), dot3(states[1].T, states[1])),
    )
    fields = att_fields + fed_fields
    full_weights = (triple_matrix, mixer_matrix, expand_matrix, shrink_matrix)
    factors = [
        math.sqrt(max(1.0, full_weights[member].shape[0] / full_weights[member].shape[1]))
        for member in range(4)
    ]
    masters = (
        own_part(triple_matrix, 1),
        own_part(mixer_matrix, 0),
        own_part(expand_matrix, 1),
        own_part(shrink_matrix, 0),
    )
    new_masters = [
        masters[member] - rate_matrix * factors[member] * fields[member] for member in range(4)
    ]
    vec_state = velocity_damping * affine_velocity + vec_full
    new_vec = affine_entries - affine_step_size * vec_state * lax.rsqrt(genuine_patch_tally)
    sharpness_buffer = velocity_damping * sharpness_velocity + sharpness_sum
    sharpness_following = sharpness - affine_step_size * sharpness_buffer * lax.rsqrt(
        genuine_patch_tally
    )
    return (
        block_out,
        incoming_adjoint,
        shard_grads[0],
        shard_grads[1],
        shard_grads[2],
        shard_grads[3],
        vec_full,
        sharpness_sum,
        new_masters[0],
        new_masters[1],
        new_masters[2],
        new_masters[3],
        states[0],
        states[1],
        states[2],
        states[3],
        new_masters[0].astype(jnp.bfloat16),
        new_masters[1].astype(jnp.bfloat16),
        new_masters[2].astype(jnp.bfloat16),
        new_masters[3].astype(jnp.bfloat16),
        new_vec,
        vec_state,
        sharpness_following,
        sharpness_buffer,
    )


def solution(mesh):
    return jax.shard_map(
        on_device,
        mesh=mesh,
        in_specs=(
            P(("wide", "narrow"), None, None),
            P(("wide", "narrow"), None, None),
            P(("wide", "narrow"), None),
            P(),
            P(),
            P(),
            P(),
            P(),
            P(),
            P(None, "narrow"),
            P("narrow", None),
            P(None, "narrow"),
            P("narrow", None),
            P(),
            P(),
        ),
        out_specs=(
            P(("wide", "narrow"), None, None),
            P(("wide", "narrow"), None, None),
            P(None, "narrow"),
            P("narrow", None),
            P(None, "narrow"),
            P("narrow", None),
            P(),
            P(),
            P(None, "narrow"),
            P("narrow", None),
            P(None, "narrow"),
            P("narrow", None),
            P(None, "narrow"),
            P("narrow", None),
            P(None, "narrow"),
            P("narrow", None),
            P(None, "narrow"),
            P("narrow", None),
            P(None, "narrow"),
            P("narrow", None),
            P(),
            P(),
            P(),
            P(),
        ),
        check_vma=False,
    )
```

```python
import functools
import math

import jax
import jax.numpy as jnp
from jax import lax
from jax.experimental import pallas as pl
from jax.experimental.pallas import tpu as pltpu
from jax.sharding import PartitionSpec as P

GRID = 24
NS_STEPS = 5
SUM_ROWS = 64

layer_eps = 1e-06
unit_eps = 1e-06
batch_eps = 1e-05
frob_eps = 1e-07
velocity_damping = 0.5
rate_matrix = 0.25
affine_step_size = 0.2
coef_first = 3.4445
coef_second = -4.775
coef_third = 2.0315
root_half = 0.7071067811865476
inverse_root_tau = 0.3989422804014327
HIGH = lax.Precision.HIGH
F32 = jnp.float32
BF16 = jnp.bfloat16


def mul_nn(left, right, precision=None):
    return lax.dot_general(
        left, right, (((1,), (0,)), ((), ())), precision=precision, preferred_element_type=F32
    )


def mul_nt(left, right, precision=None):
    return lax.dot_general(
        left, right, (((1,), (1,)), ((), ())), precision=precision, preferred_element_type=F32
    )


def mul_tn(left, right, precision=None):
    return lax.dot_general(
        left, right, (((0,), (0,)), ((), ())), precision=precision, preferred_element_type=F32
    )


def fold_rows(source):
    total = source[0:8]
    for start in range(8, source.shape[0], 8):
        total = total + source[start : start + 8]
    return total


def row_sum(total):
    return jnp.sum(total, axis=0, keepdims=True)


def norm_rows(source):
    centre = source - jnp.mean(source, axis=-1, keepdims=True)
    inverse = lax.rsqrt(jnp.mean(centre * centre, axis=-1, keepdims=True) + layer_eps)
    return centre * inverse, inverse


def norm_back(grad_norm, normal, inverse, gain):
    scaled = grad_norm * gain
    return inverse * (
        scaled
        - jnp.mean(scaled, axis=-1, keepdims=True)
        - normal * jnp.mean(scaled * normal, axis=-1, keepdims=True)
    )


def normal_cdf(source):
    return 0.5 * (1.0 + lax.erf(source * root_half))


def density(source):
    return jnp.exp(-0.5 * source * source) * inverse_root_tau


def loop(start, stop, body, carry, unroll=1):
    return lax.fori_loop(start, stop, body, carry, unroll=unroll)


def here(row):
    return pl.ds(pl.multiple_of(row * GRID, 8), GRID)


class Rows:
    def __init__(self, extent_ref, width):
        self.extent_ref = extent_ref
        self.column = lax.broadcasted_iota(jnp.int32, (GRID, width), 0)

    def inside(self, row):
        image = row // GRID
        limit = jnp.where(
            row - image * GRID < self.extent_ref[image, 0], self.extent_ref[image, 1], 0
        )
        return self.column < limit

    def put(self, pads, row, value):
        centre, left, right = pads
        place = here(row + 2 * (row // GRID) + 1)
        centre[place, :] = value
        left[place, :] = jnp.where(self.column == 0, 0.0, pltpu.roll(value, 1, 0))
        right[place, :] = jnp.where(
            self.column == GRID - 1, 0.0, pltpu.roll(value, GRID - 1, 0)
        )

    @staticmethod
    def taps(pads, row):
        centre, left, right = pads
        first = row + 2 * (row // GRID)
        for down in range(3):
            place = here(first + down)
            for plane in (left, centre, right):
                yield plane[place, :]


def clear_edges(pads, images):
    for plane in pads:
        edge = jnp.zeros((GRID, plane.shape[1]), F32)
        for image in range(images):
            base = image * (GRID + 2) * GRID
            plane[base : base + GRID, :] = edge
            plane[base + (GRID + 1) * GRID : base + (GRID + 2) * GRID, :] = edge


def pads_of(images, width):
    return [pltpu.VMEM((images * (GRID + 2) * GRID, width), F32)] * 3


VMEM = pl.BlockSpec(memory_space=pltpu.VMEM)
SMEM = pl.BlockSpec(memory_space=pltpu.SMEM)


def call(kernel, name, spaces, outs, scratch, limit, args, flops=0, size=0):
    return pl.pallas_call(
        kernel,
        in_specs=spaces,
        out_specs=[VMEM] * len(outs),
        out_shape=[jax.ShapeDtypeStruct(shape, dtype) for shape, dtype in outs],
        scratch_shapes=scratch,
        compiler_params=pltpu.CompilerParams(vmem_limit_bytes=limit << 20),
        cost_estimate=pl.CostEstimate(
            flops=int(flops), bytes_accessed=int(size), transcendentals=0
        ),
        name=name,
    )(*args)


def front_kernel(
    images, extent_ref, sharp_ref, x_ref, wq_ref, wp_ref, aff_ref,
    norm_ref, query_ref, key_ref, value_ref, inv_ref, cov_ref, attend_ref, mixing_ref,
    branch_ref, mix_ref, conv_ref, act_ref, stat_ref,
    joined, pad_c, pad_l, pad_r,
):
    tokens, width = x_ref.shape
    slots = tokens // images
    heads = sharp_ref.shape[0]
    head = width // heads
    pads = (pad_c, pad_l, pad_r)
    rows = Rows(extent_ref, width)
    clear_edges(pads, images)
    zero = jnp.zeros((8, width), F32)

    def aff(row):
        return aff_ref[row : row + 1, :]

    def first(step, carry):
        place = pl.ds(pl.multiple_of(step * 48, 16), 48)
        normal, _ = norm_rows(x_ref[place, :].astype(F32))
        norm_ref[place, :] = (normal * aff(0) + aff(1)).astype(BF16)
        return carry

    loop(0, tokens // 48, first, 0, unroll=4)
    joined[...] = mul_nn(norm_ref[...], wq_ref[...].astype(BF16))

    def second(row, carry):
        query_sum, key_sum = carry
        at = here(row)
        inside = rows.inside(row)
        query = jnp.where(inside, joined[at, :width] + aff(2), 0.0)
        key = jnp.where(inside, joined[at, width : 2 * width] + aff(3), 0.0)
        query_ref[at, :] = query
        key_ref[at, :] = key
        value_ref[at, :] = joined[at, 2 * width :] + aff(4)
        return query_sum + fold_rows(query * query), key_sum + fold_rows(key * key)

    for image in range(images):
        span = slice(image * slots, (image + 1) * slots)
        low, high = image * GRID, (image + 1) * GRID
        query_sum, key_sum = loop(low, high, second, (zero, zero), unroll=2)
        query_inv = lax.rsqrt(row_sum(query_sum) + unit_eps)
        key_inv = lax.rsqrt(row_sum(key_sum) + unit_eps)
        inv_ref[2 * image : 2 * image + 1, :] = query_inv
        inv_ref[2 * image + 1 : 2 * image + 2, :] = key_inv

        def third(row, carry):
            at = here(row)
            query_ref[at, :] = query_ref[at, :] * query_inv
            key_ref[at, :] = key_ref[at, :] * key_inv
            return carry

        loop(low, high, third, 0, unroll=2)
        cov_ref[image] = mul_tn(query_ref[span, :], key_ref[span, :], HIGH)
        lane = lax.broadcasted_iota(jnp.int32, (head, width), 1)
        for group in range(heads):
            part = slice(group * head, (group + 1) * head)
            own = (lane >= group * head) & (lane < (group + 1) * head)
            scores = jnp.where(own, cov_ref[image, part, :] * sharp_ref[group], -jnp.inf)
            raised = jnp.exp(scores - jnp.max(scores, axis=-1, keepdims=True))
            attend_ref[image, part, :] = raised / jnp.sum(raised, axis=-1, keepdims=True)
        mixing_ref[span, :] = mul_nt(value_ref[span, :], attend_ref[image], HIGH).astype(BF16)
    branch_ref[...] = mul_nn(mixing_ref[...], wp_ref[...].astype(BF16))

    def fourth(row, carry):
        at = here(row)
        inside = rows.inside(row)
        branch = branch_ref[at, :] + aff(5)
        branch_ref[at, :] = branch
        after = x_ref[at, :].astype(F32) + jnp.where(inside, aff(6) * branch, 0.0)
        mix_ref[at, :] = after
        normal, _ = norm_rows(after)
        rows.put(pads, row, jnp.where(inside, normal * aff(7) + aff(8), 0.0))
        return carry

    loop(0, images * GRID, fourth, 0, unroll=8)

    def fifth(row, total):
        at = here(row)
        summed = aff(18)
        for index, tap in enumerate(rows.taps(pads, row)):
            summed = summed + tap * aff(9 + index)
        conv_ref[at, :] = summed
        active = summed * normal_cdf(summed)
        act_ref[at, :] = active
        return total + fold_rows(jnp.where(rows.inside(row), active, 0.0))

    for image in range(images):
        low, high = image * GRID, (image + 1) * GRID
        act_sum = row_sum(loop(low, high, fifth, zero, unroll=2))
        count = (extent_ref[image, 0] * extent_ref[image, 1]).astype(F32)
        centre = act_sum / count

        def sixth(row, total):
            shifted = jnp.where(rows.inside(row), act_ref[here(row), :] - centre, 0.0)
            return total + fold_rows(shifted * shifted)

        stat_ref[image : image + 1, :] = act_sum
        stat_ref[images + image : images + image + 1, :] = row_sum(
            loop(low, high, sixth, zero, unroll=4)
        )
        stat_ref[2 * images + image : 2 * images + image + 1, :] = jnp.full_like(centre, count)


def front(images, extents, sharpness, source, wq, wp, aff):
    tokens, width = source.shape
    full, low, square = ((tokens, width), F32), ((tokens, width), BF16), ((images, width, width), F32)
    outs = [
        low, full, full, full, ((2 * images, width), F32), square, square, low,
        full, full, full, full, ((3 * images, width), F32),
    ]
    return call(
        functools.partial(front_kernel, images), "front",
        [SMEM, SMEM, VMEM, VMEM, VMEM, VMEM], outs,
        [pltpu.VMEM((tokens, 3 * width), F32), *pads_of(images, width)], 48,
        (extents, sharpness, source, wq, wp, aff), 2e10, 3e7,
    )


def middle_kernel(
    images, extent_ref, stat_ref, mix_ref, act_ref, up_ref, w1_ref, w2_ref, aff_ref,
    out_ref, norm_ref, hidlow_ref, gbranch_ref, ghid_ref, glocal_ref, gbn_ref, batch_ref,
    sum_ref, bn_ref,
    hidden, dhidden, conv_s, normal_s, inverse_s, branch_s, pad_c, pad_l, pad_r, gad_c, gad_l, gad_r,
):
    tokens, width = mix_ref.shape
    inner = w1_ref.shape[1]
    pads, gads = (pad_c, pad_l, pad_r), (gad_c, gad_l, gad_r)
    rows = Rows(extent_ref, width)
    clear_edges(pads, images)
    clear_edges(gads, images)
    zero = jnp.zeros((8, width), F32)
    all_rows = images * GRID

    def aff(row):
        return aff_ref[row : row + 1, :]

    sums, counts = stat_ref[:, 0:images, :], stat_ref[:, 2 * images : 3 * images, :]
    tally = row_sum(jnp.sum(counts, axis=0))
    centre = row_sum(jnp.sum(sums, axis=0)) / tally
    shift = sums / counts - centre[None]
    spread = stat_ref[:, images : 2 * images, :] + counts * shift * shift
    inverse_std = lax.rsqrt(row_sum(jnp.sum(spread, axis=0)) / tally + batch_eps)
    batch_ref[0:1, :] = centre
    batch_ref[1:2, :] = inverse_std
    batch_ref[2:3, :] = tally

    def first(row, carry):
        inside = rows.inside(row)
        unit = (act_ref[here(row), :] - centre) * inverse_std
        rows.put(pads, row, jnp.where(inside, unit * aff(19) + aff(20), 0.0))
        return carry

    loop(0, all_rows, first, 0, unroll=2)

    def second(row, carry):
        at = here(row)
        inside = rows.inside(row)
        summed = aff(30)
        for index, tap in enumerate(rows.taps(pads, row)):
            summed = summed + tap * aff(21 + index)
        conv_s[at, :] = summed
        after = mix_ref[at, :] + jnp.where(inside, aff(31) * summed, 0.0)
        branch_s[at, :] = after
        return carry

    loop(0, all_rows, second, 0, unroll=2)

    def second_norm(step, carry):
        at = pl.ds(pl.multiple_of(step * 48, 16), 48)
        normal, inverse = norm_rows(branch_s[at, :])
        normal_s[at, :] = normal
        inverse_s[at, :] = inverse
        norm_ref[at, :] = (normal * aff(32) + aff(33)).astype(BF16)
        return carry

    loop(0, tokens // 48, second_norm, 0, unroll=4)

    def third(row, total):
        at = here(row)
        grad = jnp.where(rows.inside(row), up_ref[at, :].astype(F32) * aff(39), 0.0).astype(BF16)
        gbranch_ref[at, :] = grad
        return total + fold_rows(grad.astype(F32))

    sum_ref[17:18, :] = row_sum(loop(0, all_rows, third, zero, unroll=2))
    slots = tokens // images
    quarters = inner // width
    bias_sums = [zero] * quarters
    for image in range(images):
        span = slice(image * slots, (image + 1) * slots)
        hidden[...] = mul_nn(norm_ref[span, :], w1_ref[...])
        dhidden[...] = mul_nt(gbranch_ref[span, :], w2_ref[...])
        for quarter in range(quarters):
            cols = slice(quarter * width, (quarter + 1) * width)
            bias = aff(34 + quarter)

            def fourth(step, total):
                at = pl.ds(pl.multiple_of(step * 16, 16), 16)
                to = pl.ds(pl.multiple_of(image * slots + step * 16, 16), 16)
                value = hidden[at, cols] + bias
                cdf = normal_cdf(value)
                hidlow_ref[to, cols] = (value * cdf).astype(BF16)
                grad = (dhidden[at, cols] * (cdf + value * density(value))).astype(BF16)
                ghid_ref[to, cols] = grad
                return total + fold_rows(grad.astype(F32))

            bias_sums[quarter] = loop(0, slots // 16, fourth, bias_sums[quarter], unroll=2)
        gbn_ref[span, :] = mul_nt(ghid_ref[span, :], w1_ref[...])
        glocal_ref[span, :] = mul_nn(hidlow_ref[span, :], w2_ref[...])
    for quarter in range(quarters):
        sum_ref[13 + quarter : 14 + quarter, :] = row_sum(bias_sums[quarter])

    def fifth(row, total):
        at = here(row)
        inside = rows.inside(row)
        branch = jnp.where(inside, glocal_ref[at, :] + aff(38), 0.0)
        out_ref[at, :] = (branch_s[at, :] + aff(39) * branch).astype(BF16)
        return total + fold_rows(up_ref[at, :].astype(F32) * branch)

    sum_ref[18:19, :] = row_sum(loop(0, all_rows, fifth, zero, unroll=2))

    def sixth(row, carry):
        gain_sum, shift_sum, scale_sum, bias_sum = carry
        at = here(row)
        inside = rows.inside(row)
        grad_norm = gbn_ref[at, :]
        normal = normal_s[at, :]
        grad = up_ref[at, :].astype(F32) + norm_back(grad_norm, normal, inverse_s[at, :], aff(32))
        glocal_ref[at, :] = grad
        kept = jnp.where(inside, grad, 0.0)
        scaled = kept * aff(31)
        rows.put(gads, row, scaled)
        return (
            gain_sum + fold_rows(grad_norm * normal), shift_sum + fold_rows(grad_norm),
            scale_sum + fold_rows(kept * conv_s[at, :]), bias_sum + fold_rows(scaled),
        )

    gain_sum, shift_sum, scale_sum, bias_sum = loop(0, all_rows, sixth, (zero,) * 4, unroll=6)
    sum_ref[11:12, :] = row_sum(gain_sum)
    sum_ref[12:13, :] = row_sum(shift_sum)
    sum_ref[10:11, :] = row_sum(scale_sum)
    sum_ref[9:10, :] = row_sum(bias_sum)

    def seventh(row, carry):
        bias_bn, gain_bn = carry
        at = here(row)
        summed = None
        for index, tap in enumerate(rows.taps(gads, row)):
            term = tap * aff(29 - index)
            summed = term if summed is None else summed + term
        summed = jnp.where(rows.inside(row), summed, 0.0)
        gbn_ref[at, :] = summed
        unit = (act_ref[at, :] - centre) * inverse_std
        return bias_bn + fold_rows(summed), gain_bn + fold_rows(summed * unit)

    bias_bn, gain_bn = loop(0, all_rows, seventh, (zero, zero), unroll=2)
    bn_ref[0:1, :] = row_sum(bias_bn)
    bn_ref[1:2, :] = row_sum(gain_bn)
    kernel_sums(rows, pads, gad_c, images, sum_ref, 0)


def kernel_sums(rows, pads, grad_plane, images, sum_ref, base):
    width = grad_plane.shape[1]
    zero = jnp.zeros((8, width), F32)

    def body(row, carry):
        grad = grad_plane[here(row + 2 * (row // GRID) + 1), :]
        return tuple(
            total + fold_rows(grad * tap) for total, tap in zip(carry, rows.taps(pads, row))
        )

    totals = loop(0, images * GRID, body, (zero,) * 9)
    for index, total in enumerate(totals):
        sum_ref[base + index : base + index + 1, :] = row_sum(total)


def middle(images, extents, stats, after_mix, act, upstream, w1, w2, aff):
    tokens, width = after_mix.shape
    inner = w1.shape[1]
    full, low, wide = ((tokens, width), F32), ((tokens, width), BF16), ((tokens, inner), BF16)
    outs = [
        low, low, wide, low, wide, full, full, ((3, width), F32), ((19, width), F32), ((2, width), F32),
    ]
    return call(
        functools.partial(middle_kernel, images), "middle",
        [SMEM] + [VMEM] * 7, outs,
        [
            pltpu.VMEM((tokens // images, inner), F32), pltpu.VMEM((tokens // images, inner), F32),
            pltpu.VMEM((tokens, width), F32), pltpu.VMEM((tokens, width), F32),
            pltpu.VMEM((tokens, 1), F32), pltpu.VMEM((tokens, width), F32),
            *pads_of(images, width), *pads_of(images, width),
        ], 56,
        (extents, stats, after_mix, act, upstream, w1, w2, aff), 3e10, 4e7,
    )


def fed_grads_kernel(shift, bit_ref, norm_ref, hidlow_ref, gbranch_ref, ghid_ref, out_ref):
    width = norm_ref.shape[1]
    pairs = out_ref.shape[0]
    size = ghid_ref.shape[1] // (2 * pairs)
    low = bit_ref[0] if shift == 0 else 1 - bit_ref[0]
    for pair in range(pairs):
        cols = pl.ds(pl.multiple_of((2 * pair + low) * size, 128), size)
        out_ref[pair, 0:size, :] = mul_tn(ghid_ref[:, cols], norm_ref[...])
        out_ref[pair, size : 2 * size, :] = mul_tn(hidlow_ref[:, cols], gbranch_ref[...])


def fed_grads(shift, parts, bit, norm, hidlow, gbranch, ghid):
    width, inner = norm.shape[1], ghid.shape[1]
    return call(
        functools.partial(fed_grads_kernel, shift), "fed_grads",
        [SMEM] + [VMEM] * 4, [((parts // 2, 2 * inner // parts, width), F32)], [], 32,
        (bit, norm, hidlow, gbranch, ghid), 3e9, 1e7,
    )[0]


def inner_back_kernel(
    images, extent_ref, total_ref, batch_ref, act_ref, conv_ref, gbn_ref, glocal_ref, mix_ref,
    branch_ref, aff_ref, gmix_ref, gbranch_ref, sum_ref, bn_ref,
    normal_s, inverse_s, pad_c, pad_l, pad_r, gad_c, gad_l, gad_r,
):
    tokens, width = act_ref.shape
    pads, gads = (pad_c, pad_l, pad_r), (gad_c, gad_l, gad_r)
    rows = Rows(extent_ref, width)
    clear_edges(pads, images)
    clear_edges(gads, images)
    zero = jnp.zeros((8, width), F32)
    all_rows = images * GRID

    def aff(row):
        return aff_ref[row : row + 1, :]

    totals = jnp.sum(total_ref[...], axis=0)
    bn_ref[...] = totals
    centre, inverse_std, tally = batch_ref[0:1, :], batch_ref[1:2, :], batch_ref[2:3, :]
    bias_mean, gain_mean = totals[0:1, :] / tally, totals[1:2, :] / tally
    factor = aff(19) * inverse_std

    def first(row, total):
        at = here(row)
        unit = (act_ref[at, :] - centre) * inverse_std
        value = conv_ref[at, :]
        slope = normal_cdf(value) + value * density(value)
        grad = factor * (gbn_ref[at, :] - (bias_mean + unit * gain_mean)) * slope
        grad = jnp.where(rows.inside(row), grad, 0.0)
        rows.put(gads, row, grad)
        return total + fold_rows(grad)

    sum_ref[13:14, :] = row_sum(loop(0, all_rows, first, zero, unroll=2))

    def second(row, carry):
        at = here(row)
        normal, inverse = norm_rows(mix_ref[at, :])
        normal_s[at, :] = normal
        inverse_s[at, :] = inverse
        rows.put(pads, row, jnp.where(rows.inside(row), normal * aff(7) + aff(8), 0.0))
        return carry

    loop(0, all_rows, second, 0, unroll=8)
    kernel_sums(rows, pads, gad_c, images, sum_ref, 4)

    def third(row, carry):
        summed = None
        for index, tap in enumerate(rows.taps(gads, row)):
            term = tap * aff(17 - index)
            summed = term if summed is None else summed + term
        gmix_ref[here(row), :] = jnp.where(rows.inside(row), summed, 0.0)
        return carry

    loop(0, all_rows, third, 0, unroll=2)

    def fourth(row, carry):
        gain_sum, shift_sum, scale_sum, bias_sum = carry
        at = here(row)
        grad_norm, normal = gmix_ref[at, :], normal_s[at, :]
        grad = glocal_ref[at, :] + norm_back(grad_norm, normal, inverse_s[at, :], aff(7))
        gmix_ref[at, :] = grad
        kept = jnp.where(rows.inside(row), grad, 0.0)
        low = (kept * aff(6)).astype(BF16)
        gbranch_ref[at, :] = low
        return (
            gain_sum + fold_rows(grad_norm * normal), shift_sum + fold_rows(grad_norm),
            scale_sum + fold_rows(kept * branch_ref[at, :]), bias_sum + fold_rows(low.astype(F32)),
        )

    gain_sum, shift_sum, scale_sum, bias_sum = loop(0, all_rows, fourth, (zero,) * 4, unroll=6)
    sum_ref[0:1, :] = row_sum(bias_sum)
    sum_ref[1:2, :] = row_sum(scale_sum)
    sum_ref[2:3, :] = row_sum(gain_sum)
    sum_ref[3:4, :] = row_sum(shift_sum)


def inner_back(images, extents, totals, batch, act, conv, gbn, glocal, after_mix, branch, aff):
    tokens, width = act.shape
    outs = [((tokens, width), F32), ((tokens, width), BF16), ((14, width), F32), ((2, width), F32)]
    return call(
        functools.partial(inner_back_kernel, images), "inner_back",
        [SMEM] + [VMEM] * 9, outs,
        [
            pltpu.VMEM((tokens, width), F32), pltpu.VMEM((tokens, 1), F32),
            *pads_of(images, width), *pads_of(images, width),
        ], 40,
        (extents, totals, batch, act, conv, gbn, glocal, after_mix, branch, aff), 2e10, 3e7,
    )


def attention_back_kernel(
    images, extent_ref, sharp_ref, bit_ref, x_ref, norm_ref, query_ref, key_ref, value_ref, inv_ref,
    cov_ref, attend_ref, mixing_ref, gbranch_ref, gmix_ref, wq_ref, wp_ref, aff_ref,
    tail_ref, inner_ref, incoming_ref, send_ref, keep_ref,
    gmixing, gscore, gjoined, gquery, gkey, matrix, vector,
):
    tokens, width = x_ref.shape
    slots = tokens // images
    heads = sharp_ref.shape[0]
    head = width // heads
    rows = Rows(extent_ref, width)
    zero = jnp.zeros((8, width), F32)

    def aff(row):
        return aff_ref[row : row + 1, :]

    vector[...] = jnp.zeros_like(vector)
    gmixing[...] = mul_nt(gbranch_ref[...], wp_ref[...])
    lane = lax.broadcasted_iota(jnp.int32, (1, width), 1)
    sharp_sum = jnp.zeros((1, width), F32)
    bias = [zero] * 3
    for image in range(images):
        span = slice(image * slots, (image + 1) * slots)
        low, high = image * GRID, (image + 1) * GRID
        gscore[...] = mul_tn(gmixing[span, :], value_ref[span, :], HIGH)
        for group in range(heads):
            part = slice(group * head, (group + 1) * head)
            attend = attend_ref[image, part, :]
            grad = gscore[part, :]
            grad = attend * (grad - jnp.sum(attend * grad, axis=-1, keepdims=True))
            gscore[part, :] = grad * sharp_ref[group]
            amount = jnp.sum(
                jnp.sum(grad * cov_ref[image, part, :], axis=0, keepdims=True),
                axis=1, keepdims=True,
            )
            sharp_sum = sharp_sum + jnp.where(lane == group, amount, 0.0)
        gquery[...] = mul_nt(key_ref[span, :], gscore[...], HIGH)
        gkey[...] = mul_nn(query_ref[span, :], gscore[...], HIGH)
        gmixing[span, :] = mul_nn(gmixing[span, :], attend_ref[image], HIGH)

        def first(row, carry):
            query_dot, key_dot = carry
            at = here(row)
            to = here(row - low)
            return (
                query_dot + fold_rows(gquery[to, :] * query_ref[at, :]),
                key_dot + fold_rows(gkey[to, :] * key_ref[at, :]),
            )

        query_dot, key_dot = loop(low, high, first, (zero, zero), unroll=2)
        query_dot, key_dot = row_sum(query_dot), row_sum(key_dot)
        query_inv = inv_ref[2 * image : 2 * image + 1, :]
        key_inv = inv_ref[2 * image + 1 : 2 * image + 2, :]

        def second(pair, carry):
            totals = list(carry)
            thirds = ([], [], [])
            for row in (2 * pair, 2 * pair + 1):
                at = here(row)
                to = here(row - low)
                inside = rows.inside(row)
                grad = query_inv * (gquery[to, :] - query_ref[at, :] * query_dot)
                thirds[0].append(jnp.where(inside, grad, 0.0))
                grad = key_inv * (gkey[to, :] - key_ref[at, :] * key_dot)
                thirds[1].append(jnp.where(inside, grad, 0.0))
                thirds[2].append(gmixing[at, :])
            at = pl.ds(pl.multiple_of(pair * 2 * GRID, 16), 2 * GRID)
            for third in range(3):
                value = jnp.concatenate(thirds[third], axis=0).astype(BF16)
                gjoined[at, third * width : (third + 1) * width] = value
                totals[third] = totals[third] + fold_rows(value.astype(F32))
            return tuple(totals)

        bias = loop(low // 2, high // 2, second, tuple(bias))
    for third in range(3):
        vector[2 + third : 3 + third, :] = row_sum(bias[third])
    gmixing[...] = mul_nt(gjoined[...], wq_ref[...])

    def third(step, carry):
        gain_sum, shift_sum = carry
        at = pl.ds(pl.multiple_of(step * 48, 16), 48)
        normal, inverse = norm_rows(x_ref[at, :].astype(F32))
        grad = gmixing[at, :]
        incoming_ref[at, :] = gmix_ref[at, :] + norm_back(grad, normal, inverse, aff(0))
        return gain_sum + fold_rows(grad * normal), shift_sum + fold_rows(grad)

    gain_sum, shift_sum = loop(0, tokens // 48, third, (zero, zero), unroll=4)
    vector[0:1, :] = row_sum(gain_sum)
    vector[1:2, :] = row_sum(shift_sum)
    vector[5:19, :] = inner_ref[...]
    vector[21:40, :] = tail_ref[...]
    vector[40:41, :] = sharp_sum

    pairs = send_ref.shape[0]
    matrix[0 : 3 * width, :] = mul_tn(gjoined[...], norm_ref[...])
    matrix[3 * width :, :] = mul_tn(mixing_ref[...], gbranch_ref[...])
    joined_rows, mixer_rows = 3 * width // (2 * pairs), width // (2 * pairs)
    for pair in range(pairs):
        for target, place in ((keep_ref, bit_ref[0]), (send_ref, 1 - bit_ref[0])):
            part = 2 * pair + place
            last = joined_rows + mixer_rows
            at = pl.ds(pl.multiple_of(part * joined_rows, 8), joined_rows)
            target[pair, 0:joined_rows, :] = matrix[at, :]
            at = pl.ds(pl.multiple_of(3 * width + part * mixer_rows, 8), mixer_rows)
            target[pair, joined_rows:last, :] = matrix[at, :]
            at = pl.ds(pl.multiple_of(part * SUM_ROWS, 8), SUM_ROWS)
            target[pair, last : last + SUM_ROWS, :] = vector[at, :]


def attention_back(
    images, parts, extents, sharpness, bit, source, norm, query, key, value, inv, cov, attend,
    mixing, gbranch, gmix, wq, wp, aff, tail_sums, inner_sums,
):
    tokens, width = source.shape
    slots = tokens // images
    share = ((parts // 2, 4 * width // parts + SUM_ROWS, width), F32)
    return call(
        functools.partial(attention_back_kernel, images), "attention_back",
        [SMEM] * 3 + [VMEM] * 16, [((tokens, width), F32), share, share],
        [
            pltpu.VMEM((tokens, width), F32), pltpu.VMEM((width, width), F32),
            pltpu.VMEM((tokens, 3 * width), BF16), pltpu.VMEM((slots, width), F32),
            pltpu.VMEM((slots, width), F32), pltpu.VMEM((4 * width, width), F32),
            pltpu.VMEM((parts * SUM_ROWS, width), F32),
        ], 40,
        (
            extents, sharpness, bit, source, norm, query, key, value, inv, cov, attend, mixing,
            gbranch, gmix, wq, wp, aff, tail_sums, inner_sums,
        ), 3e10, 4e7,
    )


def split_add_kernel(bit_ref, held_ref, other_ref, send_ref, keep_ref):
    bit = bit_ref[0]
    keep_ref[...] = held_ref[bit] + other_ref[bit]
    send_ref[...] = held_ref[1 - bit] + other_ref[1 - bit]


def split_add(bit, held, other):
    rows, width = held.shape[-2], held.shape[-1]
    half = ((rows, width), F32)
    return call(
        split_add_kernel, "split_add", [SMEM, VMEM, VMEM], [half, half], [], 24,
        (bit, held, other), 0, 12 * held.size,
    )


def add_kernel(held_ref, other_ref, out_ref):
    out_ref[...] = held_ref[...] + other_ref[...]


def add(held, other):
    return call(
        add_kernel, "add_rows", [VMEM, VMEM], [(held.shape, F32)], [], 16, (held, other), 0,
        12 * held.size,
    )[0]


def join_kernel(bit_ref, held_ref, other_ref, out_ref):
    bit = bit_ref[0]
    out_ref[bit] = held_ref[...]
    out_ref[1 - bit] = other_ref[...]


def join(bit, held, other):
    return call(
        join_kernel, "join_rows", [SMEM, VMEM, VMEM], [((2,) + held.shape, F32)], [], 16,
        (bit, held, other), 0, 16 * held.size,
    )[0]


def sweeps_kernel(mine_ref, other_ref, out_ref, now, step, total):
    size = mine_ref.shape[0]
    row = lax.broadcasted_iota(jnp.int32, (size, size), 0)
    diagonal = row == lax.broadcasted_iota(jnp.int32, (size, size), 1)
    now[...] = mine_ref[...] + other_ref[...]
    trace = jnp.where(diagonal, now[...], 0.0)
    trace = jnp.sum(jnp.sum(trace, axis=0, keepdims=True), axis=1, keepdims=True)
    norm = jnp.sqrt(trace) + frob_eps
    now[...] = now[...] / (norm * norm)
    for sweep_index in range(NS_STEPS):
        square = mul_nn(now[...], now[...], HIGH)
        step[...] = (
            jnp.where(diagonal, coef_first, 0.0) + coef_second * now[...] + coef_third * square
        )
        if sweep_index == 0:
            total[...] = step[...] / norm
        elif sweep_index < NS_STEPS - 1:
            total[...] = mul_nn(step[...], total[...], HIGH)
        else:
            out_ref[...] = mul_nn(step[...], total[...], HIGH)
        if sweep_index < NS_STEPS - 1:
            now[...] = mul_nn(mul_nn(step[...], now[...], HIGH), step[...], HIGH)


def sweeps(mine, other):
    square = pltpu.VMEM(mine.shape, F32)
    return call(
        sweeps_kernel, "sweeps", [VMEM, VMEM], [(mine.shape, F32)], [square] * 3, 24,
        (mine, other), 1e10, 4e6,
    )[0]


def prepare_kernel(
    bit_ref, share_ref, first_ref, second_ref,
    grad_one_ref, grad_two_ref, state_one_ref, state_two_ref, send_ref, keep_ref,
):
    split = first_ref.shape[1]
    tall = second_ref.shape[0]
    grad_one = share_ref[0:split, :].T
    grad_one_ref[...] = grad_one
    state_one_ref[...] = velocity_damping * first_ref[...] + grad_one
    grad_two_ref[...] = share_ref[split : split + tall, :]
    state_two_ref[...] = velocity_damping * second_ref[...] + grad_two_ref[...]
    gram_one = mul_nt(state_one_ref[...], state_one_ref[...], HIGH)
    gram_two = mul_tn(state_two_ref[...], state_two_ref[...], HIGH)
    even = bit_ref[0] == 0
    keep_ref[...] = jnp.where(even, gram_one, gram_two)
    send_ref[...] = jnp.where(even, gram_two, gram_one)


def prepare(bit, share, first, second):
    square = ((first.shape[0], first.shape[0]), F32)
    one, two = (first.shape, F32), (second.shape, F32)
    return call(
        prepare_kernel, "prepare", [SMEM] + [VMEM] * 3, [one, two, one, two, square, square], [],
        24, (bit, share, first, second), 2e9, 6e6,
    )


def renew_kernel(
    factors, bit_ref, mine_ref, other_ref, state_one_ref, state_two_ref, one_ref, two_ref,
    new_one_ref, new_two_ref, low_one_ref, low_two_ref,
):
    even = bit_ref[0] == 0
    poly_one = jnp.where(even, mine_ref[...], other_ref[...])
    poly_two = jnp.where(even, other_ref[...], mine_ref[...])
    new_one = one_ref[...] - (rate_matrix * factors[0]) * mul_nn(
        poly_one, state_one_ref[...], HIGH
    )
    new_one_ref[...] = new_one
    low_one_ref[...] = new_one.astype(BF16)
    new_two = two_ref[...] - (rate_matrix * factors[1]) * mul_nn(
        state_two_ref[...], poly_two, HIGH
    )
    new_two_ref[...] = new_two
    low_two_ref[...] = new_two.astype(BF16)


def renew(factors, bit, mine, other, state_one, state_two, one, two):
    outs = [(one.shape, F32), (two.shape, F32), (one.shape, BF16), (two.shape, BF16)]
    return call(
        functools.partial(renew_kernel, factors), "renew", [SMEM] + [VMEM] * 6, outs, [], 24,
        (bit, mine, other, state_one, state_two, one, two), 2e9, 6e6,
    )


def bits_of(size):
    return [1 << place for place in range(size.bit_length() - 1)]


def swap(source, axis, bit):
    size = lax.axis_size(axis)
    return lax.ppermute(source, axis, [(member, member ^ bit) for member in range(size)])


def everyone(rows):
    devices = lax.axis_size("wide") * lax.axis_size("narrow")
    copies = jnp.broadcast_to(rows[None], (devices,) + rows.shape)
    return lax.all_to_all(copies, ("wide", "narrow"), 0, 0, tiled=True)


def own_bit(axis, bit):
    return ((lax.axis_index(axis) // bit) % 2).astype(jnp.int32).reshape(1)


def scatter_sum(send, keep):
    steps = [("narrow", bit) for bit in bits_of(lax.axis_size("narrow"))]
    steps += [("wide", bit) for bit in bits_of(lax.axis_size("wide"))]
    for index, (axis, bit) in enumerate(steps):
        other = swap(send, axis, bit)
        if index + 1 == len(steps):
            return add(keep, other)
        next_axis, next_bit = steps[index + 1]
        shape = keep.shape
        if next_axis == "narrow":
            pair = (2, shape[0] // 2) + shape[1:]
            keep = keep.reshape((shape[0] // 2, 2) + shape[1:]).swapaxes(0, 1)
            other = other.reshape((shape[0] // 2, 2) + shape[1:]).swapaxes(0, 1)
            rows = pair[1] * pair[2]
        else:
            rows = keep.size // shape[-1] // 2
        keep, other = (array.reshape(2, rows, shape[-1]) for array in (keep, other))
        send, keep = split_add(own_bit(next_axis, next_bit), keep, other)
        if next_axis == "narrow":
            send, keep = (array.reshape((-1,) + shape[1:]) for array in (send, keep))


def gather(share, axis):
    held = share
    for bit in reversed(bits_of(lax.axis_size(axis))):
        held = join(own_bit(axis, bit), held, swap(held, axis, bit))
        held = held.reshape(-1, share.shape[-1])
    return held


def gather_parts(share, axis):
    held = share[None]
    for bit in reversed(bits_of(lax.axis_size(axis))):
        other = swap(held, axis, bit)
        low = (lax.axis_index(axis) // bit) % 2 == 0
        held = jnp.stack([jnp.where(low, held, other), jnp.where(low, other, held)], axis=1)
        held = held.reshape((-1,) + share.shape)
    return held


def pair_update(bit, share, states, masters, factors):
    grads_one, grads_two, state_one, state_two, send, keep = prepare(bit, share, *states)
    other = swap(send, "narrow", 1)
    rest = bits_of(lax.axis_size("narrow"))[1:]
    for axis_bit in rest:
        keep = add(keep, other)
        other = swap(keep, "narrow", axis_bit)
    result = sweeps(keep, other)
    new = renew(factors, bit, result, swap(result, "narrow", 1), state_one, state_two, *masters)
    return (grads_one, grads_two, state_one, state_two) + tuple(new)


def on_device(
    block_source,
    upstream_adjoint,
    picture_patch_extents,
    triple_matrix,
    mixer_matrix,
    expand_matrix,
    shrink_matrix,
    affine_entries,
    sharpness,
    triple_velocity,
    mixer_velocity,
    expand_velocity,
    shrink_velocity,
    affine_velocity,
    sharpness_velocity,
):
    images, slot_count, model_width = block_source.shape
    group_index = sharpness.shape[0]
    narrow_parts = lax.axis_size("narrow")
    narrow_pos = lax.axis_index("narrow")
    pair_bit = own_bit("narrow", 1)
    source = block_source.reshape(-1, model_width)
    upstream = upstream_adjoint.reshape(-1, model_width)

    (
        norm_one, query, key, value, inv, cov, attend, mixing, branch, after_mix, conv_one, act,
        stats,
    ) = front(
        images, picture_patch_extents, sharpness, source, triple_matrix, mixer_matrix,
        affine_entries,
    )
    all_stats = everyone(stats)
    (
        block_out, norm_three, hidden_low, grad_branch3, grad_hidden, grad_local, grad_bn, batch,
        tail_sums, bn_sums,
    ) = middle(
        images, picture_patch_extents, all_stats, after_mix, act, upstream,
        expand_matrix.astype(BF16), shrink_matrix.astype(BF16), affine_entries,
    )
    all_bn = everyone(bn_sums)
    fed_send, fed_keep = (
        fed_grads(shift, narrow_parts, pair_bit, norm_three, hidden_low, grad_branch3, grad_hidden)
        for shift in (1, 0)
    )
    fed_share = gather(scatter_sum(fed_send, fed_keep), "wide")
    grad_mix, grad_branch1, inner_sums, bn_totals = inner_back(
        images, picture_patch_extents, all_bn, batch, act, conv_one, grad_bn, grad_local,
        after_mix, branch, affine_entries,
    )
    incoming_adjoint, att_send, att_keep = attention_back(
        images, narrow_parts, picture_patch_extents, sharpness, pair_bit, source, norm_one, query,
        key, value, inv, cov, attend, mixing, grad_branch1, grad_mix,
        triple_matrix.astype(BF16), mixer_matrix.astype(BF16), affine_entries, tail_sums,
        inner_sums,
    )
    att_share = gather(scatter_sum(att_send, att_keep), "wide")

    def own_part(full_matrix, along):
        part_size = full_matrix.shape[along] // narrow_parts
        return lax.dynamic_slice_in_dim(full_matrix, narrow_pos * part_size, part_size, along)

    full_weights = (triple_matrix, mixer_matrix, expand_matrix, shrink_matrix)
    factors = [math.sqrt(max(1.0, full.shape[0] / full.shape[1])) for full in full_weights]
    fed = pair_update(
        pair_bit, fed_share, (expand_velocity, shrink_velocity),
        (own_part(expand_matrix, 1), own_part(shrink_matrix, 0)), factors[2:],
    )
    att_rows = att_share.shape[0] - SUM_ROWS
    att = pair_update(
        pair_bit, att_share[:att_rows], (triple_velocity, mixer_velocity),
        (own_part(triple_matrix, 1), own_part(mixer_matrix, 0)), factors[:2],
    )
    vec_share = gather_parts(att_share[att_rows:], "narrow").reshape(-1, model_width)
    vec_rows = affine_entries.shape[0]
    vec_total = vec_share[:vec_rows]
    sharpness_sum = vec_share[vec_rows, :group_index]
    vec_full = jnp.concatenate(
        [vec_total[:19], bn_totals[1:2], bn_totals[0:1], vec_total[21:]]
    )
    step_size = affine_step_size * lax.rsqrt(batch[2, 0])
    vec_state = velocity_damping * affine_velocity + vec_full
    new_vec = affine_entries - step_size * vec_state
    sharpness_buffer = velocity_damping * sharpness_velocity + sharpness_sum
    sharpness_following = sharpness - step_size * sharpness_buffer
    return (
        block_out.reshape(block_source.shape),
        incoming_adjoint.reshape(block_source.shape),
        att[0],
        att[1],
        fed[0],
        fed[1],
        vec_full,
        sharpness_sum,
        att[4],
        att[5],
        fed[4],
        fed[5],
        att[2],
        att[3],
        fed[2],
        fed[3],
        att[6],
        att[7],
        fed[6],
        fed[7],
        new_vec,
        vec_state,
        sharpness_following,
        sharpness_buffer,
    )


def solution(mesh):
    return jax.shard_map(
        on_device,
        mesh=mesh,
        in_specs=(
            P(("wide", "narrow"), None, None),
            P(("wide", "narrow"), None, None),
            P(("wide", "narrow"), None),
            P(),
            P(),
            P(),
            P(),
            P(),
            P(),
            P(None, "narrow"),
            P("narrow", None),
            P(None, "narrow"),
            P("narrow", None),
            P(),
            P(),
        ),
        out_specs=(
            P(("wide", "narrow"), None, None),
            P(("wide", "narrow"), None, None),
            P(None, "narrow"),
            P("narrow", None),
            P(None, "narrow"),
            P("narrow", None),
            P(),
            P(),
            P(None, "narrow"),
            P("narrow", None),
            P(None, "narrow"),
            P("narrow", None),
            P(None, "narrow"),
            P("narrow", None),
            P(None, "narrow"),
            P("narrow", None),
            P(None, "narrow"),
            P("narrow", None),
            P(None, "narrow"),
            P("narrow", None),
            P(),
            P(),
            P(),
            P(),
        ),
        check_vma=False,
    )
```

```python
import functools
import math

import jax
import jax.numpy as jnp
from jax import lax
from jax.experimental import pallas as pl
from jax.experimental.pallas import tpu as pltpu
from jax.sharding import PartitionSpec as P

GRID = 24
NS_STEPS = 5
SUM_ROWS = 64

layer_eps = 1e-06
unit_eps = 1e-06
batch_eps = 1e-05
frob_eps = 1e-07
velocity_damping = 0.5
rate_matrix = 0.25
affine_step_size = 0.2
coef_first = 3.4445
coef_second = -4.775
coef_third = 2.0315
root_half = 0.7071067811865476
inverse_root_tau = 0.3989422804014327
HIGH = lax.Precision.HIGH
F32 = jnp.float32
BF16 = jnp.bfloat16


def mul_nn(left, right, precision=None):
    return lax.dot_general(
        left, right, (((1,), (0,)), ((), ())), precision=precision, preferred_element_type=F32
    )


def mul_nt(left, right, precision=None):
    return lax.dot_general(
        left, right, (((1,), (1,)), ((), ())), precision=precision, preferred_element_type=F32
    )


def mul_tn(left, right, precision=None):
    return lax.dot_general(
        left, right, (((0,), (0,)), ((), ())), precision=precision, preferred_element_type=F32
    )


def fold_rows(source):
    total = source[0:8]
    for start in range(8, source.shape[0], 8):
        total = total + source[start : start + 8]
    return total


def row_sum(total):
    return jnp.sum(total, axis=0, keepdims=True)


def norm_rows(source):
    centre = source - jnp.mean(source, axis=-1, keepdims=True)
    inverse = lax.rsqrt(jnp.mean(centre * centre, axis=-1, keepdims=True) + layer_eps)
    return centre * inverse, inverse


def norm_back(grad_norm, normal, inverse, gain):
    scaled = grad_norm * gain
    return inverse * (
        scaled
        - jnp.mean(scaled, axis=-1, keepdims=True)
        - normal * jnp.mean(scaled * normal, axis=-1, keepdims=True)
    )


def normal_cdf(source):
    return 0.5 * (1.0 + lax.erf(source * root_half))


def density(source):
    return jnp.exp(-0.5 * source * source) * inverse_root_tau


def loop(start, stop, body, carry, unroll=1):
    return lax.fori_loop(start, stop, body, carry, unroll=unroll)


def here(row):
    return pl.ds(pl.multiple_of(row * GRID, 8), GRID)


class Rows:
    def __init__(self, extent_ref, width):
        self.extent_ref = extent_ref
        self.column = lax.broadcasted_iota(jnp.int32, (GRID, width), 0)

    def inside(self, row):
        image = row // GRID
        limit = jnp.where(
            row - image * GRID < self.extent_ref[image, 0], self.extent_ref[image, 1], 0
        )
        return self.column < limit

    def after(self, value):
        return jnp.where(self.column == 0, 0.0, pltpu.roll(value, 1, 0))

    def before(self, value):
        return jnp.where(self.column == GRID - 1, 0.0, pltpu.roll(value, GRID - 1, 0))

    def convolve(self, plane, row, tap):
        columns = [None] * 3
        for down, source in enumerate(three_rows(plane, row)):
            for across in range(3):
                term = source * tap(3 * down + across)
                columns[across] = term if down == 0 else columns[across] + term
        return columns[1] + self.after(columns[0]) + self.before(columns[2])


def padded(row):
    return row + 2 * (row // GRID) + 1


def three_rows(plane, row):
    first = padded(row) - 1
    for down in range(3):
        yield plane[here(first + down), :]


def clear_edges(plane, images):
    edge = jnp.zeros((GRID, plane.shape[1]), F32)
    for image in range(images):
        base = image * (GRID + 2) * GRID
        plane[base : base + GRID, :] = edge
        plane[base + (GRID + 1) * GRID : base + (GRID + 2) * GRID, :] = edge


def plane_of(images, width):
    return pltpu.VMEM((images * (GRID + 2) * GRID, width), F32)


VMEM = pl.BlockSpec(memory_space=pltpu.VMEM)
SMEM = pl.BlockSpec(memory_space=pltpu.SMEM)


ANY = pl.BlockSpec(memory_space=pl.ANY)


def call(kernel, name, spaces, outs, scratch, limit, args, flops=0, size=0, later=()):
    inputs, extra = len(args), len(later)

    def body(*refs):
        kernel(*refs[:inputs], *refs[inputs + extra :])

    return pl.pallas_call(
        body,
        in_specs=list(spaces) + [ANY] * extra,
        out_specs=[VMEM] * len(outs),
        out_shape=[jax.ShapeDtypeStruct(shape, dtype) for shape, dtype in outs],
        scratch_shapes=scratch,
        compiler_params=pltpu.CompilerParams(vmem_limit_bytes=limit << 20),
        cost_estimate=pl.CostEstimate(
            flops=int(flops), bytes_accessed=int(size), transcendentals=0
        ),
        name=name,
    )(*args, *later)


def merge_stats(one, two):
    shift = one[0] / one[2] - two[0] / two[2]
    count = one[2] + two[2]
    spread = one[1] + two[1] + shift * shift * (one[2] * two[2] / count)
    return one[0] + two[0], spread, count


def get_rows(ref):
    return [ref[row : row + 1, :] for row in range(ref.shape[0])]


def put_rows(ref, values):
    for row, value in enumerate(values):
        ref[row : row + 1, :] = value


def merge_kernel(held_ref, other_ref, out_ref):
    put_rows(out_ref, merge_stats(get_rows(held_ref), get_rows(other_ref)))


def merge(held, other):
    return call(
        merge_kernel, "merge_rows", [VMEM, VMEM], [(held.shape, F32)], [], 1, (held, other), 1e4,
        1e4,
    )[0]


def front_kernel(
    images, extent_ref, sharp_ref, x_ref, wq_ref, wp_ref, aff_ref,
    norm_ref, query_ref, key_ref, value_ref, inv_ref, cov_ref, attend_ref, mixing_ref,
    branch_ref, mix_ref, conv_ref, act_ref, stat_ref,
    joined, plane,
):
    tokens, width = x_ref.shape
    slots = tokens // images
    heads = sharp_ref.shape[0]
    head = width // heads
    rows = Rows(extent_ref, width)
    clear_edges(plane, images)
    zero = jnp.zeros((8, width), F32)

    def aff(row):
        return aff_ref[row : row + 1, :]

    def first(step, carry):
        place = pl.ds(pl.multiple_of(step * 48, 16), 48)
        normal, _ = norm_rows(x_ref[place, :].astype(F32))
        norm_ref[place, :] = (normal * aff(0) + aff(1)).astype(BF16)
        return carry

    loop(0, tokens // 48, first, 0, unroll=4)
    joined[...] = mul_nn(norm_ref[...], wq_ref[...].astype(BF16))

    def second(row, carry):
        query_sum, key_sum = carry
        at = here(row)
        inside = rows.inside(row)
        query = jnp.where(inside, joined[at, :width] + aff(2), 0.0)
        key = jnp.where(inside, joined[at, width : 2 * width] + aff(3), 0.0)
        query_ref[at, :] = query
        key_ref[at, :] = key
        value_ref[at, :] = joined[at, 2 * width :] + aff(4)
        return query_sum + fold_rows(query * query), key_sum + fold_rows(key * key)

    for image in range(images):
        span = slice(image * slots, (image + 1) * slots)
        low, high = image * GRID, (image + 1) * GRID
        query_sum, key_sum = loop(low, high, second, (zero, zero), unroll=2)
        query_inv = lax.rsqrt(row_sum(query_sum) + unit_eps)
        key_inv = lax.rsqrt(row_sum(key_sum) + unit_eps)
        inv_ref[2 * image : 2 * image + 1, :] = query_inv
        inv_ref[2 * image + 1 : 2 * image + 2, :] = key_inv

        def third(row, carry):
            at = here(row)
            query_ref[at, :] = query_ref[at, :] * query_inv
            key_ref[at, :] = key_ref[at, :] * key_inv
            return carry

        loop(low, high, third, 0, unroll=2)
        cov_ref[image] = mul_tn(query_ref[span, :], key_ref[span, :], HIGH)
        lane = lax.broadcasted_iota(jnp.int32, (head, width), 1)
        for group in range(heads):
            part = slice(group * head, (group + 1) * head)
            own = (lane >= group * head) & (lane < (group + 1) * head)
            scores = jnp.where(own, cov_ref[image, part, :] * sharp_ref[group], -jnp.inf)
            raised = jnp.exp(scores - jnp.max(scores, axis=-1, keepdims=True))
            attend_ref[image, part, :] = raised / jnp.sum(raised, axis=-1, keepdims=True)
        mixing_ref[span, :] = mul_nt(value_ref[span, :], attend_ref[image], HIGH).astype(BF16)
    branch_ref[...] = mul_nn(mixing_ref[...], wp_ref[...].astype(BF16))

    def fourth(row, carry):
        at = here(row)
        inside = rows.inside(row)
        branch = branch_ref[at, :] + aff(5)
        branch_ref[at, :] = branch
        after = x_ref[at, :].astype(F32) + jnp.where(inside, aff(6) * branch, 0.0)
        mix_ref[at, :] = after
        normal, _ = norm_rows(after)
        plane[here(padded(row)), :] = jnp.where(inside, normal * aff(7) + aff(8), 0.0)
        return carry

    loop(0, images * GRID, fourth, 0, unroll=8)

    def fifth(row, total):
        at = here(row)
        summed = rows.convolve(plane, row, lambda index: aff(9 + index)) + aff(18)
        conv_ref[at, :] = summed
        active = summed * normal_cdf(summed)
        act_ref[at, :] = active
        return total + fold_rows(jnp.where(rows.inside(row), active, 0.0))

    for image in range(images):
        low, high = image * GRID, (image + 1) * GRID
        act_sum = row_sum(loop(low, high, fifth, zero, unroll=2))
        count = (extent_ref[image, 0] * extent_ref[image, 1]).astype(F32)
        centre = act_sum / count

        def sixth(row, total):
            shifted = jnp.where(rows.inside(row), act_ref[here(row), :] - centre, 0.0)
            return total + fold_rows(shifted * shifted)

        spread = row_sum(loop(low, high, sixth, zero, unroll=4))
        own = (act_sum, spread, jnp.full_like(centre, count))
        stats = own if image == 0 else merge_stats(stats, own)
    put_rows(stat_ref, stats)


def front(images, extents, sharpness, source, wq, wp, aff, later):
    tokens, width = source.shape
    full, low, square = ((tokens, width), F32), ((tokens, width), BF16), ((images, width, width), F32)
    outs = [
        low, full, full, full, ((2 * images, width), F32), square, square, low,
        full, full, full, full, ((3, width), F32),
    ]
    return call(
        functools.partial(front_kernel, images), "front",
        [SMEM, SMEM, VMEM, VMEM, VMEM, VMEM], outs,
        [pltpu.VMEM((tokens, 3 * width), F32), plane_of(images, width)], 12,
        (extents, sharpness, source, wq, wp, aff), 2e10, 3e7, later,
    )


def middle_kernel(
    images, extent_ref, stat_ref, stat_two_ref, mix_ref, act_ref, up_ref, w1_ref, w2_ref, aff_ref,
    out_ref, norm_ref, hidlow_ref, gbranch_ref, ghid_ref, glocal_ref, gbn_ref, batch_ref,
    sum_ref, bn_ref,
    hidden, dhidden, conv_s, normal_s, inverse_s, branch_s, plane, grad_plane,
):
    tokens, width = mix_ref.shape
    inner = w1_ref.shape[1]
    rows = Rows(extent_ref, width)
    clear_edges(plane, images)
    clear_edges(grad_plane, images)
    zero = jnp.zeros((8, width), F32)
    all_rows = images * GRID

    def aff(row):
        return aff_ref[row : row + 1, :]

    act_sum, spread, tally = merge_stats(get_rows(stat_ref), get_rows(stat_two_ref))
    centre = act_sum / tally
    inverse_std = lax.rsqrt(spread / tally + batch_eps)
    batch_ref[0:1, :] = centre
    batch_ref[1:2, :] = inverse_std
    batch_ref[2:3, :] = tally

    def first(row, carry):
        inside = rows.inside(row)
        unit = (act_ref[here(row), :] - centre) * inverse_std
        plane[here(padded(row)), :] = jnp.where(inside, unit * aff(19) + aff(20), 0.0)
        return carry

    loop(0, all_rows, first, 0, unroll=2)

    def second(row, carry):
        at = here(row)
        inside = rows.inside(row)
        summed = rows.convolve(plane, row, lambda index: aff(21 + index)) + aff(30)
        conv_s[at, :] = summed
        after = mix_ref[at, :] + jnp.where(inside, aff(31) * summed, 0.0)
        branch_s[at, :] = after
        return carry

    loop(0, all_rows, second, 0, unroll=2)

    def second_norm(step, carry):
        at = pl.ds(pl.multiple_of(step * 48, 16), 48)
        normal, inverse = norm_rows(branch_s[at, :])
        normal_s[at, :] = normal
        inverse_s[at, :] = inverse
        norm_ref[at, :] = (normal * aff(32) + aff(33)).astype(BF16)
        return carry

    loop(0, tokens // 48, second_norm, 0, unroll=4)

    def third(row, total):
        at = here(row)
        grad = jnp.where(rows.inside(row), up_ref[at, :].astype(F32) * aff(39), 0.0).astype(BF16)
        gbranch_ref[at, :] = grad
        return total + fold_rows(grad.astype(F32))

    sum_ref[17:18, :] = row_sum(loop(0, all_rows, third, zero, unroll=2))
    slots = tokens // images
    quarters = inner // width
    bias_sums = [zero] * quarters
    for image in range(images):
        span = slice(image * slots, (image + 1) * slots)
        hidden[...] = mul_nn(norm_ref[span, :], w1_ref[...])
        dhidden[...] = mul_nt(gbranch_ref[span, :], w2_ref[...])
        for quarter in range(quarters):
            cols = slice(quarter * width, (quarter + 1) * width)
            bias = aff(34 + quarter)

            def fourth(step, total):
                at = pl.ds(pl.multiple_of(step * 16, 16), 16)
                to = pl.ds(pl.multiple_of(image * slots + step * 16, 16), 16)
                value = hidden[at, cols] + bias
                cdf = normal_cdf(value)
                hidlow_ref[to, cols] = (value * cdf).astype(BF16)
                grad = (dhidden[at, cols] * (cdf + value * density(value))).astype(BF16)
                ghid_ref[to, cols] = grad
                return total + fold_rows(grad.astype(F32))

            bias_sums[quarter] = loop(0, slots // 16, fourth, bias_sums[quarter], unroll=2)
        gbn_ref[span, :] = mul_nt(ghid_ref[span, :], w1_ref[...])
        glocal_ref[span, :] = mul_nn(hidlow_ref[span, :], w2_ref[...])
    for quarter in range(quarters):
        sum_ref[13 + quarter : 14 + quarter, :] = row_sum(bias_sums[quarter])

    def fifth(row, total):
        at = here(row)
        inside = rows.inside(row)
        branch = jnp.where(inside, glocal_ref[at, :] + aff(38), 0.0)
        out_ref[at, :] = (branch_s[at, :] + aff(39) * branch).astype(BF16)
        return total + fold_rows(up_ref[at, :].astype(F32) * branch)

    sum_ref[18:19, :] = row_sum(loop(0, all_rows, fifth, zero, unroll=2))

    def sixth(row, carry):
        gain_sum, shift_sum, scale_sum, bias_sum = carry
        at = here(row)
        inside = rows.inside(row)
        grad_norm = gbn_ref[at, :]
        normal = normal_s[at, :]
        grad = up_ref[at, :].astype(F32) + norm_back(grad_norm, normal, inverse_s[at, :], aff(32))
        glocal_ref[at, :] = grad
        kept = jnp.where(inside, grad, 0.0)
        scaled = kept * aff(31)
        grad_plane[here(padded(row)), :] = scaled
        return (
            gain_sum + fold_rows(grad_norm * normal), shift_sum + fold_rows(grad_norm),
            scale_sum + fold_rows(kept * conv_s[at, :]), bias_sum + fold_rows(scaled),
        )

    gain_sum, shift_sum, scale_sum, bias_sum = loop(0, all_rows, sixth, (zero,) * 4, unroll=6)
    sum_ref[11:12, :] = row_sum(gain_sum)
    sum_ref[12:13, :] = row_sum(shift_sum)
    sum_ref[10:11, :] = row_sum(scale_sum)
    sum_ref[9:10, :] = row_sum(bias_sum)

    def seventh(row, carry):
        bias_bn, gain_bn = carry
        at = here(row)
        summed = rows.convolve(grad_plane, row, lambda index: aff(29 - index))
        summed = jnp.where(rows.inside(row), summed, 0.0)
        gbn_ref[at, :] = summed
        unit = (act_ref[at, :] - centre) * inverse_std
        return bias_bn + fold_rows(summed), gain_bn + fold_rows(summed * unit)

    bias_bn, gain_bn = loop(0, all_rows, seventh, (zero, zero), unroll=2)
    bn_ref[0:1, :] = row_sum(bias_bn)
    bn_ref[1:2, :] = row_sum(gain_bn)
    kernel_sums(rows, plane, grad_plane, images, sum_ref, 0)


def kernel_sums(rows, plane, grad_plane, images, sum_ref, base):
    zero = jnp.zeros((8, plane.shape[1]), F32)

    def body(row, carry):
        grad = grad_plane[here(padded(row)), :]
        grads = (rows.before(grad), grad, rows.after(grad))
        totals = list(carry)
        for down, source in enumerate(three_rows(plane, row)):
            for across in range(3):
                index = 3 * down + across
                totals[index] = totals[index] + fold_rows(grads[across] * source)
        return tuple(totals)

    totals = loop(0, images * GRID, body, (zero,) * 9)
    for index, total in enumerate(totals):
        sum_ref[base + index : base + index + 1, :] = row_sum(total)


def middle(images, extents, stats, stats_two, after_mix, act, upstream, w1, w2, aff):
    tokens, width = after_mix.shape
    inner = w1.shape[1]
    full, low, wide = ((tokens, width), F32), ((tokens, width), BF16), ((tokens, inner), BF16)
    outs = [
        low, low, wide, low, wide, full, full, ((3, width), F32), ((19, width), F32), ((2, width), F32),
    ]
    return call(
        functools.partial(middle_kernel, images), "middle",
        [SMEM] + [VMEM] * 8, outs,
        [
            pltpu.VMEM((tokens // images, inner), F32), pltpu.VMEM((tokens // images, inner), F32),
            pltpu.VMEM((tokens, width), F32), pltpu.VMEM((tokens, width), F32),
            pltpu.VMEM((tokens, 1), F32), pltpu.VMEM((tokens, width), F32),
            plane_of(images, width), plane_of(images, width),
        ], 18,
        (extents, stats, stats_two, after_mix, act, upstream, w1, w2, aff), 3e10, 4e7,
    )


def fed_grads_kernel(shift, bit_ref, norm_ref, hidlow_ref, gbranch_ref, ghid_ref, out_ref):
    width = norm_ref.shape[1]
    pairs = out_ref.shape[0]
    size = ghid_ref.shape[1] // (2 * pairs)
    low = bit_ref[0] if shift == 0 else 1 - bit_ref[0]
    for pair in range(pairs):
        cols = pl.ds(pl.multiple_of((2 * pair + low) * size, 128), size)
        out_ref[pair, 0:size, :] = mul_tn(ghid_ref[:, cols], norm_ref[...])
        out_ref[pair, size : 2 * size, :] = mul_tn(hidlow_ref[:, cols], gbranch_ref[...])


def fed_grads(shift, parts, bit, norm, hidlow, gbranch, ghid):
    width, inner = norm.shape[1], ghid.shape[1]
    return call(
        functools.partial(fed_grads_kernel, shift), "fed_grads",
        [SMEM] + [VMEM] * 4, [((parts // 2, 2 * inner // parts, width), F32)], [], 6,
        (bit, norm, hidlow, gbranch, ghid), 3e9, 1e7,
    )[0]


def inner_back_kernel(
    images, extent_ref, total_ref, total_two_ref, batch_ref, act_ref, conv_ref, gbn_ref, glocal_ref, mix_ref,
    branch_ref, aff_ref, gmix_ref, gbranch_ref, sum_ref, bn_ref,
    normal_s, inverse_s, plane, grad_plane,
):
    tokens, width = act_ref.shape
    rows = Rows(extent_ref, width)
    clear_edges(plane, images)
    clear_edges(grad_plane, images)
    zero = jnp.zeros((8, width), F32)
    all_rows = images * GRID

    def aff(row):
        return aff_ref[row : row + 1, :]

    totals = total_ref[...] + total_two_ref[...]
    bn_ref[...] = totals
    centre, inverse_std, tally = batch_ref[0:1, :], batch_ref[1:2, :], batch_ref[2:3, :]
    bias_mean, gain_mean = totals[0:1, :] / tally, totals[1:2, :] / tally
    factor = aff(19) * inverse_std

    def first(row, total):
        at = here(row)
        unit = (act_ref[at, :] - centre) * inverse_std
        value = conv_ref[at, :]
        slope = normal_cdf(value) + value * density(value)
        grad = factor * (gbn_ref[at, :] - (bias_mean + unit * gain_mean)) * slope
        grad = jnp.where(rows.inside(row), grad, 0.0)
        grad_plane[here(padded(row)), :] = grad
        return total + fold_rows(grad)

    sum_ref[13:14, :] = row_sum(loop(0, all_rows, first, zero, unroll=2))

    def second(row, carry):
        at = here(row)
        normal, inverse = norm_rows(mix_ref[at, :])
        normal_s[at, :] = normal
        inverse_s[at, :] = inverse
        plane[here(padded(row)), :] = jnp.where(rows.inside(row), normal * aff(7) + aff(8), 0.0)
        return carry

    loop(0, all_rows, second, 0, unroll=8)
    kernel_sums(rows, plane, grad_plane, images, sum_ref, 4)

    def third(row, carry):
        summed = rows.convolve(grad_plane, row, lambda index: aff(17 - index))
        gmix_ref[here(row), :] = jnp.where(rows.inside(row), summed, 0.0)
        return carry

    loop(0, all_rows, third, 0, unroll=2)

    def fourth(row, carry):
        gain_sum, shift_sum, scale_sum, bias_sum = carry
        at = here(row)
        grad_norm, normal = gmix_ref[at, :], normal_s[at, :]
        grad = glocal_ref[at, :] + norm_back(grad_norm, normal, inverse_s[at, :], aff(7))
        gmix_ref[at, :] = grad
        kept = jnp.where(rows.inside(row), grad, 0.0)
        low = (kept * aff(6)).astype(BF16)
        gbranch_ref[at, :] = low
        return (
            gain_sum + fold_rows(grad_norm * normal), shift_sum + fold_rows(grad_norm),
            scale_sum + fold_rows(kept * branch_ref[at, :]), bias_sum + fold_rows(low.astype(F32)),
        )

    gain_sum, shift_sum, scale_sum, bias_sum = loop(0, all_rows, fourth, (zero,) * 4, unroll=6)
    sum_ref[0:1, :] = row_sum(bias_sum)
    sum_ref[1:2, :] = row_sum(scale_sum)
    sum_ref[2:3, :] = row_sum(gain_sum)
    sum_ref[3:4, :] = row_sum(shift_sum)


def inner_back(
    images, extents, totals, totals_two, batch, act, conv, gbn, glocal, after_mix, branch, aff,
    later,
):
    tokens, width = act.shape
    outs = [((tokens, width), F32), ((tokens, width), BF16), ((14, width), F32), ((2, width), F32)]
    return call(
        functools.partial(inner_back_kernel, images), "inner_back",
        [SMEM] + [VMEM] * 10, outs,
        [
            pltpu.VMEM((tokens, width), F32), pltpu.VMEM((tokens, 1), F32),
            plane_of(images, width), plane_of(images, width),
        ], 10,
        (extents, totals, totals_two, batch, act, conv, gbn, glocal, after_mix, branch, aff), 2e10, 3e7,
        later,
    )


def attention_back_kernel(
    images, extent_ref, sharp_ref, query_ref, key_ref, value_ref, inv_ref, cov_ref, attend_ref,
    gbranch_ref, wp_ref, gjoined, head_ref,
    gmixing, gscore, gquery, gkey,
):
    tokens, width = query_ref.shape
    slots = tokens // images
    heads = sharp_ref.shape[0]
    head = width // heads
    rows = Rows(extent_ref, width)
    zero = jnp.zeros((8, width), F32)

    gmixing[...] = mul_nt(gbranch_ref[...], wp_ref[...])
    lane = lax.broadcasted_iota(jnp.int32, (1, width), 1)
    sharp_sum = jnp.zeros((1, width), F32)
    bias = [zero] * 3
    for image in range(images):
        span = slice(image * slots, (image + 1) * slots)
        low, high = image * GRID, (image + 1) * GRID
        gscore[...] = mul_tn(gmixing[span, :], value_ref[span, :], HIGH)
        for group in range(heads):
            part = slice(group * head, (group + 1) * head)
            attend = attend_ref[image, part, :]
            grad = gscore[part, :]
            grad = attend * (grad - jnp.sum(attend * grad, axis=-1, keepdims=True))
            gscore[part, :] = grad * sharp_ref[group]
            amount = jnp.sum(
                jnp.sum(grad * cov_ref[image, part, :], axis=0, keepdims=True),
                axis=1, keepdims=True,
            )
            sharp_sum = sharp_sum + jnp.where(lane == group, amount, 0.0)
        gquery[...] = mul_nt(key_ref[span, :], gscore[...], HIGH)
        gkey[...] = mul_nn(query_ref[span, :], gscore[...], HIGH)
        gmixing[span, :] = mul_nn(gmixing[span, :], attend_ref[image], HIGH)

        def first(row, carry):
            query_dot, key_dot = carry
            at = here(row)
            to = here(row - low)
            return (
                query_dot + fold_rows(gquery[to, :] * query_ref[at, :]),
                key_dot + fold_rows(gkey[to, :] * key_ref[at, :]),
            )

        query_dot, key_dot = loop(low, high, first, (zero, zero), unroll=2)
        query_dot, key_dot = row_sum(query_dot), row_sum(key_dot)
        query_inv = inv_ref[2 * image : 2 * image + 1, :]
        key_inv = inv_ref[2 * image + 1 : 2 * image + 2, :]

        def second(pair, carry):
            totals = list(carry)
            thirds = ([], [], [])
            for row in (2 * pair, 2 * pair + 1):
                at = here(row)
                to = here(row - low)
                inside = rows.inside(row)
                grad = query_inv * (gquery[to, :] - query_ref[at, :] * query_dot)
                thirds[0].append(jnp.where(inside, grad, 0.0))
                grad = key_inv * (gkey[to, :] - key_ref[at, :] * key_dot)
                thirds[1].append(jnp.where(inside, grad, 0.0))
                thirds[2].append(gmixing[at, :])
            at = pl.ds(pl.multiple_of(pair * 2 * GRID, 16), 2 * GRID)
            for third in range(3):
                value = jnp.concatenate(thirds[third], axis=0).astype(BF16)
                gjoined[at, third * width : (third + 1) * width] = value
                totals[third] = totals[third] + fold_rows(value.astype(F32))
            return tuple(totals)

        bias = loop(low // 2, high // 2, second, tuple(bias))
    put_rows(head_ref, [row_sum(total) for total in bias] + [sharp_sum])


def attention_back(
    images, extents, sharpness, query, key, value, inv, cov, attend, gbranch, wp,
):
    tokens, width = query.shape
    slots = tokens // images
    return call(
        functools.partial(attention_back_kernel, images), "attention_back",
        [SMEM] * 2 + [VMEM] * 8, [((tokens, 3 * width), BF16), ((4, width), F32)],
        [
            pltpu.VMEM((tokens, width), F32), pltpu.VMEM((width, width), F32),
            pltpu.VMEM((slots, width), F32), pltpu.VMEM((slots, width), F32),
        ], 10,
        (extents, sharpness, query, key, value, inv, cov, attend, gbranch, wp), 2e10, 2e7,
    )


def att_grads_kernel(
    bits_ref, norm_ref, gjoined_ref, mixing_ref, gbranch_ref, head_ref, inner_ref, tail_ref,
    outer_ref, send_ref, keep_ref, matrix, vector,
):
    width = norm_ref.shape[1]
    vector[...] = jnp.zeros_like(vector)
    vector[0:2, :] = outer_ref[...]
    vector[2:5, :] = head_ref[0:3, :]
    vector[5:19, :] = inner_ref[...]
    vector[21:40, :] = tail_ref[...]
    vector[40:41, :] = head_ref[3:4, :]
    pairs = send_ref.shape[0]
    matrix[0 : 3 * width, :] = mul_tn(gjoined_ref[...], norm_ref[...])
    matrix[3 * width :, :] = mul_tn(mixing_ref[...], gbranch_ref[...])
    joined_rows, mixer_rows = 3 * width // (2 * pairs), width // (2 * pairs)
    for pair in range(pairs):
        for target, place in ((keep_ref, bits_ref[0]), (send_ref, 1 - bits_ref[0])):
            part = 2 * pair + place
            last = joined_rows + mixer_rows
            at = pl.ds(pl.multiple_of(part * joined_rows, 8), joined_rows)
            target[pair, 0:joined_rows, :] = matrix[at, :]
            at = pl.ds(pl.multiple_of(3 * width + part * mixer_rows, 8), mixer_rows)
            target[pair, joined_rows:last, :] = matrix[at, :]
            at = pl.ds(pl.multiple_of(part * SUM_ROWS, 8), SUM_ROWS)
            target[pair, last : last + SUM_ROWS, :] = vector[at, :]


def att_grads(parts, bits, norm, gjoined, mixing, gbranch, head, inner, tail, outer):
    width = norm.shape[1]
    share = ((parts // 2, 4 * width // parts + SUM_ROWS, width), F32)
    return call(
        att_grads_kernel, "att_grads", [SMEM] + [VMEM] * 8, [share, share],
        [pltpu.VMEM((4 * width, width), F32), pltpu.VMEM((parts * SUM_ROWS, width), F32)], 8,
        (bits, norm, gjoined, mixing, gbranch, head, inner, tail, outer), 2e9, 8e6,
    )


def outer_back_kernel(x_ref, gjoined_ref, gmix_ref, wq_ref, aff_ref, incoming_ref, outer_ref, gnorm):
    tokens, width = x_ref.shape
    zero = jnp.zeros((8, width), F32)
    gnorm[...] = mul_nt(gjoined_ref[...], wq_ref[...])

    def body(step, carry):
        gain_sum, shift_sum = carry
        at = pl.ds(pl.multiple_of(step * 48, 16), 48)
        normal, inverse = norm_rows(x_ref[at, :].astype(F32))
        grad = gnorm[at, :]
        incoming_ref[at, :] = gmix_ref[at, :] + norm_back(grad, normal, inverse, aff_ref[0:1, :])
        return gain_sum + fold_rows(grad * normal), shift_sum + fold_rows(grad)

    put_rows(outer_ref, map(row_sum, loop(0, tokens // 48, body, (zero, zero), unroll=4)))


def outer_back(source, gjoined, gmix, wq, aff, later):
    tokens, width = source.shape
    return call(
        outer_back_kernel, "outer_back", [VMEM] * 5,
        [((tokens, width), F32), ((2, width), F32)], [pltpu.VMEM((tokens, width), F32)], 6,
        (source, gjoined, gmix, wq, aff), 5e9, 1e7, later,
    )


def row_blocks(rows):
    step = next(size for size in (32, 24, 16, 8, rows) if rows % size == 0)
    return rows // step, step


def split_add_kernel(place, bits_ref, held_ref, other_ref, send_ref, keep_ref):
    bit = bits_ref[place]
    count, step = row_blocks(held_ref.shape[1])

    def body(index, carry):
        at = pl.ds(pl.multiple_of(index * step, 8) if step % 8 == 0 else index * step, step)
        send_ref[at, :] = held_ref[1 - bit, at, :] + other_ref[1 - bit, at, :]
        keep_ref[at, :] = held_ref[bit, at, :] + other_ref[bit, at, :]
        return carry

    loop(0, count, body, 0)


def split_add(bits, place, held, other):
    half = (held.shape[-2:], F32)
    return call(
        functools.partial(split_add_kernel, place), "split_add", [SMEM, VMEM, VMEM], [half, half],
        [], 2, (bits, held, other), held.size, 16 * held.size,
    )


def add_kernel(held_ref, other_ref, out_ref):
    count, step = row_blocks(held_ref.shape[0])

    def body(index, carry):
        at = pl.ds(pl.multiple_of(index * step, 8) if step % 8 == 0 else index * step, step)
        out_ref[at, :] = held_ref[at, :] + other_ref[at, :]
        return carry

    loop(0, count, body, 0)


def add(held, other):
    return call(
        add_kernel, "add_rows", [VMEM, VMEM], [(held.shape, F32)], [], 2, (held, other),
        held.size, 12 * held.size,
    )[0]


def join_kernel(place, bits_ref, held_ref, other_ref, out_ref):
    bit = bits_ref[place]
    count, step = row_blocks(held_ref.shape[0])

    def body(index, carry):
        at = pl.ds(pl.multiple_of(index * step, 8) if step % 8 == 0 else index * step, step)
        out_ref[bit, at, :] = held_ref[at, :]
        out_ref[1 - bit, at, :] = other_ref[at, :]
        return carry

    loop(0, count, body, 0)


def join(bits, place, held, other):
    return call(
        functools.partial(join_kernel, place), "join_rows", [SMEM, VMEM, VMEM],
        [((2,) + held.shape, F32)], [], 2, (bits, held, other), held.size, 16 * held.size,
    )[0]


def sweeps_kernel(mine_ref, other_ref, out_ref, now, step, total):
    size = mine_ref.shape[0]
    row = lax.broadcasted_iota(jnp.int32, (size, size), 0)
    diagonal = row == lax.broadcasted_iota(jnp.int32, (size, size), 1)
    now[...] = mine_ref[...] + other_ref[...]
    trace = jnp.where(diagonal, now[...], 0.0)
    trace = jnp.sum(jnp.sum(trace, axis=0, keepdims=True), axis=1, keepdims=True)
    norm = jnp.sqrt(trace) + frob_eps
    now[...] = now[...] / (norm * norm)
    for sweep_index in range(NS_STEPS):
        square = mul_nn(now[...], now[...], HIGH)
        step[...] = (
            jnp.where(diagonal, coef_first, 0.0) + coef_second * now[...] + coef_third * square
        )
        if sweep_index == 0:
            total[...] = step[...] / norm
        elif sweep_index < NS_STEPS - 1:
            total[...] = mul_nn(step[...], total[...], HIGH)
        else:
            out_ref[...] = mul_nn(step[...], total[...], HIGH)
        if sweep_index < NS_STEPS - 1:
            now[...] = mul_nn(mul_nn(step[...], now[...], HIGH), step[...], HIGH)


def sweeps(mine, other):
    square = pltpu.VMEM(mine.shape, F32)
    return call(
        sweeps_kernel, "sweeps", [VMEM, VMEM], [(mine.shape, F32)], [square] * 3, 8,
        (mine, other), 1e10, 4e6,
    )[0]


def prepare_kernel(
    turned, bit_ref, share_ref, first_ref, second_ref,
    grad_one_ref, grad_two_ref, state_one_ref, state_two_ref, send_ref, keep_ref,
):
    split = first_ref.shape[0 if turned else 1]
    tall = second_ref.shape[0]
    grad_one = share_ref[0:split, :]
    grad_one_ref[...] = grad_one if turned else grad_one.T
    state_one_ref[...] = velocity_damping * first_ref[...] + grad_one_ref[...]
    grad_two_ref[...] = share_ref[split : split + tall, :]
    state_two_ref[...] = velocity_damping * second_ref[...] + grad_two_ref[...]
    gram = mul_tn if turned else mul_nt
    gram_one = gram(state_one_ref[...], state_one_ref[...], HIGH)
    gram_two = mul_tn(state_two_ref[...], state_two_ref[...], HIGH)
    even = bit_ref[0] == 0
    keep_ref[...] = jnp.where(even, gram_one, gram_two)
    send_ref[...] = jnp.where(even, gram_two, gram_one)


def prepare(turned, bit, share, first, second):
    width = share.shape[1]
    square = ((width, width), F32)
    one, two = (first.shape, F32), (second.shape, F32)
    return call(
        functools.partial(prepare_kernel, turned), "prepare", [SMEM] + [VMEM] * 3,
        [one, two, one, two, square, square], [], 8, (bit, share, first, second), 2e9, 6e6,
    )


def renew_kernel(
    turned, factors, bit_ref, mine_ref, other_ref, state_one_ref, state_two_ref, one_ref, two_ref,
    new_one_ref, new_two_ref, low_one_ref, low_two_ref,
):
    even = bit_ref[0] == 0
    poly_one = jnp.where(even, mine_ref[...], other_ref[...])
    poly_two = jnp.where(even, other_ref[...], mine_ref[...])
    if turned:
        field_one = mul_nn(state_one_ref[...], poly_one, HIGH)
    else:
        field_one = mul_nn(poly_one, state_one_ref[...], HIGH)
    new_one = one_ref[...] - (rate_matrix * factors[0]) * field_one
    new_one_ref[...] = new_one
    low_one_ref[...] = new_one.astype(BF16)
    new_two = two_ref[...] - (rate_matrix * factors[1]) * mul_nn(
        state_two_ref[...], poly_two, HIGH
    )
    new_two_ref[...] = new_two
    low_two_ref[...] = new_two.astype(BF16)


def renew(turned, factors, bit, mine, other, state_one, state_two, one, two):
    outs = [(one.shape, F32), (two.shape, F32), (one.shape, BF16), (two.shape, BF16)]
    return call(
        functools.partial(renew_kernel, turned, factors), "renew", [SMEM] + [VMEM] * 6, outs, [],
        8, (bit, mine, other, state_one, state_two, one, two), 2e9, 6e6,
    )


def bits_of(size):
    return [1 << place for place in range(size.bit_length() - 1)]


def swap(source, axis, bit):
    size = lax.axis_size(axis)
    return lax.ppermute(source, axis, [(member, member ^ bit) for member in range(size)])


def axis_steps(axis):
    base = 0 if axis == "narrow" else len(bits_of(lax.axis_size("narrow")))
    return [(axis, bit, base + place) for place, bit in enumerate(bits_of(lax.axis_size(axis)))]


def all_steps():
    return axis_steps("narrow") + axis_steps("wide")


def own_bits():
    steps = all_steps()
    places = jnp.stack([lax.axis_index(axis) for axis, _, _ in steps]).astype(jnp.int32)
    return (places & jnp.array([bit for _, bit, _ in steps], jnp.int32)).clip(0, 1)


def everyone(rows, combine):
    steps = all_steps()
    for axis, bit, _ in steps[:-1]:
        rows = combine(rows, swap(rows, axis, bit))
    axis, bit, _ = steps[-1]
    return rows, swap(rows, axis, bit)


class Sum:
    def __init__(self, bits, send, keep):
        self.bits, self.send, self.keep = bits, send, keep
        self.steps = all_steps()

    def move(self):
        axis, bit, _ = self.steps.pop(0)
        self.other = swap(self.send, axis, bit)
        return self.other

    def settle(self):
        keep, other = self.keep, self.other
        if not self.steps:
            self.keep = add(keep.reshape(-1, keep.shape[-1]), other.reshape(-1, keep.shape[-1]))
            return
        axis, _, place = self.steps[0]
        shape = keep.shape
        if axis == "narrow":
            pair = (shape[0] // 2, 2) + shape[1:]
            keep, other = (array.reshape(pair).swapaxes(0, 1) for array in (keep, other))
        keep, other = (array.reshape(2, -1, shape[-1]) for array in (keep, other))
        self.send, self.keep = split_add(self.bits, place, keep, other)
        if axis == "narrow":
            self.send, self.keep = (
                array.reshape((-1,) + shape[1:]) for array in (self.send, self.keep)
            )


class Gather:
    def __init__(self, bits, share, axis):
        self.bits, self.held = bits, share
        self.steps = axis_steps(axis)[::-1]

    def move(self):
        axis, bit, self.place = self.steps.pop(0)
        self.other = swap(self.held, axis, bit)
        return self.other

    def settle(self):
        width = self.held.shape[-1]
        self.held = join(self.bits, self.place, self.held, self.other).reshape(-1, width)


def finish(work):
    while work.steps:
        work.move()
        work.settle()
    return work


def gather_parts(share, axis):
    held = share[None]
    for axis, bit, _ in reversed(axis_steps(axis)):
        other = swap(held, axis, bit)
        low = (lax.axis_index(axis) // bit) % 2 == 0
        held = jnp.stack([jnp.where(low, held, other), jnp.where(low, other, held)], axis=1)
        held = held.reshape((-1,) + share.shape)
    return held


def pair_update(turned, bits, share, states, masters, factors):
    grads_one, grads_two, state_one, state_two, send, keep = prepare(turned, bits, share, *states)
    other = swap(send, "narrow", 1)
    for axis, bit, _ in axis_steps("narrow")[1:]:
        keep = add(keep, other)
        other = swap(keep, axis, bit)
    result = sweeps(keep, other)
    new = renew(
        turned, factors, bits, result, swap(result, "narrow", 1), state_one, state_two, *masters
    )
    return [grads_one, grads_two, state_one, state_two] + list(new)


def on_device(
    block_source,
    upstream_adjoint,
    picture_patch_extents,
    triple_matrix,
    mixer_matrix,
    expand_matrix,
    shrink_matrix,
    affine_entries,
    sharpness,
    triple_velocity,
    mixer_velocity,
    expand_velocity,
    shrink_velocity,
    affine_velocity,
    sharpness_velocity,
):
    images, slot_count, model_width = block_source.shape
    group_index = sharpness.shape[0]
    narrow_parts = lax.axis_size("narrow")
    narrow_pos = lax.axis_index("narrow")
    bits = own_bits()
    source = block_source.reshape(-1, model_width)
    upstream = upstream_adjoint.reshape(-1, model_width)

    def own_part(full_matrix, along):
        part_size = full_matrix.shape[along] // narrow_parts
        return lax.dynamic_slice_in_dim(full_matrix, narrow_pos * part_size, part_size, along)

    (
        norm_one, query, key, value, inv, cov, attend, mixing, branch, after_mix, conv_one, act,
        stats,
    ) = front(
        images, picture_patch_extents, sharpness, source, triple_matrix, mixer_matrix,
        affine_entries, (bits,),
    )
    stats, stats_two = everyone(stats, merge)
    (
        block_out, norm_three, hidden_low, grad_branch3, grad_hidden, grad_local, grad_bn, batch,
        tail_sums, bn_sums,
    ) = middle(
        images, picture_patch_extents, stats, stats_two, after_mix, act, upstream,
        expand_matrix.astype(BF16), shrink_matrix.astype(BF16), affine_entries,
    )
    bn_sums, bn_two = everyone(bn_sums, add)
    fed_send, fed_keep = (
        fed_grads(shift, narrow_parts, bits, norm_three, hidden_low, grad_branch3, grad_hidden)
        for shift in (1, 0)
    )
    fed = Sum(bits, fed_send, fed_keep)
    fed.move()
    fed.settle()
    grad_mix, grad_branch1, inner_sums, bn_totals = inner_back(
        images, picture_patch_extents, bn_sums, bn_two, batch, act, conv_one, grad_bn, grad_local,
        after_mix, branch, affine_entries, (fed.send,),
    )
    grad_joined, head_sums = attention_back(
        images, picture_patch_extents, sharpness, query, key, value, inv, cov, attend,
        grad_branch1, mixer_matrix.astype(BF16),
    )
    fed.move()
    fed.settle()
    incoming_adjoint, outer_sums = outer_back(
        source, grad_joined, grad_mix, triple_matrix.astype(BF16), affine_entries, (fed.send,)
    )
    att_send, att_keep = att_grads(
        narrow_parts, bits, norm_one, grad_joined, mixing, grad_branch1, head_sums, inner_sums,
        tail_sums, outer_sums,
    )
    fed_share = finish(Gather(bits, finish(fed).keep, "wide")).held
    att_share = finish(Gather(bits, finish(Sum(bits, att_send, att_keep)).keep, "wide")).held

    full_weights = (triple_matrix, mixer_matrix, expand_matrix, shrink_matrix)
    factors = [math.sqrt(max(1.0, full.shape[0] / full.shape[1])) for full in full_weights]
    fed = pair_update(
        False, bits, fed_share, (expand_velocity, shrink_velocity),
        (own_part(expand_matrix, 1), own_part(shrink_matrix, 0)), factors[2:],
    )
    att_rows = att_share.shape[0] - SUM_ROWS
    att = pair_update(
        True, bits, att_share[:att_rows], (triple_velocity.T, mixer_velocity),
        (own_part(triple_matrix, 1).T, own_part(mixer_matrix, 0)), factors[:2],
    )
    for member in (0, 2, 4, 6):
        att[member] = att[member].T
    vec_share = gather_parts(att_share[att_rows:], "narrow").reshape(-1, model_width)
    vec_rows = affine_entries.shape[0]
    vec_total = vec_share[:vec_rows]
    sharpness_sum = vec_share[vec_rows, :group_index]
    vec_full = jnp.concatenate(
        [vec_total[:19], bn_totals[1:2], bn_totals[0:1], vec_total[21:]]
    )
    step_size = affine_step_size * lax.rsqrt(batch[2, 0])
    vec_state = velocity_damping * affine_velocity + vec_full
    new_vec = affine_entries - step_size * vec_state
    sharpness_buffer = velocity_damping * sharpness_velocity + sharpness_sum
    sharpness_following = sharpness - step_size * sharpness_buffer
    return (
        block_out.reshape(block_source.shape),
        incoming_adjoint.reshape(block_source.shape),
        att[0],
        att[1],
        fed[0],
        fed[1],
        vec_full,
        sharpness_sum,
        att[4],
        att[5],
        fed[4],
        fed[5],
        att[2],
        att[3],
        fed[2],
        fed[3],
        att[6],
        att[7],
        fed[6],
        fed[7],
        new_vec,
        vec_state,
        sharpness_following,
        sharpness_buffer,
    )


def solution(mesh):
    return jax.shard_map(
        on_device,
        mesh=mesh,
        in_specs=(
            P(("wide", "narrow"), None, None),
            P(("wide", "narrow"), None, None),
            P(("wide", "narrow"), None),
            P(),
            P(),
            P(),
            P(),
            P(),
            P(),
            P(None, "narrow"),
            P("narrow", None),
            P(None, "narrow"),
            P("narrow", None),
            P(),
            P(),
        ),
        out_specs=(
            P(("wide", "narrow"), None, None),
            P(("wide", "narrow"), None, None),
            P(None, "narrow"),
            P("narrow", None),
            P(None, "narrow"),
            P("narrow", None),
            P(),
            P(),
            P(None, "narrow"),
            P("narrow", None),
            P(None, "narrow"),
            P("narrow", None),
            P(None, "narrow"),
            P("narrow", None),
            P(None, "narrow"),
            P("narrow", None),
            P(None, "narrow"),
            P("narrow", None),
            P(None, "narrow"),
            P("narrow", None),
            P(),
            P(),
            P(),
            P(),
        ),
        check_vma=False,
    )
```

```python
import functools
import math

import jax
import jax.numpy as jnp
from jax import lax
from jax.experimental import pallas as pl
from jax.experimental.pallas import tpu as pltpu
from jax.sharding import PartitionSpec as P

GRID = 24
NS_STEPS = 5
SUM_ROWS = 48

layer_eps = 1e-06
unit_eps = 1e-06
batch_eps = 1e-05
frob_eps = 1e-07
velocity_damping = 0.5
rate_matrix = 0.25
affine_step_size = 0.2
coef_first = 3.4445
coef_second = -4.775
coef_third = 2.0315
root_half = 0.7071067811865476
inverse_root_tau = 0.3989422804014327
HIGH = lax.Precision.HIGH
F32 = jnp.float32
BF16 = jnp.bfloat16


def mul_nn(left, right, precision=None):
    return lax.dot_general(
        left, right, (((1,), (0,)), ((), ())), precision=precision, preferred_element_type=F32
    )


def mul_nt(left, right, precision=None):
    return lax.dot_general(
        left, right, (((1,), (1,)), ((), ())), precision=precision, preferred_element_type=F32
    )


def mul_tn(left, right, precision=None):
    return lax.dot_general(
        left, right, (((0,), (0,)), ((), ())), precision=precision, preferred_element_type=F32
    )


def fold_rows(source):
    total = source[0:8]
    for start in range(8, source.shape[0], 8):
        total = total + source[start : start + 8]
    return total


def row_sum(total):
    return jnp.sum(total, axis=0, keepdims=True)


def norm_rows(source):
    centre = source - jnp.mean(source, axis=-1, keepdims=True)
    inverse = lax.rsqrt(jnp.mean(centre * centre, axis=-1, keepdims=True) + layer_eps)
    return centre * inverse, inverse


def norm_back(grad_norm, normal, inverse, gain):
    scaled = grad_norm * gain
    return inverse * (
        scaled
        - jnp.mean(scaled, axis=-1, keepdims=True)
        - normal * jnp.mean(scaled * normal, axis=-1, keepdims=True)
    )


def normal_cdf(source):
    return 0.5 * (1.0 + lax.erf(source * root_half))


def density(source):
    return jnp.exp(-0.5 * source * source) * inverse_root_tau


def loop(start, stop, body, carry, unroll=1):
    return lax.fori_loop(start, stop, body, carry, unroll=unroll)


def here(row):
    return pl.ds(pl.multiple_of(row * GRID, 8), GRID)


class Rows:
    def __init__(self, extent_ref, width):
        self.extent_ref = extent_ref
        self.column = lax.broadcasted_iota(jnp.int32, (GRID, width), 0)

    def inside(self, row):
        image = row // GRID
        limit = jnp.where(
            row - image * GRID < self.extent_ref[image, 0], self.extent_ref[image, 1], 0
        )
        return self.column < limit

    def after(self, value):
        return jnp.where(self.column == 0, 0.0, pltpu.roll(value, 1, 0))

    def before(self, value):
        return jnp.where(self.column == GRID - 1, 0.0, pltpu.roll(value, GRID - 1, 0))

    def convolve(self, plane, row, tap):
        columns = [None] * 3
        for down, source in enumerate(three_rows(plane, row)):
            for across in range(3):
                term = source * tap(3 * down + across)
                columns[across] = term if down == 0 else columns[across] + term
        return columns[1] + self.after(columns[0]) + self.before(columns[2])


def padded(row):
    return row + 2 * (row // GRID) + 1


def three_rows(plane, row):
    first = padded(row) - 1
    for down in range(3):
        yield plane[here(first + down), :]


def clear_edges(plane, images):
    edge = jnp.zeros((GRID, plane.shape[1]), F32)
    for image in range(images):
        base = image * (GRID + 2) * GRID
        plane[base : base + GRID, :] = edge
        plane[base + (GRID + 1) * GRID : base + (GRID + 2) * GRID, :] = edge


def plane_of(images, width):
    return pltpu.VMEM((images * (GRID + 2) * GRID, width), F32)


VMEM = pl.BlockSpec(memory_space=pltpu.VMEM)
SMEM = pl.BlockSpec(memory_space=pltpu.SMEM)


ANY = pl.BlockSpec(memory_space=pl.ANY)
FAR = pl.BlockSpec(memory_space=pltpu.HBM)
COST_UNIT = 1e9
KERNEL_COST = {
    "front": 15.0, "middle": 27.0, "fed_grads": 2.7, "inner_back": 13.0, "attention_back": 5.5,
    "att_grads": 3.0, "outer_back": 5.0, "sweeps": 9.5, "prepare": 2.5, "renew": 2.5,
}


def call(kernel, name, spaces, outs, scratch, limit, args, flops=0, size=0, later=()):
    del flops, size
    cost = KERNEL_COST.get(name, 1.0)
    inputs, extra = len(args), len(later)

    def body(*refs):
        kernel(*refs[:inputs], *refs[inputs + extra :])

    return pl.pallas_call(
        body,
        in_specs=list(spaces) + [ANY] * extra,
        out_specs=[VMEM] * len(outs),
        out_shape=[jax.ShapeDtypeStruct(shape, dtype) for shape, dtype in outs],
        scratch_shapes=scratch,
        compiler_params=pltpu.CompilerParams(vmem_limit_bytes=limit << 20),
        cost_estimate=pl.CostEstimate(
            flops=int(cost * COST_UNIT), bytes_accessed=1024, transcendentals=0
        ),
        name=name,
    )(*args, *later)


def merge_stats(one, two):
    shift = one[0] / one[2] - two[0] / two[2]
    count = one[2] + two[2]
    spread = one[1] + two[1] + shift * shift * (one[2] * two[2] / count)
    return one[0] + two[0], spread, count


def get_rows(ref):
    return [ref[row : row + 1, :] for row in range(ref.shape[0])]


def put_rows(ref, values):
    for row, value in enumerate(values):
        ref[row : row + 1, :] = value


def merge_kernel(held_ref, other_ref, out_ref):
    put_rows(out_ref, merge_stats(get_rows(held_ref), get_rows(other_ref)))


def merge(held, other, later=()):
    return call(
        merge_kernel, "merge_rows", [VMEM, VMEM], [(held.shape, F32)], [], 1, (held, other), 1e4,
        1e4, later,
    )[0]


def front_kernel(
    images, extent_ref, sharp_ref, x_far, wq_far, wp_far, aff_far,
    norm_ref, query_ref, key_ref, value_ref, inv_ref, cov_ref, attend_ref, mixing_ref,
    branch_ref, mix_ref, conv_ref, act_ref, stat_ref,
    joined, plane, x_ref, wq_ref, wp_ref, aff_ref, arrived,
):
    copies = [
        pltpu.make_async_copy(far, near, arrived.at[index])
        for index, (far, near) in enumerate(
            ((x_far, x_ref), (aff_far, aff_ref), (wq_far, wq_ref), (wp_far, wp_ref))
        )
    ]
    for copy in copies:
        copy.start()
    tokens, width = x_ref.shape
    slots = tokens // images
    heads = sharp_ref.shape[0]
    head = width // heads
    rows = Rows(extent_ref, width)
    clear_edges(plane, images)
    zero = jnp.zeros((8, width), F32)

    def aff(row):
        return aff_ref[row : row + 1, :]

    def first(step, carry):
        place = pl.ds(pl.multiple_of(step * 48, 16), 48)
        value = x_ref[place, :].astype(F32)
        mix_ref[place, :] = value
        normal, _ = norm_rows(value)
        norm_ref[place, :] = (normal * aff(0) + aff(1)).astype(BF16)
        return carry

    copies[0].wait()
    copies[1].wait()
    loop(0, tokens // 48, first, 0, unroll=4)
    copies[2].wait()
    joined[...] = mul_nn(norm_ref[...], wq_ref[...].astype(BF16))

    def second(row, carry):
        query_sum, key_sum = carry
        at = here(row)
        inside = rows.inside(row)
        query = jnp.where(inside, joined[at, :width] + aff(2), 0.0)
        key = jnp.where(inside, joined[at, width : 2 * width] + aff(3), 0.0)
        query_ref[at, :] = query
        key_ref[at, :] = key
        value_ref[at, :] = joined[at, 2 * width :] + aff(4)
        return query_sum + fold_rows(query * query), key_sum + fold_rows(key * key)

    for image in range(images):
        span = slice(image * slots, (image + 1) * slots)
        low, high = image * GRID, (image + 1) * GRID
        query_sum, key_sum = loop(low, high, second, (zero, zero), unroll=2)
        query_inv = lax.rsqrt(row_sum(query_sum) + unit_eps)
        key_inv = lax.rsqrt(row_sum(key_sum) + unit_eps)
        inv_ref[2 * image : 2 * image + 1, :] = query_inv
        inv_ref[2 * image + 1 : 2 * image + 2, :] = key_inv

        def third(row, carry):
            at = here(row)
            query_ref[at, :] = query_ref[at, :] * query_inv
            key_ref[at, :] = key_ref[at, :] * key_inv
            return carry

        loop(low, high, third, 0, unroll=2)
        cov_ref[image] = mul_tn(query_ref[span, :], key_ref[span, :], HIGH)
        lane = lax.broadcasted_iota(jnp.int32, (head, width), 1)
        for group in range(heads):
            part = slice(group * head, (group + 1) * head)
            own = (lane >= group * head) & (lane < (group + 1) * head)
            scores = jnp.where(own, cov_ref[image, part, :] * sharp_ref[group], -jnp.inf)
            raised = jnp.exp(scores - jnp.max(scores, axis=-1, keepdims=True))
            attend_ref[image, part, :] = raised / jnp.sum(raised, axis=-1, keepdims=True)
        mixing_ref[span, :] = mul_nt(value_ref[span, :], attend_ref[image], HIGH).astype(BF16)
    copies[3].wait()
    branch_ref[...] = mul_nn(mixing_ref[...], wp_ref[...].astype(BF16))

    def fourth(row, carry):
        at = here(row)
        inside = rows.inside(row)
        branch = branch_ref[at, :] + aff(5)
        branch_ref[at, :] = branch
        after = mix_ref[at, :] + jnp.where(inside, aff(6) * branch, 0.0)
        mix_ref[at, :] = after
        normal, _ = norm_rows(after)
        plane[here(padded(row)), :] = jnp.where(inside, normal * aff(7) + aff(8), 0.0)
        return carry

    loop(0, images * GRID, fourth, 0, unroll=8)

    def fifth(row, total):
        at = here(row)
        summed = rows.convolve(plane, row, lambda index: aff(9 + index)) + aff(18)
        conv_ref[at, :] = summed
        active = summed * normal_cdf(summed)
        act_ref[at, :] = active
        return total + fold_rows(jnp.where(rows.inside(row), active, 0.0))

    for image in range(images):
        low, high = image * GRID, (image + 1) * GRID
        act_sum = row_sum(loop(low, high, fifth, zero, unroll=2))
        count = (extent_ref[image, 0] * extent_ref[image, 1]).astype(F32)
        centre = act_sum / count

        def sixth(row, total):
            shifted = jnp.where(rows.inside(row), act_ref[here(row), :] - centre, 0.0)
            return total + fold_rows(shifted * shifted)

        spread = row_sum(loop(low, high, sixth, zero, unroll=4))
        own = (act_sum, spread, jnp.full_like(centre, count))
        stats = own if image == 0 else merge_stats(stats, own)
    put_rows(stat_ref, stats)


def front(images, extents, sharpness, source, wq, wp, aff, later):
    tokens, width = source.shape
    full, low, square = ((tokens, width), F32), ((tokens, width), BF16), ((images, width, width), F32)
    far = (extents, sharpness, source, wq, wp, aff)
    outs = [
        low, full, full, full, ((2 * images, width), F32), square, square, low,
        full, full, full, full, ((3, width), F32),
    ]
    return call(
        functools.partial(front_kernel, images), "front",
        [SMEM, SMEM, FAR, FAR, FAR, FAR], outs,
        [
            pltpu.VMEM((tokens, 3 * width), F32), plane_of(images, width),
            pltpu.VMEM(source.shape, source.dtype), pltpu.VMEM(wq.shape, F32),
            pltpu.VMEM(wp.shape, F32), pltpu.VMEM(aff.shape, F32), pltpu.SemaphoreType.DMA((4,)),
        ], 16,
        [pltpu.with_memory_space_constraint(array, pltpu.HBM) for array in far], 2e10, 3e7, later,
    )


def cast_kernel(source_ref, out_ref):
    out_ref[...] = source_ref[...].astype(BF16)


def cast(source, later=()):
    return call(
        cast_kernel, "cast", [VMEM], [(source.shape, BF16)], [], 2, (source,), later=later
    )[0]


def upstream_kernel(image, extent_ref, up_ref, w2_ref, aff_ref, gbranch_ref, dhidden_ref, sum_ref):
    slots, width = gbranch_ref.shape
    rows = Rows(extent_ref, width)
    low, high = image * GRID, (image + 1) * GRID

    def body(pair, total):
        grads = []
        for row in (2 * pair, 2 * pair + 1):
            value = up_ref[here(row), :].astype(F32) * aff_ref[39:40, :]
            grads.append(jnp.where(rows.inside(row), value, 0.0))
        grad = jnp.concatenate(grads, axis=0).astype(BF16)
        gbranch_ref[pl.ds(pl.multiple_of((2 * pair - low) * GRID, 16), 2 * GRID), :] = grad
        return total + fold_rows(grad.astype(F32))

    sum_ref[...] = loop(low // 2, high // 2, body, jnp.zeros((8, width), F32), unroll=2)
    dhidden_ref[...] = mul_nt(gbranch_ref[...], w2_ref[...])


def upstream(images, image, extents, up, w2, aff, later=()):
    tokens, width = up.shape
    slots, inner = tokens // images, w2.shape[0]
    return call(
        functools.partial(upstream_kernel, image), "upstream", [SMEM] + [VMEM] * 3,
        [((slots, width), BF16), ((slots, inner), F32), ((8, width), F32)], [], 2,
        (extents, up, w2, aff), later=later,
    )


def middle_kernel(
    images, extent_ref, stat_ref, stat_two_ref, mix_ref, act_ref, up_ref, w1_ref, w2_ref, aff_ref,
    *refs
):
    dhidden_refs, branch_sum_refs, refs = refs[:images], refs[images : 2 * images], refs[2 * images :]
    (
        out_ref, norm_ref, hidlow_ref, ghid_ref, glocal_ref, gbn_ref, batch_ref, sum_ref, bn_ref,
        hidden, conv_s, normal_s, inverse_s, branch_s, plane, grad_plane,
    ) = refs
    tokens, width = mix_ref.shape
    inner = w1_ref.shape[1]
    rows = Rows(extent_ref, width)
    clear_edges(plane, images)
    clear_edges(grad_plane, images)
    zero = jnp.zeros((8, width), F32)
    all_rows = images * GRID

    def aff(row):
        return aff_ref[row : row + 1, :]

    act_sum, spread, tally = merge_stats(get_rows(stat_ref), get_rows(stat_two_ref))
    centre = act_sum / tally
    inverse_std = lax.rsqrt(spread / tally + batch_eps)
    batch_ref[0:1, :] = centre
    batch_ref[1:2, :] = inverse_std
    batch_ref[2:3, :] = tally

    def first(row, carry):
        inside = rows.inside(row)
        unit = (act_ref[here(row), :] - centre) * inverse_std
        plane[here(padded(row)), :] = jnp.where(inside, unit * aff(19) + aff(20), 0.0)
        return carry

    loop(0, all_rows, first, 0, unroll=2)

    def second(row, carry):
        at = here(row)
        inside = rows.inside(row)
        summed = rows.convolve(plane, row, lambda index: aff(21 + index)) + aff(30)
        conv_s[at, :] = summed
        after = mix_ref[at, :] + jnp.where(inside, aff(31) * summed, 0.0)
        branch_s[at, :] = after
        return carry

    loop(0, all_rows, second, 0, unroll=2)

    def second_norm(step, carry):
        at = pl.ds(pl.multiple_of(step * 48, 16), 48)
        normal, inverse = norm_rows(branch_s[at, :])
        normal_s[at, :] = normal
        inverse_s[at, :] = inverse
        norm_ref[at, :] = (normal * aff(32) + aff(33)).astype(BF16)
        return carry

    loop(0, tokens // 48, second_norm, 0, unroll=4)

    sum_ref[17:18, :] = row_sum(sum(ref[...] for ref in branch_sum_refs))
    slots = tokens // images
    quarters = inner // width
    bias_sums = [zero] * quarters
    for image in range(images):
        span = slice(image * slots, (image + 1) * slots)
        hidden[...] = mul_nn(norm_ref[span, :], w1_ref[...])
        dhidden = dhidden_refs[image]
        for quarter in range(quarters):
            cols = slice(quarter * width, (quarter + 1) * width)
            bias = aff(34 + quarter)

            def fourth(step, total):
                at = pl.ds(pl.multiple_of(step * 16, 16), 16)
                to = pl.ds(pl.multiple_of(image * slots + step * 16, 16), 16)
                value = hidden[at, cols] + bias
                cdf = normal_cdf(value)
                hidlow_ref[to, cols] = (value * cdf).astype(BF16)
                grad = (dhidden[at, cols] * (cdf + value * density(value))).astype(BF16)
                ghid_ref[to, cols] = grad
                return total + fold_rows(grad.astype(F32))

            bias_sums[quarter] = loop(0, slots // 16, fourth, bias_sums[quarter], unroll=2)
        gbn_ref[span, :] = mul_nt(ghid_ref[span, :], w1_ref[...])
        glocal_ref[span, :] = mul_nn(hidlow_ref[span, :], w2_ref[...])
    for quarter in range(quarters):
        sum_ref[13 + quarter : 14 + quarter, :] = row_sum(bias_sums[quarter])

    def fifth(row, total):
        at = here(row)
        inside = rows.inside(row)
        branch = jnp.where(inside, glocal_ref[at, :] + aff(38), 0.0)
        out_ref[at, :] = (branch_s[at, :] + aff(39) * branch).astype(BF16)
        return total + fold_rows(up_ref[at, :].astype(F32) * branch)

    sum_ref[18:19, :] = row_sum(loop(0, all_rows, fifth, zero, unroll=2))

    def sixth(row, carry):
        gain_sum, shift_sum, scale_sum, bias_sum = carry
        at = here(row)
        inside = rows.inside(row)
        grad_norm = gbn_ref[at, :]
        normal = normal_s[at, :]
        grad = up_ref[at, :].astype(F32) + norm_back(grad_norm, normal, inverse_s[at, :], aff(32))
        glocal_ref[at, :] = grad
        kept = jnp.where(inside, grad, 0.0)
        scaled = kept * aff(31)
        grad_plane[here(padded(row)), :] = scaled
        return (
            gain_sum + fold_rows(grad_norm * normal), shift_sum + fold_rows(grad_norm),
            scale_sum + fold_rows(kept * conv_s[at, :]), bias_sum + fold_rows(scaled),
        )

    gain_sum, shift_sum, scale_sum, bias_sum = loop(0, all_rows, sixth, (zero,) * 4, unroll=6)
    sum_ref[11:12, :] = row_sum(gain_sum)
    sum_ref[12:13, :] = row_sum(shift_sum)
    sum_ref[10:11, :] = row_sum(scale_sum)
    sum_ref[9:10, :] = row_sum(bias_sum)

    def seventh(row, carry):
        bias_bn, gain_bn = carry
        at = here(row)
        summed = rows.convolve(grad_plane, row, lambda index: aff(29 - index))
        summed = jnp.where(rows.inside(row), summed, 0.0)
        gbn_ref[at, :] = summed
        unit = (act_ref[at, :] - centre) * inverse_std
        return bias_bn + fold_rows(summed), gain_bn + fold_rows(summed * unit)

    bias_bn, gain_bn = loop(0, all_rows, seventh, (zero, zero), unroll=2)
    bn_ref[0:1, :] = row_sum(bias_bn)
    bn_ref[1:2, :] = row_sum(gain_bn)
    kernel_sums(rows, plane, grad_plane, images, sum_ref, 0)


def kernel_sums(rows, plane, grad_plane, images, sum_ref, base):
    zero = jnp.zeros((8, plane.shape[1]), F32)

    def body(row, carry):
        grad = grad_plane[here(padded(row)), :]
        grads = (rows.before(grad), grad, rows.after(grad))
        totals = list(carry)
        for down, source in enumerate(three_rows(plane, row)):
            for across in range(3):
                index = 3 * down + across
                totals[index] = totals[index] + fold_rows(grads[across] * source)
        return tuple(totals)

    totals = loop(0, images * GRID, body, (zero,) * 9)
    for index, total in enumerate(totals):
        sum_ref[base + index : base + index + 1, :] = row_sum(total)


def middle(
    images, extents, stats, stats_two, after_mix, act, up, w1, w2, aff, dhidden, branch_sums,
    later=(),
):
    tokens, width = after_mix.shape
    inner = w1.shape[1]
    full, low, wide = ((tokens, width), F32), ((tokens, width), BF16), ((tokens, inner), BF16)
    outs = [
        low, low, wide, wide, full, full, ((3, width), F32), ((19, width), F32), ((2, width), F32),
    ]
    return call(
        functools.partial(middle_kernel, images), "middle",
        [SMEM] + [VMEM] * (8 + 2 * images), outs,
        [
            pltpu.VMEM((tokens // images, inner), F32),
            pltpu.VMEM((tokens, width), F32), pltpu.VMEM((tokens, width), F32),
            pltpu.VMEM((tokens, 1), F32), pltpu.VMEM((tokens, width), F32),
            plane_of(images, width), plane_of(images, width),
        ], 18,
        (extents, stats, stats_two, after_mix, act, up, w1, w2, aff, *dhidden, *branch_sums), 3e10,
        4e7, later,
    )


def fed_grads_kernel(shift, bit_ref, norm_ref, hidlow_ref, ghid_ref, *refs):
    *gbranch_refs, out_ref = refs
    slots = gbranch_refs[0].shape[0]
    width = norm_ref.shape[1]
    pairs = out_ref.shape[0]
    size = ghid_ref.shape[1] // (2 * pairs)
    low = bit_ref[0] if shift == 0 else 1 - bit_ref[0]
    for pair in range(pairs):
        cols = pl.ds(pl.multiple_of((2 * pair + low) * size, 128), size)
        out_ref[pair, 0:size, :] = mul_tn(ghid_ref[:, cols], norm_ref[...])
        total = None
        for image, gbranch_ref in enumerate(gbranch_refs):
            span = slice(image * slots, (image + 1) * slots)
            part = mul_tn(hidlow_ref[span, cols], gbranch_ref[...])
            total = part if image == 0 else total + part
        out_ref[pair, size : 2 * size, :] = total


def fed_grads(shift, parts, bit, norm, hidlow, ghid, gbranch, later=()):
    width, inner = norm.shape[1], ghid.shape[1]
    return call(
        functools.partial(fed_grads_kernel, shift), "fed_grads",
        [SMEM] + [VMEM] * (3 + len(gbranch)),
        [((parts // 2, 2 * inner // parts, width), F32)], [], 6,
        (bit, norm, hidlow, ghid, *gbranch), 3e9, 1e7, later,
    )[0]


def inner_back_kernel(
    images, extent_ref, total_ref, total_two_ref, batch_ref, act_ref, conv_ref, gbn_ref, glocal_ref, mix_ref,
    branch_ref, aff_ref, gmix_ref, gbranch_ref, sum_ref, bn_ref,
    normal_s, inverse_s, plane, grad_plane,
):
    tokens, width = act_ref.shape
    rows = Rows(extent_ref, width)
    clear_edges(plane, images)
    clear_edges(grad_plane, images)
    zero = jnp.zeros((8, width), F32)
    all_rows = images * GRID

    def aff(row):
        return aff_ref[row : row + 1, :]

    totals = total_ref[...] + total_two_ref[...]
    bn_ref[...] = totals
    centre, inverse_std, tally = batch_ref[0:1, :], batch_ref[1:2, :], batch_ref[2:3, :]
    bias_mean, gain_mean = totals[0:1, :] / tally, totals[1:2, :] / tally
    factor = aff(19) * inverse_std

    def first(row, total):
        at = here(row)
        unit = (act_ref[at, :] - centre) * inverse_std
        value = conv_ref[at, :]
        slope = normal_cdf(value) + value * density(value)
        grad = factor * (gbn_ref[at, :] - (bias_mean + unit * gain_mean)) * slope
        grad = jnp.where(rows.inside(row), grad, 0.0)
        grad_plane[here(padded(row)), :] = grad
        return total + fold_rows(grad)

    sum_ref[13:14, :] = row_sum(loop(0, all_rows, first, zero, unroll=2))

    def second(row, carry):
        at = here(row)
        normal, inverse = norm_rows(mix_ref[at, :])
        normal_s[at, :] = normal
        inverse_s[at, :] = inverse
        plane[here(padded(row)), :] = jnp.where(rows.inside(row), normal * aff(7) + aff(8), 0.0)
        return carry

    loop(0, all_rows, second, 0, unroll=8)
    kernel_sums(rows, plane, grad_plane, images, sum_ref, 4)

    def third(row, carry):
        summed = rows.convolve(grad_plane, row, lambda index: aff(17 - index))
        gmix_ref[here(row), :] = jnp.where(rows.inside(row), summed, 0.0)
        return carry

    loop(0, all_rows, third, 0, unroll=2)

    def fourth(row, carry):
        gain_sum, shift_sum, scale_sum, bias_sum = carry
        at = here(row)
        grad_norm, normal = gmix_ref[at, :], normal_s[at, :]
        grad = glocal_ref[at, :] + norm_back(grad_norm, normal, inverse_s[at, :], aff(7))
        gmix_ref[at, :] = grad
        kept = jnp.where(rows.inside(row), grad, 0.0)
        low = (kept * aff(6)).astype(BF16)
        gbranch_ref[at, :] = low
        return (
            gain_sum + fold_rows(grad_norm * normal), shift_sum + fold_rows(grad_norm),
            scale_sum + fold_rows(kept * branch_ref[at, :]), bias_sum + fold_rows(low.astype(F32)),
        )

    gain_sum, shift_sum, scale_sum, bias_sum = loop(0, all_rows, fourth, (zero,) * 4, unroll=6)
    sum_ref[0:1, :] = row_sum(bias_sum)
    sum_ref[1:2, :] = row_sum(scale_sum)
    sum_ref[2:3, :] = row_sum(gain_sum)
    sum_ref[3:4, :] = row_sum(shift_sum)


def inner_back(
    images, extents, totals, totals_two, batch, act, conv, gbn, glocal, after_mix, branch, aff,
    later=(),
):
    tokens, width = act.shape
    outs = [((tokens, width), F32), ((tokens, width), BF16), ((14, width), F32), ((2, width), F32)]
    return call(
        functools.partial(inner_back_kernel, images), "inner_back",
        [SMEM] + [VMEM] * 10, outs,
        [
            pltpu.VMEM((tokens, width), F32), pltpu.VMEM((tokens, 1), F32),
            plane_of(images, width), plane_of(images, width),
        ], 10,
        (extents, totals, totals_two, batch, act, conv, gbn, glocal, after_mix, branch, aff), 2e10, 3e7,
        later,
    )


def attention_back_kernel(
    image, extent_ref, sharp_ref, query_ref, key_ref, value_ref, inv_ref, cov_ref, attend_ref,
    gbranch_ref, wp_ref, gjoined, head_ref,
    gmixing, gscore, gquery, gkey,
):
    slots, width = gmixing.shape
    heads = sharp_ref.shape[0]
    head = width // heads
    rows = Rows(extent_ref, width)
    zero = jnp.zeros((8, width), F32)
    span = slice(image * slots, (image + 1) * slots)
    low, high = image * GRID, (image + 1) * GRID
    gmixing[...] = mul_nt(gbranch_ref[span, :], wp_ref[...])
    lane = lax.broadcasted_iota(jnp.int32, (1, width), 1)
    sharp_sum = jnp.zeros((1, width), F32)
    gscore[...] = mul_tn(gmixing[...], value_ref[span, :], HIGH)
    for group in range(heads):
        part = slice(group * head, (group + 1) * head)
        attend = attend_ref[image, part, :]
        grad = gscore[part, :]
        grad = attend * (grad - jnp.sum(attend * grad, axis=-1, keepdims=True))
        gscore[part, :] = grad * sharp_ref[group]
        amount = jnp.sum(
            jnp.sum(grad * cov_ref[image, part, :], axis=0, keepdims=True), axis=1, keepdims=True
        )
        sharp_sum = sharp_sum + jnp.where(lane == group, amount, 0.0)
    gquery[...] = mul_nt(key_ref[span, :], gscore[...], HIGH)
    gkey[...] = mul_nn(query_ref[span, :], gscore[...], HIGH)
    gmixing[...] = mul_nn(gmixing[...], attend_ref[image], HIGH)

    def first(row, carry):
        query_dot, key_dot = carry
        at = here(row)
        to = here(row - low)
        return (
            query_dot + fold_rows(gquery[to, :] * query_ref[at, :]),
            key_dot + fold_rows(gkey[to, :] * key_ref[at, :]),
        )

    query_dot, key_dot = loop(low, high, first, (zero, zero), unroll=2)
    query_dot, key_dot = row_sum(query_dot), row_sum(key_dot)
    query_inv = inv_ref[2 * image : 2 * image + 1, :]
    key_inv = inv_ref[2 * image + 1 : 2 * image + 2, :]

    def second(pair, carry):
        totals = list(carry)
        thirds = ([], [], [])
        for row in (2 * pair, 2 * pair + 1):
            at = here(row)
            to = here(row - low)
            inside = rows.inside(row)
            grad = query_inv * (gquery[to, :] - query_ref[at, :] * query_dot)
            thirds[0].append(jnp.where(inside, grad, 0.0))
            grad = key_inv * (gkey[to, :] - key_ref[at, :] * key_dot)
            thirds[1].append(jnp.where(inside, grad, 0.0))
            thirds[2].append(gmixing[to, :])
        to = pl.ds(pl.multiple_of((2 * pair - low) * GRID, 16), 2 * GRID)
        for third in range(3):
            value = jnp.concatenate(thirds[third], axis=0).astype(BF16)
            gjoined[to, third * width : (third + 1) * width] = value
            totals[third] = totals[third] + fold_rows(value.astype(F32))
        return tuple(totals)

    bias = loop(low // 2, high // 2, second, (zero,) * 3)
    put_rows(head_ref, [row_sum(total) for total in bias] + [sharp_sum])


def attention_back(
    images, image, extents, sharpness, query, key, value, inv, cov, attend, gbranch, wp, later=(),
):
    tokens, width = query.shape
    slots = tokens // images
    return call(
        functools.partial(attention_back_kernel, image), "attention_back",
        [SMEM] * 2 + [VMEM] * 8, [((slots, 3 * width), BF16), ((4, width), F32)],
        [
            pltpu.VMEM((slots, width), F32), pltpu.VMEM((width, width), F32),
            pltpu.VMEM((slots, width), F32), pltpu.VMEM((slots, width), F32),
        ], 8,
        (extents, sharpness, query, key, value, inv, cov, attend, gbranch, wp), 2e10, 2e7, later,
    )


def att_grads_kernel(
    bits_ref, norm_ref, mixing_ref, gbranch_ref, *refs
):
    *gjoined_refs, send_ref, keep_ref, matrix = refs
    slots = gjoined_refs[0].shape[0]
    width = norm_ref.shape[1]
    pairs = send_ref.shape[0]
    for image, gjoined_ref in enumerate(gjoined_refs):
        part = mul_tn(gjoined_ref[...], norm_ref[image * slots : (image + 1) * slots, :])
        rows = slice(0, 3 * width)
        matrix[rows, :] = part if image == 0 else matrix[rows, :] + part
    matrix[3 * width :, :] = mul_tn(mixing_ref[...], gbranch_ref[...])
    joined_rows, mixer_rows = 3 * width // (2 * pairs), width // (2 * pairs)
    for pair in range(pairs):
        for target, place in ((keep_ref, bits_ref[0]), (send_ref, 1 - bits_ref[0])):
            part = 2 * pair + place
            at = pl.ds(pl.multiple_of(part * joined_rows, 8), joined_rows)
            target[pair, 0:joined_rows, :] = matrix[at, :]
            at = pl.ds(pl.multiple_of(3 * width + part * mixer_rows, 8), mixer_rows)
            target[pair, joined_rows:, :] = matrix[at, :]


def att_grads(parts, bits, norm, mixing, gbranch, gjoined, later=()):
    width = norm.shape[1]
    share = ((parts // 2, 4 * width // parts, width), F32)
    return call(
        att_grads_kernel, "att_grads", [SMEM] + [VMEM] * (3 + len(gjoined)), [share, share],
        [pltpu.VMEM((4 * width, width), F32)], 8,
        (bits, norm, mixing, gbranch, *gjoined), 2e9, 8e6, later,
    )


def outer_back_kernel(
    x_ref, gmix_ref, wq_ref, aff_ref, inner_ref, tail_ref, *refs
):
    *refs, incoming_ref, vector_ref, gnorm = refs
    images = len(refs) // 2
    gjoined_refs, head_refs = refs[:images], refs[images:]
    slots = gjoined_refs[0].shape[0]
    tokens, width = x_ref.shape
    zero = jnp.zeros((8, width), F32)
    for image, gjoined_ref in enumerate(gjoined_refs):
        gnorm[image * slots : (image + 1) * slots, :] = mul_nt(gjoined_ref[...], wq_ref[...])

    def body(step, carry):
        gain_sum, shift_sum = carry
        at = pl.ds(pl.multiple_of(step * 48, 16), 48)
        normal, inverse = norm_rows(x_ref[at, :].astype(F32))
        grad = gnorm[at, :]
        incoming_ref[at, :] = gmix_ref[at, :] + norm_back(grad, normal, inverse, aff_ref[0:1, :])
        return gain_sum + fold_rows(grad * normal), shift_sum + fold_rows(grad)

    gain_sum, shift_sum = loop(0, tokens // 48, body, (zero, zero), unroll=4)
    vector_ref[...] = jnp.zeros_like(vector_ref)
    vector_ref[0:1, :] = row_sum(gain_sum)
    vector_ref[1:2, :] = row_sum(shift_sum)
    head = sum(ref[...] for ref in head_refs[1:]) + head_refs[0][...]
    vector_ref[2:5, :] = head[0:3, :]
    vector_ref[5:19, :] = inner_ref[...]
    vector_ref[21:40, :] = tail_ref[...]
    vector_ref[40:41, :] = head[3:4, :]


def outer_back(source, gmix, wq, aff, inner, tail, gjoined, head, later=()):
    tokens, width = source.shape
    return call(
        outer_back_kernel, "outer_back", [VMEM] * (6 + 2 * len(head)),
        [((tokens, width), F32), ((SUM_ROWS, width), F32)], [pltpu.VMEM((tokens, width), F32)], 6,
        (source, gmix, wq, aff, inner, tail, *gjoined, *head), 5e9, 1e7, later,
    )


def row_blocks(rows):
    step = next(size for size in (32, 24, 16, 8, rows) if rows % size == 0)
    return rows // step, step


def blocks(rows, body):
    count, step = row_blocks(rows)

    def inner(index, carry):
        start = index * step
        body(pl.multiple_of(start, 8) if step % 8 == 0 else start, step)
        return carry

    loop(0, count, inner, 0)


def halve_first_kernel(
    high, side, bits_ref, held_ref, other_ref, send_high_ref, keep_high_ref, send_side_ref,
    keep_side_ref,
):
    half, quarter = send_high_ref.shape[0], send_side_ref.shape[1]
    high_bit, side_bit = bits_ref[high], bits_ref[side]

    def first(start, size):
        at = pl.ds(start, size)
        send_high_ref[at, :] = held_ref[1 - high_bit, at, :] + other_ref[1 - high_bit, at, :]
        keep_high_ref[at, :] = held_ref[high_bit, at, :] + other_ref[high_bit, at, :]

    def second(start, size):
        at = pl.ds(start, size)
        for target, bit in ((send_side_ref, 1 - side_bit), (keep_side_ref, side_bit)):
            here = pl.ds(pl.multiple_of(half + bit * quarter, 8) + start, size)
            for part in range(2):
                target[part, at, :] = held_ref[part, here, :] + other_ref[part, here, :]

    blocks(half, first)
    blocks(quarter, second)


def halve_first(bits, high, side, held, other, later=()):
    rows, width = held.shape[-2:]
    half, quarter = ((rows // 2, width), F32), ((2, rows // 4, width), F32)
    return call(
        functools.partial(halve_first_kernel, high, side), "halve_first", [SMEM, VMEM, VMEM],
        [half, half, quarter, quarter], [], 2, (bits, held, other), held.size, 16 * held.size,
        later,
    )


def halve_second_kernel(
    high, side, bits_ref, one_ref, one_other_ref, two_ref, two_other_ref,
    send_one_ref, keep_one_ref, send_two_ref, keep_two_ref,
):
    quarter = send_one_ref.shape[0]
    high_bit, side_bit = bits_ref[high], bits_ref[side]

    def body(start, size):
        at = pl.ds(start, size)
        for target, bit in ((send_one_ref, 1 - side_bit), (keep_one_ref, side_bit)):
            here = pl.ds(pl.multiple_of(bit * quarter, 8) + start, size)
            target[at, :] = one_ref[here, :] + one_other_ref[here, :]
        for target, bit in ((send_two_ref, 1 - high_bit), (keep_two_ref, high_bit)):
            target[at, :] = two_ref[bit, at, :] + two_other_ref[bit, at, :]

    blocks(quarter, body)


def halve_second(bits, high, side, one, one_other, two, two_other, later=()):
    quarter = (two.shape[-2:], F32)
    return call(
        functools.partial(halve_second_kernel, high, side), "halve_second",
        [SMEM] + [VMEM] * 4, [quarter] * 4, [], 2,
        (bits, one, one_other, two, two_other), one.size, 32 * one.size, later,
    )


def halve_third_kernel(
    place, bits_ref, one_ref, one_other_ref, two_ref, two_other_ref, send_ref, keep_ref
):
    bit = bits_ref[place]
    eighth = one_ref.shape[0] // 2

    def body(start, size):
        for target, half in ((send_ref, 1 - bit), (keep_ref, bit)):
            here = pl.ds(pl.multiple_of(half * eighth, 8) + start, size)
            target[pl.ds(start, size), :] = one_ref[here, :] + one_other_ref[here, :]
            target[pl.ds(eighth + start, size), :] = two_ref[here, :] + two_other_ref[here, :]

    blocks(eighth, body)


def halve_third(bits, place, one, one_other, two, two_other, later=()):
    return call(
        functools.partial(halve_third_kernel, place), "halve_third", [SMEM] + [VMEM] * 4,
        [(one.shape, F32)] * 2, [], 2, (bits, one, one_other, two, two_other), one.size,
        32 * one.size, later,
    )


def split_add_kernel(place, bits_ref, held_ref, other_ref, send_ref, keep_ref):
    bit = bits_ref[place]

    def body(start, size):
        at = pl.ds(start, size)
        send_ref[at, :] = held_ref[1 - bit, at, :] + other_ref[1 - bit, at, :]
        keep_ref[at, :] = held_ref[bit, at, :] + other_ref[bit, at, :]

    blocks(send_ref.shape[0], body)


def split_add(bits, place, held, other, later=()):
    half = (held.shape[-2:], F32)
    return call(
        functools.partial(split_add_kernel, place), "split_add", [SMEM, VMEM, VMEM], [half, half],
        [], 2, (bits, held, other), held.size, 16 * held.size, later,
    )


def add_kernel(held_ref, other_ref, out_ref):
    def body(start, size):
        at = pl.ds(start, size)
        out_ref[at, :] = held_ref[at, :] + other_ref[at, :]

    blocks(held_ref.shape[0], body)


def add(held, other, later=()):
    return call(
        add_kernel, "add_rows", [VMEM, VMEM], [(held.shape, F32)], [], 2, (held, other),
        held.size, 12 * held.size, later,
    )[0]


def append_kernel(held_ref, other_ref, rider_ref, rider_other_ref, out_ref):
    rows = held_ref.shape[0]

    def body(start, size):
        at = pl.ds(start, size)
        out_ref[at, :] = held_ref[at, :] + other_ref[at, :]

    blocks(rows, body)
    out_ref[rows:, :] = rider_ref[...] + rider_other_ref[...]


def append(held, other, rider, rider_other, later=()):
    rows, width = held.shape
    return call(
        append_kernel, "append_rows", [VMEM] * 4, [((rows + rider.shape[0], width), F32)], [], 2,
        (held, other, rider, rider_other), held.size, 12 * held.size, later,
    )[0]


def join_kernel(place, rider, bits_ref, held_ref, other_ref, out_ref):
    bit = bits_ref[place]
    rows = held_ref.shape[0] - rider

    def body(start, size):
        mine = pl.ds(pl.multiple_of(bit * rows, 8) + start, size)
        others = pl.ds(pl.multiple_of((1 - bit) * rows, 8) + start, size)
        out_ref[mine, :] = held_ref[pl.ds(start, size), :]
        out_ref[others, :] = other_ref[pl.ds(start, size), :]

    blocks(rows, body)
    if rider:
        out_ref[2 * rows :, :] = held_ref[rows:, :] + other_ref[rows:, :]


def join(bits, place, rider, held, other, later=()):
    rows, width = held.shape
    return call(
        functools.partial(join_kernel, place, rider), "join_rows", [SMEM, VMEM, VMEM],
        [((2 * rows - rider, width), F32)], [], 2, (bits, held, other), held.size,
        16 * held.size, later,
    )[0]


def join_last_kernel(place, rider, bits_ref, held_ref, other_ref, out_ref, rider_ref):
    bit = bits_ref[place]
    rows = (held_ref.shape[0] - rider) // 4

    def body(start, size):
        for half in range(2):
            for following in range(2):
                source = pl.ds((2 * following + half) * rows + start, size)
                for side, ref in ((bit, held_ref), (1 - bit, other_ref)):
                    first = pl.multiple_of((4 * half + 2 * side + following) * rows, 8)
                    out_ref[pl.ds(first + start, size), :] = ref[source, :]

    blocks(rows, body)
    if rider:
        rider_ref[...] = held_ref[4 * rows :, :] + other_ref[4 * rows :, :]
    else:
        rider_ref[...] = jnp.zeros_like(rider_ref)


def join_last(bits, place, rider, held, other, later=()):
    rows, width = held.shape
    return call(
        functools.partial(join_last_kernel, place, rider), "join_last", [SMEM, VMEM, VMEM],
        [((2 * (rows - rider), width), F32), ((max(rider, 8), width), F32)], [], 2,
        (bits, held, other), held.size, 16 * held.size, later,
    )


def upper_blocks(size):
    count = size // 128
    return [(row, column) for row in range(count) for column in range(row, count)]


def block(index):
    return slice(128 * index, 128 * index + 128)


def pack_kernel(held_ref, other_ref, rider_ref, out_ref, rider_out_ref):
    size = held_ref.shape[0]
    pieces = upper_blocks(size)
    for index, (row, column) in enumerate(pieces):
        part = block(row), block(column)
        out_ref[block(index), :] = held_ref[part] + other_ref[part]
    rider = other_ref.shape[0] - size
    if rider:
        total = rider_ref[...] + other_ref[size:, :]
        rider_out_ref[...] = total
        for column in range(size // 128):
            first = 128 * len(pieces) + column * rider
            out_ref[first : first + rider, :] = total[:, block(column)]
    else:
        rider_out_ref[...] = jnp.zeros_like(rider_out_ref)


def pack(held, other, rider, later=()):
    size = held.shape[0]
    extra = other.shape[0] - size
    rows = 128 * len(upper_blocks(size)) + extra * (size // 128)
    return call(
        pack_kernel, "pack_rows", [VMEM] * 3, [((rows, 128), F32), (rider.shape, F32)], [], 2,
        (held, other, rider), held.size, 12 * held.size, later,
    )


def halves(source):
    high = source.astype(BF16)
    return high, (source - high.astype(F32)).astype(BF16)


def put_left(left, source):
    high, low = halves(source)
    size = source.shape[1]
    left[:, 0:size], left[:, size : 2 * size], left[:, 2 * size :] = high, high, low


def put_right(right, columns, source):
    high, low = halves(source)
    size = source.shape[0]
    right[0:size, columns], right[size : 2 * size, columns] = high, low
    right[2 * size :, columns] = high


def sweeps_kernel(mine_ref, other_ref, out_ref, now, total, left, right, step):
    size = out_ref.shape[0]
    for index, (row, column) in enumerate(upper_blocks(size)):
        part = mine_ref[block(index), :] + other_ref[block(index), :]
        now[block(row), block(column)] = part
        if row != column:
            now[block(column), block(row)] = part.T
    row = lax.broadcasted_iota(jnp.int32, (size, size), 0)
    diagonal = row == lax.broadcasted_iota(jnp.int32, (size, size), 1)
    trace = jnp.where(diagonal, now[...], 0.0)
    trace = jnp.sum(jnp.sum(trace, axis=0, keepdims=True), axis=1, keepdims=True)
    norm = jnp.sqrt(trace) + frob_eps
    now[...] = now[...] / (norm * norm)
    near, far = slice(0, size), slice(size, 2 * size)
    for sweep_index in range(NS_STEPS):
        last = sweep_index == NS_STEPS - 1
        put_left(left, now[...])
        put_right(right, near, now[...])
        square = mul_nn(left[...], right[:, near])
        step[...] = (
            jnp.where(diagonal, coef_first, 0.0) + coef_second * now[...] + coef_third * square
        )
        put_left(left, step[...])
        if sweep_index == 0:
            total[...] = step[...] / norm
            now[...] = mul_nn(left[...], right[:, near])
        elif last:
            put_right(right, near, total[...])
            out_ref[...] = mul_nn(left[...], right[:, near])
        else:
            put_right(right, far, total[...])
            both = mul_nn(left[...], right[...])
            now[...] = both[:, near]
            total[...] = both[:, far]
        if not last:
            put_right(right, near, now[...])
            now[...] = mul_nn(left[...], right[:, near])


def sweeps(width, mine, other, later=()):
    square = pltpu.VMEM((width, width), F32)
    return call(
        sweeps_kernel, "sweeps", [VMEM, VMEM], [((width, width), F32)],
        [
            square, square, pltpu.VMEM((width, 3 * width), BF16),
            pltpu.VMEM((3 * width, 2 * width), BF16), square,
        ], 9, (mine, other), 1e10, 4e6, later,
    )[0]


def prepare_kernel(
    turned, rider, bit_ref, share_ref, first_ref, second_ref, rider_ref,
    grad_one_ref, grad_two_ref, state_one_ref, state_two_ref, send_ref, keep_ref,
):
    split = first_ref.shape[0 if turned else 1]
    tall = second_ref.shape[0]
    grad_one = share_ref[0:split, :]
    grad_one_ref[...] = grad_one if turned else grad_one.T
    state_one_ref[...] = velocity_damping * first_ref[...] + grad_one_ref[...]
    grad_two_ref[...] = share_ref[split : split + tall, :]
    state_two_ref[...] = velocity_damping * second_ref[...] + grad_two_ref[...]
    gram = mul_tn if turned else mul_nt
    gram_one = gram(state_one_ref[...], state_one_ref[...], HIGH)
    gram_two = mul_tn(state_two_ref[...], state_two_ref[...], HIGH)
    even = bit_ref[0] == 0
    keep_ref[...] = jnp.where(even, gram_one, gram_two)
    width = share_ref.shape[1]
    send_ref[0:width, :] = jnp.where(even, gram_two, gram_one)
    if rider:
        send_ref[width:, :] = rider_ref[...]


def prepare(turned, rider, bit, share, first, second, rows, later=()):
    width = share.shape[1]
    square, send = ((width, width), F32), ((width + rider, width), F32)
    one, two = (first.shape, F32), (second.shape, F32)
    return call(
        functools.partial(prepare_kernel, turned, rider), "prepare", [SMEM] + [VMEM] * 4,
        [one, two, one, two, send, square], [], 8, (bit, share, first, second, rows), 2e9, 6e6, later,
    )


def renew_kernel(
    turned, factors, bit_ref, mine_ref, other_ref, state_one_ref, state_two_ref, one_ref, two_ref,
    new_one_ref, new_two_ref, low_one_ref, low_two_ref,
):
    even = bit_ref[0] == 0
    poly_one = jnp.where(even, mine_ref[...], other_ref[...])
    poly_two = jnp.where(even, other_ref[...], mine_ref[...])
    if turned:
        field_one = mul_nn(state_one_ref[...], poly_one, HIGH)
    else:
        field_one = mul_nn(poly_one, state_one_ref[...], HIGH)
    new_one = one_ref[...] - (rate_matrix * factors[0]) * field_one
    new_one_ref[...] = new_one
    low_one_ref[...] = new_one.astype(BF16)
    new_two = two_ref[...] - (rate_matrix * factors[1]) * mul_nn(
        state_two_ref[...], poly_two, HIGH
    )
    new_two_ref[...] = new_two
    low_two_ref[...] = new_two.astype(BF16)


def renew(
    turned, factors, bit, mine, other, state_one, state_two, one, two, later=(),
):
    outs = [(one.shape, F32), (two.shape, F32), (one.shape, BF16), (two.shape, BF16)]
    return call(
        functools.partial(renew_kernel, turned, factors), "renew", [SMEM] + [VMEM] * 6, outs, [],
        8, (bit, mine, other, state_one, state_two, one, two), 2e9, 6e6, later,
    )


def vectors_kernel(
    start, rider_ref, other_ref, bn_ref, batch_ref, aff_ref, aff_velocity_ref, sharp_ref,
    sharp_velocity_ref, full_ref, sharp_sum_ref, new_aff_ref, aff_state_ref, new_sharp_ref,
    sharp_state_ref,
):
    rows, width = aff_ref.shape
    rider = rider_ref.shape[0]
    group = sharp_ref.shape[1]
    for column in range(width // 128):
        first = start + column * rider
        total = rider_ref[:, block(column)] + other_ref[first : first + rider, :]
        full_ref[:, block(column)] = total[0:rows, :]
        if column == 0:
            sharp_sum_ref[...] = total[rows : rows + 1, 0:group]
    full_ref[rows // 2 - 1 : rows // 2, :] = bn_ref[1:2, :]
    full_ref[rows // 2 : rows // 2 + 1, :] = bn_ref[0:1, :]
    step_size = affine_step_size * lax.rsqrt(batch_ref[2:3, :])
    state = velocity_damping * aff_velocity_ref[...] + full_ref[...]
    aff_state_ref[...] = state
    new_aff_ref[...] = aff_ref[...] - step_size * state
    state = velocity_damping * sharp_velocity_ref[...] + sharp_sum_ref[...]
    sharp_state_ref[...] = state
    new_sharp_ref[...] = sharp_ref[...] - step_size[:, 0:group] * state


def vectors(
    width, rider, other, bn_totals, batch, aff, aff_velocity, sharp, sharp_velocity, later=(),
):
    start = 128 * len(upper_blocks(width))
    sharp, sharp_velocity = sharp[None], sharp_velocity[None]
    large, small = (aff.shape, F32), (sharp.shape, F32)
    return call(
        functools.partial(vectors_kernel, start), "vectors", [VMEM] * 8,
        [large, small, large, large, small, small], [], 2,
        (rider, other, bn_totals, batch, aff, aff_velocity, sharp, sharp_velocity), 0, 0, later,
    )


def bits_of(size):
    return [1 << place for place in range(size.bit_length() - 1)]


def swap(source, axis, bit):
    size = lax.axis_size(axis)
    return lax.ppermute(source, axis, [(member, member ^ bit) for member in range(size)])


def axis_steps(axis):
    base = 0 if axis == "narrow" else len(bits_of(lax.axis_size("narrow")))
    return [(axis, bit, base + place) for place, bit in enumerate(bits_of(lax.axis_size(axis)))]


def all_steps():
    return axis_steps("narrow") + axis_steps("wide")


def own_bits():
    steps = all_steps()
    places = jnp.stack([lax.axis_index(axis) for axis, _, _ in steps]).astype(jnp.int32)
    return (places & jnp.array([bit for _, bit, _ in steps], jnp.int32)).clip(0, 1)


class Line:
    def __init__(self):
        self.last = ()

    def __call__(self, kernel, *args):
        out = kernel(*args, later=self.last)
        self.last = (out[-1] if isinstance(out, (list, tuple)) else out,)
        return out


def everyone(line, rows, combine, fillers=()):
    fillers = list(fillers)
    steps = all_steps()
    for axis, bit, _ in steps[:-1]:
        other = swap(rows, axis, bit)
        if axis != "narrow" or bit > 1:
            if fillers:
                fillers.pop(0)()
        rows = line(combine, rows, other)
    axis, bit, _ = steps[-1]
    other = swap(rows, axis, bit)
    for filler in fillers:
        filler()
    return rows, other


class Sum:
    def __init__(self, line, bits, send, keep):
        self.line, self.bits, self.keep = line, bits, keep
        (_, self.low, _), (_, self.high, self.high_place) = axis_steps("narrow")
        _, self.side, self.side_place = axis_steps("wide")[0]
        self.rest = axis_steps("wide")[1:]
        self.other = swap(send, "narrow", self.low)
        self.rider = 0

    def first(self):
        send, self.one, send_two, self.two = self.line(
            halve_first, self.bits, self.high_place, self.side_place, self.keep, self.other
        )
        self.one_other = swap(send, "narrow", self.high)
        self.two_other = swap(send_two, "wide", self.side)

    def second(self):
        send, self.one, send_two, self.two = self.line(
            halve_second, self.bits, self.high_place, self.side_place, self.one, self.one_other,
            self.two, self.two_other,
        )
        self.one_other = swap(send, "wide", self.side)
        self.two_other = swap(send_two, "narrow", self.high)

    def third(self):
        axis, bit, place = self.rest[0]
        send, self.keep = self.line(
            halve_third, self.bits, place, self.one, self.one_other, self.two, self.two_other
        )
        self.other = swap(send, axis, bit)
        self.done = 1

    def more(self):
        axis, bit, place = self.rest[self.done]
        shape = self.keep.shape
        self.done += 1
        if self.done < len(self.rest):
            keep, other = (array.reshape(2, -1, shape[1]) for array in (self.keep, self.other))
            send, self.keep = self.line(split_add, self.bits, place, keep, other)
            self.other = swap(send, axis, bit)
        else:
            self.keep = self.line(add, self.keep, self.other)
            self.other = swap(self.keep, axis, bit)

    def mores(self):
        while self.done < len(self.rest):
            self.more()

    def last_step(self):
        axis, bit, _ = self.rest[-1]
        return axis, bit

    def turn(self, rider=None):
        if rider is None:
            self.held = self.line(add, self.keep, self.other)
        else:
            self.held = self.line(append, self.keep, self.other, *rider)
            self.rider = rider[0].shape[0]
        self.place = len(self.rest) - 1
        self.back_move()

    def back_move(self):
        self.place -= 1
        axis, bit, _ = self.rest[self.place] if self.place >= 0 else axis_steps("wide")[0]
        self.other = swap(self.held, axis, bit)

    def back(self):
        _, _, place = self.rest[self.place]
        self.held = self.line(join, self.bits, place, self.rider, self.held, self.other)
        self.back_move()

    def backs(self):
        while self.place >= 0:
            self.back()

    def last(self):
        return self.line(
            join_last, self.bits, self.side_place, self.rider, self.held, self.other
        )


class Update:
    def __init__(self, line, turned, bits, gathered, states, rider=0):
        share, self.rows = gathered
        self.line, self.turned, self.bits = line, turned, bits
        self.width = share.shape[1]
        *self.grads, self.one, self.two, send, self.keep = line(
            prepare, turned, rider, bits, share, *states, self.rows
        )
        self.other = swap(send, "narrow", 1)

    def across(self):
        (axis, bit, _) = axis_steps("narrow")[1]
        self.keep, self.rows = self.line(pack, self.keep, self.other, self.rows)
        self.other = swap(self.keep, axis, bit)
        self.rows_other = self.other

    def sweep(self):
        self.keep = self.line(sweeps, self.width, self.keep, self.other)
        self.other = swap(self.keep, "narrow", 1)

    def renew(self, factors, masters):
        new = self.line(
            renew, self.turned, factors, self.bits, self.keep, self.other, self.one, self.two,
            *masters,
        )
        return self.grads + [self.one, self.two] + list(new)


def on_device(
    block_source,
    upstream_adjoint,
    picture_patch_extents,
    triple_matrix,
    mixer_matrix,
    expand_matrix,
    shrink_matrix,
    affine_entries,
    sharpness,
    triple_velocity,
    mixer_velocity,
    expand_velocity,
    shrink_velocity,
    affine_velocity,
    sharpness_velocity,
):
    images, slot_count, model_width = block_source.shape
    group_index = sharpness.shape[0]
    narrow_parts = lax.axis_size("narrow")
    narrow_pos = lax.axis_index("narrow")
    bits = own_bits()
    source = block_source.reshape(-1, model_width)
    above = upstream_adjoint.reshape(-1, model_width)

    def own_part(full_matrix, along):
        part_size = full_matrix.shape[along] // narrow_parts
        return lax.dynamic_slice_in_dim(full_matrix, narrow_pos * part_size, part_size, along)

    (
        norm_one, query, key, value, inv, cov, attend, mixing, branch, after_mix, conv_one, act,
        stats,
    ) = front(
        images, picture_patch_extents, sharpness, source, triple_matrix, mixer_matrix,
        affine_entries, (bits,),
    )
    line = Line()
    low_weights, backs = [], []

    def lower(matrix):
        low_weights.append(line(cast, matrix))

    def from_above():
        backs.append(
            line(
                upstream, images, len(backs), picture_patch_extents, above, low_weights[0],
                affine_entries,
            )
        )

    stats, stats_two = everyone(
        line, stats, merge,
        (lambda: lower(shrink_matrix), lambda: lower(expand_matrix))
        + (from_above,) * images,
    )
    shrink_low, expand_low = low_weights
    grad_branch3, grad_above, branch_sums = zip(*backs)
    (
        block_out, norm_three, hidden_low, grad_hidden, grad_local, grad_bn, batch, tail_sums,
        bn_sums,
    ) = line(
        middle, images, picture_patch_extents, stats, stats_two, after_mix, act, above,
        expand_low, shrink_low, affine_entries, grad_above, branch_sums,
    )
    fed_halves = []

    def fed_half():
        fed_halves.append(
            line(
                fed_grads, 1 - len(fed_halves), narrow_parts, bits, norm_three, hidden_low,
                grad_hidden, grad_branch3,
            )
        )

    bn_sums, bn_two = everyone(line, bn_sums, add, (fed_half, fed_half))
    fed = Sum(line, bits, *fed_halves)
    fed.first()
    grad_mix, grad_branch1, inner_sums, bn_totals = line(
        inner_back, images, picture_patch_extents, bn_sums, bn_two, batch, act, conv_one, grad_bn,
        grad_local, after_mix, branch, affine_entries,
    )
    fed.second()
    mixer_low = mixer_matrix.astype(BF16)
    backs = []
    for image in range(images):
        backs.append(
            line(
                attention_back, images, image, picture_patch_extents, sharpness, query, key,
                value, inv, cov, attend, grad_branch1, mixer_low,
            )
        )
        if image == 0:
            fed.third()
    grad_joined, head_sums = zip(*backs)
    att_send, att_keep = line(
        att_grads, narrow_parts, bits, norm_one, mixing, grad_branch1, grad_joined
    )
    att = Sum(line, bits, att_send, att_keep)
    incoming_adjoint, vector_sums = line(
        outer_back, source, grad_mix, triple_matrix.astype(BF16), affine_entries, inner_sums,
        tail_sums, grad_joined, head_sums,
    )
    rider = (vector_sums, swap(vector_sums, *fed.last_step()))
    att.first()
    fed.mores()
    att.second()
    fed.turn(rider)
    att.third()
    att.mores()
    fed.backs()
    att.turn()
    att.backs()
    full_weights = (triple_matrix, mixer_matrix, expand_matrix, shrink_matrix)
    factors = [math.sqrt(max(1.0, full.shape[0] / full.shape[1])) for full in full_weights]
    masters = (
        own_part(triple_matrix, 1).T, own_part(mixer_matrix, 0), own_part(expand_matrix, 1),
        own_part(shrink_matrix, 0),
    )
    fed = Update(line, False, bits, fed.last(), (expand_velocity, shrink_velocity), SUM_ROWS)
    fed.across()
    att = Update(line, True, bits, att.last(), (triple_velocity.T, mixer_velocity))
    att.across()
    line.last += masters
    fed.sweep()
    vector_outs = line(
        vectors, model_width, fed.rows, fed.rows_other, bn_totals, batch, affine_entries,
        affine_velocity, sharpness, sharpness_velocity,
    )
    att.sweep()
    fed = fed.renew(factors[2:], masters[2:])
    att = att.renew(factors[:2], masters[:2])
    vec_full, sharpness_sum, new_vec, vec_state, sharpness_following, sharpness_buffer = (
        vector_outs
    )
    sharpness_sum, sharpness_following, sharpness_buffer = (
        row.reshape(-1) for row in (sharpness_sum, sharpness_following, sharpness_buffer)
    )
    for member in (0, 2, 4, 6):
        att[member] = att[member].T
    return (
        block_out.reshape(block_source.shape),
        incoming_adjoint.reshape(block_source.shape),
        att[0],
        att[1],
        fed[0],
        fed[1],
        vec_full,
        sharpness_sum,
        att[4],
        att[5],
        fed[4],
        fed[5],
        att[2],
        att[3],
        fed[2],
        fed[3],
        att[6],
        att[7],
        fed[6],
        fed[7],
        new_vec,
        vec_state,
        sharpness_following,
        sharpness_buffer,
    )


def solution(mesh):
    return jax.shard_map(
        on_device,
        mesh=mesh,
        in_specs=(
            P(("wide", "narrow"), None, None),
            P(("wide", "narrow"), None, None),
            P(("wide", "narrow"), None),
            P(),
            P(),
            P(),
            P(),
            P(),
            P(),
            P(None, "narrow"),
            P("narrow", None),
            P(None, "narrow"),
            P("narrow", None),
            P(),
            P(),
        ),
        out_specs=(
            P(("wide", "narrow"), None, None),
            P(("wide", "narrow"), None, None),
            P(None, "narrow"),
            P("narrow", None),
            P(None, "narrow"),
            P("narrow", None),
            P(),
            P(),
            P(None, "narrow"),
            P("narrow", None),
            P(None, "narrow"),
            P("narrow", None),
            P(None, "narrow"),
            P("narrow", None),
            P(None, "narrow"),
            P("narrow", None),
            P(None, "narrow"),
            P("narrow", None),
            P(None, "narrow"),
            P("narrow", None),
            P(),
            P(),
            P(),
            P(),
        ),
        check_vma=False,
    )
```

```python
import functools
import math

import jax
import jax.numpy as jnp
from jax import lax
from jax.experimental import pallas as pl
from jax.experimental.pallas import tpu as pltpu
from jax.sharding import PartitionSpec as P

GRID = 24
NS_STEPS = 5
SUM_ROWS = 48

layer_eps = 1e-06
unit_eps = 1e-06
batch_eps = 1e-05
frob_eps = 1e-07
velocity_damping = 0.5
rate_matrix = 0.25
affine_step_size = 0.2
coef_first = 3.4445
coef_second = -4.775
coef_third = 2.0315
root_half = 0.7071067811865476
inverse_root_tau = 0.3989422804014327
HIGH = lax.Precision.HIGH
F32 = jnp.float32
BF16 = jnp.bfloat16


def mul_nn(left, right, precision=None):
    return lax.dot_general(
        left, right, (((1,), (0,)), ((), ())), precision=precision, preferred_element_type=F32
    )


def mul_nt(left, right, precision=None):
    return lax.dot_general(
        left, right, (((1,), (1,)), ((), ())), precision=precision, preferred_element_type=F32
    )


def mul_tn(left, right, precision=None):
    return lax.dot_general(
        left, right, (((0,), (0,)), ((), ())), precision=precision, preferred_element_type=F32
    )


def fold_rows(source):
    total = source[0:8]
    for start in range(8, source.shape[0], 8):
        total = total + source[start : start + 8]
    return total


def row_sum(total):
    return jnp.sum(total, axis=0, keepdims=True)


def norm_rows(source):
    centre = source - jnp.mean(source, axis=-1, keepdims=True)
    inverse = lax.rsqrt(jnp.mean(centre * centre, axis=-1, keepdims=True) + layer_eps)
    return centre * inverse, inverse


def norm_back(grad_norm, normal, inverse, gain):
    scaled = grad_norm * gain
    return inverse * (
        scaled
        - jnp.mean(scaled, axis=-1, keepdims=True)
        - normal * jnp.mean(scaled * normal, axis=-1, keepdims=True)
    )


def normal_cdf(source):
    return 0.5 * (1.0 + lax.erf(source * root_half))


def density(source):
    return jnp.exp(-0.5 * source * source) * inverse_root_tau


def loop(start, stop, body, carry, unroll=1):
    return lax.fori_loop(start, stop, body, carry, unroll=unroll)


def here(row):
    return pl.ds(pl.multiple_of(row * GRID, 8), GRID)


class Rows:
    def __init__(self, extent_ref, width):
        self.extent_ref = extent_ref
        self.column = lax.broadcasted_iota(jnp.int32, (GRID, width), 0)

    def inside(self, row):
        image = row // GRID
        limit = jnp.where(
            row - image * GRID < self.extent_ref[image, 0], self.extent_ref[image, 1], 0
        )
        return self.column < limit

    def after(self, value):
        return jnp.where(self.column == 0, 0.0, pltpu.roll(value, 1, 0))

    def before(self, value):
        return jnp.where(self.column == GRID - 1, 0.0, pltpu.roll(value, GRID - 1, 0))

    def convolve(self, plane, row, tap):
        columns = [None] * 3
        for down, source in enumerate(three_rows(plane, row)):
            for across in range(3):
                term = source * tap(3 * down + across)
                columns[across] = term if down == 0 else columns[across] + term
        return columns[1] + self.after(columns[0]) + self.before(columns[2])


def padded(row):
    return row + 2 * (row // GRID) + 1


def three_rows(plane, row):
    first = padded(row) - 1
    for down in range(3):
        yield plane[here(first + down), :]


def clear_edges(plane, images):
    edge = jnp.zeros((GRID, plane.shape[1]), F32)
    for image in range(images):
        base = image * (GRID + 2) * GRID
        plane[base : base + GRID, :] = edge
        plane[base + (GRID + 1) * GRID : base + (GRID + 2) * GRID, :] = edge


def plane_of(images, width):
    return pltpu.VMEM((images * (GRID + 2) * GRID, width), F32)


VMEM = pl.BlockSpec(memory_space=pltpu.VMEM)
SMEM = pl.BlockSpec(memory_space=pltpu.SMEM)


ANY = pl.BlockSpec(memory_space=pl.ANY)
FAR = pl.BlockSpec(memory_space=pltpu.HBM)
COST_UNIT = 1e9
KERNEL_COST = {
    "front": 15.0, "middle": 27.0, "fed_grads": 2.7, "inner_back": 13.0, "attention_back": 5.5,
    "att_grads": 3.0, "outer_back": 5.0, "sweeps": 9.5, "prepare": 6.0, "renew": 2.5,
}


def call(kernel, name, spaces, outs, scratch, limit, args, flops=0, size=0, later=()):
    del flops, size
    cost = KERNEL_COST.get(name, 1.0)
    inputs, extra = len(args), len(later)

    def body(*refs):
        kernel(*refs[:inputs], *refs[inputs + extra :])

    return pl.pallas_call(
        body,
        in_specs=list(spaces) + [ANY] * extra,
        out_specs=[VMEM] * len(outs),
        out_shape=[jax.ShapeDtypeStruct(shape, dtype) for shape, dtype in outs],
        scratch_shapes=scratch,
        compiler_params=pltpu.CompilerParams(vmem_limit_bytes=limit << 20),
        cost_estimate=pl.CostEstimate(
            flops=int(cost * COST_UNIT), bytes_accessed=1024, transcendentals=0
        ),
        name=name,
    )(*args, *later)


def merge_stats(one, two):
    shift = one[0] / one[2] - two[0] / two[2]
    count = one[2] + two[2]
    spread = one[1] + two[1] + shift * shift * (one[2] * two[2] / count)
    return one[0] + two[0], spread, count


def get_rows(ref):
    return [ref[row : row + 1, :] for row in range(ref.shape[0])]


def put_rows(ref, values):
    for row, value in enumerate(values):
        ref[row : row + 1, :] = value


def merge_kernel(held_ref, other_ref, out_ref):
    put_rows(out_ref, merge_stats(get_rows(held_ref), get_rows(other_ref)))


def merge(held, other, later=()):
    return call(
        merge_kernel, "merge_rows", [VMEM, VMEM], [(held.shape, F32)], [], 1, (held, other), 1e4,
        1e4, later,
    )[0]


def front_kernel(
    images, extent_ref, sharp_ref, x_far, wq_far, wp_far, aff_far,
    norm_ref, query_ref, key_ref, value_ref, inv_ref, cov_ref, attend_ref, mixing_ref,
    branch_ref, mix_ref, conv_ref, act_ref, stat_ref,
    joined, plane, x_ref, wq_ref, wp_ref, aff_ref, arrived,
):
    copies = [
        pltpu.make_async_copy(far, near, arrived.at[index])
        for index, (far, near) in enumerate(
            ((x_far, x_ref), (aff_far, aff_ref), (wq_far, wq_ref), (wp_far, wp_ref))
        )
    ]
    for copy in copies:
        copy.start()
    tokens, width = x_ref.shape
    slots = tokens // images
    heads = sharp_ref.shape[0]
    head = width // heads
    rows = Rows(extent_ref, width)
    clear_edges(plane, images)
    zero = jnp.zeros((8, width), F32)

    def aff(row):
        return aff_ref[row : row + 1, :]

    def first(step, carry):
        place = pl.ds(pl.multiple_of(step * 48, 16), 48)
        value = x_ref[place, :].astype(F32)
        mix_ref[place, :] = value
        normal, _ = norm_rows(value)
        norm_ref[place, :] = (normal * aff(0) + aff(1)).astype(BF16)
        return carry

    copies[0].wait()
    copies[1].wait()
    loop(0, tokens // 48, first, 0, unroll=4)
    copies[2].wait()
    joined[...] = mul_nn(norm_ref[...], wq_ref[...].astype(BF16))

    def second(row, carry):
        query_sum, key_sum = carry
        at = here(row)
        inside = rows.inside(row)
        query = jnp.where(inside, joined[at, :width] + aff(2), 0.0)
        key = jnp.where(inside, joined[at, width : 2 * width] + aff(3), 0.0)
        query_ref[at, :] = query
        key_ref[at, :] = key
        value_ref[at, :] = joined[at, 2 * width :] + aff(4)
        return query_sum + fold_rows(query * query), key_sum + fold_rows(key * key)

    for image in range(images):
        span = slice(image * slots, (image + 1) * slots)
        low, high = image * GRID, (image + 1) * GRID
        query_sum, key_sum = loop(low, high, second, (zero, zero), unroll=2)
        query_inv = lax.rsqrt(row_sum(query_sum) + unit_eps)
        key_inv = lax.rsqrt(row_sum(key_sum) + unit_eps)
        inv_ref[2 * image : 2 * image + 1, :] = query_inv
        inv_ref[2 * image + 1 : 2 * image + 2, :] = key_inv

        def third(row, carry):
            at = here(row)
            query_ref[at, :] = query_ref[at, :] * query_inv
            key_ref[at, :] = key_ref[at, :] * key_inv
            return carry

        loop(low, high, third, 0, unroll=2)
        cov_ref[image] = mul_tn(query_ref[span, :], key_ref[span, :], HIGH)
        lane = lax.broadcasted_iota(jnp.int32, (head, width), 1)
        for group in range(heads):
            part = slice(group * head, (group + 1) * head)
            own = (lane >= group * head) & (lane < (group + 1) * head)
            scores = jnp.where(own, cov_ref[image, part, :] * sharp_ref[group], -jnp.inf)
            raised = jnp.exp(scores - jnp.max(scores, axis=-1, keepdims=True))
            attend_ref[image, part, :] = raised / jnp.sum(raised, axis=-1, keepdims=True)
        mixing_ref[span, :] = mul_nt(value_ref[span, :], attend_ref[image], HIGH).astype(BF16)
    copies[3].wait()
    branch_ref[...] = mul_nn(mixing_ref[...], wp_ref[...].astype(BF16))

    def fourth(row, carry):
        at = here(row)
        inside = rows.inside(row)
        branch = branch_ref[at, :] + aff(5)
        branch_ref[at, :] = branch
        after = mix_ref[at, :] + jnp.where(inside, aff(6) * branch, 0.0)
        mix_ref[at, :] = after
        normal, _ = norm_rows(after)
        plane[here(padded(row)), :] = jnp.where(inside, normal * aff(7) + aff(8), 0.0)
        return carry

    loop(0, images * GRID, fourth, 0, unroll=8)

    def fifth(row, total):
        at = here(row)
        summed = rows.convolve(plane, row, lambda index: aff(9 + index)) + aff(18)
        conv_ref[at, :] = summed
        active = summed * normal_cdf(summed)
        act_ref[at, :] = active
        return total + fold_rows(jnp.where(rows.inside(row), active, 0.0))

    for image in range(images):
        low, high = image * GRID, (image + 1) * GRID
        act_sum = row_sum(loop(low, high, fifth, zero, unroll=2))
        count = (extent_ref[image, 0] * extent_ref[image, 1]).astype(F32)
        centre = act_sum / count

        def sixth(row, total):
            shifted = jnp.where(rows.inside(row), act_ref[here(row), :] - centre, 0.0)
            return total + fold_rows(shifted * shifted)

        spread = row_sum(loop(low, high, sixth, zero, unroll=4))
        own = (act_sum, spread, jnp.full_like(centre, count))
        stats = own if image == 0 else merge_stats(stats, own)
    put_rows(stat_ref, stats)


def front(images, extents, sharpness, source, wq, wp, aff, later=()):
    tokens, width = source.shape
    full, low, square = ((tokens, width), F32), ((tokens, width), BF16), ((images, width, width), F32)
    far = (extents, sharpness, source, wq, wp, aff)
    outs = [
        low, full, full, full, ((2 * images, width), F32), square, square, low,
        full, full, full, full, ((3, width), F32),
    ]
    return call(
        functools.partial(front_kernel, images), "front",
        [SMEM, SMEM, FAR, FAR, FAR, FAR], outs,
        [
            pltpu.VMEM((tokens, 3 * width), F32), plane_of(images, width),
            pltpu.VMEM(source.shape, source.dtype), pltpu.VMEM(wq.shape, F32),
            pltpu.VMEM(wp.shape, F32), pltpu.VMEM(aff.shape, F32), pltpu.SemaphoreType.DMA((4,)),
        ], 16,
        [pltpu.with_memory_space_constraint(array, pltpu.HBM) for array in far], 2e10, 3e7, later,
    )


def cast_kernel(source_ref, out_ref):
    out_ref[...] = source_ref[...].astype(BF16)


def cast(source, later=()):
    return call(
        cast_kernel, "cast", [VMEM], [(source.shape, BF16)], [], 2, (source,), later=later
    )[0]


def upstream_kernel(image, extent_ref, up_ref, w2_ref, aff_ref, gbranch_ref, dhidden_ref, sum_ref):
    slots, width = gbranch_ref.shape
    rows = Rows(extent_ref, width)
    low, high = image * GRID, (image + 1) * GRID

    def body(pair, total):
        grads = []
        for row in (2 * pair, 2 * pair + 1):
            value = up_ref[here(row), :].astype(F32) * aff_ref[39:40, :]
            grads.append(jnp.where(rows.inside(row), value, 0.0))
        grad = jnp.concatenate(grads, axis=0).astype(BF16)
        gbranch_ref[pl.ds(pl.multiple_of((2 * pair - low) * GRID, 16), 2 * GRID), :] = grad
        return total + fold_rows(grad.astype(F32))

    sum_ref[...] = loop(low // 2, high // 2, body, jnp.zeros((8, width), F32), unroll=2)
    dhidden_ref[...] = mul_nt(gbranch_ref[...], w2_ref[...])


def upstream(images, image, extents, up, w2, aff, later=()):
    tokens, width = up.shape
    slots, inner = tokens // images, w2.shape[0]
    return call(
        functools.partial(upstream_kernel, image), "upstream", [SMEM] + [VMEM] * 3,
        [((slots, width), BF16), ((slots, inner), F32), ((8, width), F32)], [], 2,
        (extents, up, w2, aff), later=later,
    )


def middle_kernel(
    images, extent_ref, stat_ref, stat_two_ref, mix_ref, act_ref, up_ref, w1_ref, w2_ref, aff_ref,
    *refs
):
    dhidden_refs, branch_sum_refs, refs = refs[:images], refs[images : 2 * images], refs[2 * images :]
    (
        out_ref, norm_ref, hidlow_ref, ghid_ref, glocal_ref, gbn_ref, batch_ref, sum_ref, bn_ref,
        hidden, conv_s, normal_s, inverse_s, branch_s, plane, grad_plane,
    ) = refs
    tokens, width = mix_ref.shape
    inner = w1_ref.shape[1]
    rows = Rows(extent_ref, width)
    clear_edges(plane, images)
    clear_edges(grad_plane, images)
    zero = jnp.zeros((8, width), F32)
    all_rows = images * GRID

    def aff(row):
        return aff_ref[row : row + 1, :]

    act_sum, spread, tally = merge_stats(get_rows(stat_ref), get_rows(stat_two_ref))
    centre = act_sum / tally
    inverse_std = lax.rsqrt(spread / tally + batch_eps)
    batch_ref[0:1, :] = centre
    batch_ref[1:2, :] = inverse_std
    batch_ref[2:3, :] = tally

    def first(row, carry):
        inside = rows.inside(row)
        unit = (act_ref[here(row), :] - centre) * inverse_std
        plane[here(padded(row)), :] = jnp.where(inside, unit * aff(19) + aff(20), 0.0)
        return carry

    loop(0, all_rows, first, 0, unroll=2)

    def second(row, carry):
        at = here(row)
        inside = rows.inside(row)
        summed = rows.convolve(plane, row, lambda index: aff(21 + index)) + aff(30)
        conv_s[at, :] = summed
        after = mix_ref[at, :] + jnp.where(inside, aff(31) * summed, 0.0)
        branch_s[at, :] = after
        return carry

    loop(0, all_rows, second, 0, unroll=2)

    def second_norm(step, carry):
        at = pl.ds(pl.multiple_of(step * 48, 16), 48)
        normal, inverse = norm_rows(branch_s[at, :])
        normal_s[at, :] = normal
        inverse_s[at, :] = inverse
        norm_ref[at, :] = (normal * aff(32) + aff(33)).astype(BF16)
        return carry

    loop(0, tokens // 48, second_norm, 0, unroll=4)

    sum_ref[17:18, :] = row_sum(sum(ref[...] for ref in branch_sum_refs))
    slots = tokens // images
    quarters = inner // width
    bias_sums = [zero] * quarters
    for image in range(images):
        span = slice(image * slots, (image + 1) * slots)
        hidden[...] = mul_nn(norm_ref[span, :], w1_ref[...])
        dhidden = dhidden_refs[image]
        for quarter in range(quarters):
            cols = slice(quarter * width, (quarter + 1) * width)
            bias = aff(34 + quarter)

            def fourth(step, total):
                at = pl.ds(pl.multiple_of(step * 16, 16), 16)
                to = pl.ds(pl.multiple_of(image * slots + step * 16, 16), 16)
                value = hidden[at, cols] + bias
                cdf = normal_cdf(value)
                hidlow_ref[to, cols] = (value * cdf).astype(BF16)
                grad = (dhidden[at, cols] * (cdf + value * density(value))).astype(BF16)
                ghid_ref[to, cols] = grad
                return total + fold_rows(grad.astype(F32))

            bias_sums[quarter] = loop(0, slots // 16, fourth, bias_sums[quarter], unroll=2)
        gbn_ref[span, :] = mul_nt(ghid_ref[span, :], w1_ref[...])
        glocal_ref[span, :] = mul_nn(hidlow_ref[span, :], w2_ref[...])
    for quarter in range(quarters):
        sum_ref[13 + quarter : 14 + quarter, :] = row_sum(bias_sums[quarter])

    def fifth(row, total):
        at = here(row)
        inside = rows.inside(row)
        branch = jnp.where(inside, glocal_ref[at, :] + aff(38), 0.0)
        out_ref[at, :] = (branch_s[at, :] + aff(39) * branch).astype(BF16)
        return total + fold_rows(up_ref[at, :].astype(F32) * branch)

    sum_ref[18:19, :] = row_sum(loop(0, all_rows, fifth, zero, unroll=2))

    def sixth(row, carry):
        gain_sum, shift_sum, scale_sum, bias_sum = carry
        at = here(row)
        inside = rows.inside(row)
        grad_norm = gbn_ref[at, :]
        normal = normal_s[at, :]
        grad = up_ref[at, :].astype(F32) + norm_back(grad_norm, normal, inverse_s[at, :], aff(32))
        glocal_ref[at, :] = grad
        kept = jnp.where(inside, grad, 0.0)
        scaled = kept * aff(31)
        grad_plane[here(padded(row)), :] = scaled
        return (
            gain_sum + fold_rows(grad_norm * normal), shift_sum + fold_rows(grad_norm),
            scale_sum + fold_rows(kept * conv_s[at, :]), bias_sum + fold_rows(scaled),
        )

    gain_sum, shift_sum, scale_sum, bias_sum = loop(0, all_rows, sixth, (zero,) * 4, unroll=6)
    sum_ref[11:12, :] = row_sum(gain_sum)
    sum_ref[12:13, :] = row_sum(shift_sum)
    sum_ref[10:11, :] = row_sum(scale_sum)
    sum_ref[9:10, :] = row_sum(bias_sum)

    def seventh(row, carry):
        bias_bn, gain_bn = carry
        at = here(row)
        summed = rows.convolve(grad_plane, row, lambda index: aff(29 - index))
        summed = jnp.where(rows.inside(row), summed, 0.0)
        gbn_ref[at, :] = summed
        unit = (act_ref[at, :] - centre) * inverse_std
        return bias_bn + fold_rows(summed), gain_bn + fold_rows(summed * unit)

    bias_bn, gain_bn = loop(0, all_rows, seventh, (zero, zero), unroll=2)
    bn_ref[0:1, :] = row_sum(bias_bn)
    bn_ref[1:2, :] = row_sum(gain_bn)
    kernel_sums(rows, plane, grad_plane, images, sum_ref, 0)


def kernel_sums(rows, plane, grad_plane, images, sum_ref, base):
    zero = jnp.zeros((8, plane.shape[1]), F32)

    def body(row, carry):
        grad = grad_plane[here(padded(row)), :]
        grads = (rows.before(grad), grad, rows.after(grad))
        totals = list(carry)
        for down, source in enumerate(three_rows(plane, row)):
            for across in range(3):
                index = 3 * down + across
                totals[index] = totals[index] + fold_rows(grads[across] * source)
        return tuple(totals)

    totals = loop(0, images * GRID, body, (zero,) * 9)
    for index, total in enumerate(totals):
        sum_ref[base + index : base + index + 1, :] = row_sum(total)


def middle(
    images, extents, stats, stats_two, after_mix, act, up, w1, w2, aff, dhidden, branch_sums,
    later=(),
):
    tokens, width = after_mix.shape
    inner = w1.shape[1]
    full, low, wide = ((tokens, width), F32), ((tokens, width), BF16), ((tokens, inner), BF16)
    outs = [
        low, low, wide, wide, full, full, ((3, width), F32), ((19, width), F32), ((2, width), F32),
    ]
    return call(
        functools.partial(middle_kernel, images), "middle",
        [SMEM] + [VMEM] * (8 + 2 * images), outs,
        [
            pltpu.VMEM((tokens // images, inner), F32),
            pltpu.VMEM((tokens, width), F32), pltpu.VMEM((tokens, width), F32),
            pltpu.VMEM((tokens, 1), F32), pltpu.VMEM((tokens, width), F32),
            plane_of(images, width), plane_of(images, width),
        ], 18,
        (extents, stats, stats_two, after_mix, act, up, w1, w2, aff, *dhidden, *branch_sums), 3e10,
        4e7, later,
    )


def fed_grads_kernel(shift, bit_ref, norm_ref, hidlow_ref, ghid_ref, *refs):
    *gbranch_refs, out_ref = refs
    slots = gbranch_refs[0].shape[0]
    width = norm_ref.shape[1]
    pairs = out_ref.shape[0]
    size = ghid_ref.shape[1] // (2 * pairs)
    low = bit_ref[0] if shift == 0 else 1 - bit_ref[0]
    for pair in range(pairs):
        cols = pl.ds(pl.multiple_of((2 * pair + low) * size, 128), size)
        out_ref[pair, 0:size, :] = mul_tn(ghid_ref[:, cols], norm_ref[...])
        total = None
        for image, gbranch_ref in enumerate(gbranch_refs):
            span = slice(image * slots, (image + 1) * slots)
            part = mul_tn(hidlow_ref[span, cols], gbranch_ref[...])
            total = part if image == 0 else total + part
        out_ref[pair, size : 2 * size, :] = total


def fed_grads(shift, parts, bit, norm, hidlow, ghid, gbranch, later=()):
    width, inner = norm.shape[1], ghid.shape[1]
    return call(
        functools.partial(fed_grads_kernel, shift, bit), "fed_grads", [VMEM] * (3 + len(gbranch)),
        [((parts // 2, 2 * inner // parts, width), F32)], [], 6,
        (norm, hidlow, ghid, *gbranch), 3e9, 1e7, later,
    )[0]


def inner_back_kernel(
    images, extent_ref, total_ref, total_two_ref, batch_ref, act_ref, conv_ref, gbn_ref, glocal_ref, mix_ref,
    branch_ref, aff_ref, gmix_ref, gbranch_ref, sum_ref, bn_ref,
    normal_s, inverse_s, plane, grad_plane,
):
    tokens, width = act_ref.shape
    rows = Rows(extent_ref, width)
    clear_edges(plane, images)
    clear_edges(grad_plane, images)
    zero = jnp.zeros((8, width), F32)
    all_rows = images * GRID

    def aff(row):
        return aff_ref[row : row + 1, :]

    totals = total_ref[...] + total_two_ref[...]
    bn_ref[...] = totals
    centre, inverse_std, tally = batch_ref[0:1, :], batch_ref[1:2, :], batch_ref[2:3, :]
    bias_mean, gain_mean = totals[0:1, :] / tally, totals[1:2, :] / tally
    factor = aff(19) * inverse_std

    def first(row, total):
        at = here(row)
        unit = (act_ref[at, :] - centre) * inverse_std
        value = conv_ref[at, :]
        slope = normal_cdf(value) + value * density(value)
        grad = factor * (gbn_ref[at, :] - (bias_mean + unit * gain_mean)) * slope
        grad = jnp.where(rows.inside(row), grad, 0.0)
        grad_plane[here(padded(row)), :] = grad
        return total + fold_rows(grad)

    sum_ref[13:14, :] = row_sum(loop(0, all_rows, first, zero, unroll=2))

    def second(row, carry):
        at = here(row)
        normal, inverse = norm_rows(mix_ref[at, :])
        normal_s[at, :] = normal
        inverse_s[at, :] = inverse
        plane[here(padded(row)), :] = jnp.where(rows.inside(row), normal * aff(7) + aff(8), 0.0)
        return carry

    loop(0, all_rows, second, 0, unroll=8)
    kernel_sums(rows, plane, grad_plane, images, sum_ref, 4)

    def third(row, carry):
        summed = rows.convolve(grad_plane, row, lambda index: aff(17 - index))
        gmix_ref[here(row), :] = jnp.where(rows.inside(row), summed, 0.0)
        return carry

    loop(0, all_rows, third, 0, unroll=2)

    def fourth(row, carry):
        gain_sum, shift_sum, scale_sum, bias_sum = carry
        at = here(row)
        grad_norm, normal = gmix_ref[at, :], normal_s[at, :]
        grad = glocal_ref[at, :] + norm_back(grad_norm, normal, inverse_s[at, :], aff(7))
        gmix_ref[at, :] = grad
        kept = jnp.where(rows.inside(row), grad, 0.0)
        low = (kept * aff(6)).astype(BF16)
        gbranch_ref[at, :] = low
        return (
            gain_sum + fold_rows(grad_norm * normal), shift_sum + fold_rows(grad_norm),
            scale_sum + fold_rows(kept * branch_ref[at, :]), bias_sum + fold_rows(low.astype(F32)),
        )

    gain_sum, shift_sum, scale_sum, bias_sum = loop(0, all_rows, fourth, (zero,) * 4, unroll=6)
    sum_ref[0:1, :] = row_sum(bias_sum)
    sum_ref[1:2, :] = row_sum(scale_sum)
    sum_ref[2:3, :] = row_sum(gain_sum)
    sum_ref[3:4, :] = row_sum(shift_sum)


def inner_back(
    images, extents, totals, totals_two, batch, act, conv, gbn, glocal, after_mix, branch, aff,
    later=(),
):
    tokens, width = act.shape
    outs = [((tokens, width), F32), ((tokens, width), BF16), ((14, width), F32), ((2, width), F32)]
    return call(
        functools.partial(inner_back_kernel, images), "inner_back",
        [SMEM] + [VMEM] * 10, outs,
        [
            pltpu.VMEM((tokens, width), F32), pltpu.VMEM((tokens, 1), F32),
            plane_of(images, width), plane_of(images, width),
        ], 10,
        (extents, totals, totals_two, batch, act, conv, gbn, glocal, after_mix, branch, aff), 2e10, 3e7,
        later,
    )


def attention_back_kernel(
    image, extent_ref, sharp_ref, query_ref, key_ref, value_ref, inv_ref, cov_ref, attend_ref,
    gbranch_ref, wp_ref, gjoined, head_ref,
    gmixing, gscore, gquery, gkey,
):
    slots, width = gmixing.shape
    heads = sharp_ref.shape[0]
    head = width // heads
    rows = Rows(extent_ref, width)
    zero = jnp.zeros((8, width), F32)
    span = slice(image * slots, (image + 1) * slots)
    low, high = image * GRID, (image + 1) * GRID
    gmixing[...] = mul_nt(gbranch_ref[span, :], wp_ref[...])
    lane = lax.broadcasted_iota(jnp.int32, (1, width), 1)
    sharp_sum = jnp.zeros((1, width), F32)
    gscore[...] = mul_tn(gmixing[...], value_ref[span, :], HIGH)
    for group in range(heads):
        part = slice(group * head, (group + 1) * head)
        attend = attend_ref[image, part, :]
        grad = gscore[part, :]
        grad = attend * (grad - jnp.sum(attend * grad, axis=-1, keepdims=True))
        gscore[part, :] = grad * sharp_ref[group]
        amount = jnp.sum(
            jnp.sum(grad * cov_ref[image, part, :], axis=0, keepdims=True), axis=1, keepdims=True
        )
        sharp_sum = sharp_sum + jnp.where(lane == group, amount, 0.0)
    gquery[...] = mul_nt(key_ref[span, :], gscore[...], HIGH)
    gkey[...] = mul_nn(query_ref[span, :], gscore[...], HIGH)
    gmixing[...] = mul_nn(gmixing[...], attend_ref[image], HIGH)

    def first(row, carry):
        query_dot, key_dot = carry
        at = here(row)
        to = here(row - low)
        return (
            query_dot + fold_rows(gquery[to, :] * query_ref[at, :]),
            key_dot + fold_rows(gkey[to, :] * key_ref[at, :]),
        )

    query_dot, key_dot = loop(low, high, first, (zero, zero), unroll=2)
    query_dot, key_dot = row_sum(query_dot), row_sum(key_dot)
    query_inv = inv_ref[2 * image : 2 * image + 1, :]
    key_inv = inv_ref[2 * image + 1 : 2 * image + 2, :]

    def second(pair, carry):
        totals = list(carry)
        thirds = ([], [], [])
        for row in (2 * pair, 2 * pair + 1):
            at = here(row)
            to = here(row - low)
            inside = rows.inside(row)
            grad = query_inv * (gquery[to, :] - query_ref[at, :] * query_dot)
            thirds[0].append(jnp.where(inside, grad, 0.0))
            grad = key_inv * (gkey[to, :] - key_ref[at, :] * key_dot)
            thirds[1].append(jnp.where(inside, grad, 0.0))
            thirds[2].append(gmixing[to, :])
        to = pl.ds(pl.multiple_of((2 * pair - low) * GRID, 16), 2 * GRID)
        for third in range(3):
            value = jnp.concatenate(thirds[third], axis=0).astype(BF16)
            gjoined[to, third * width : (third + 1) * width] = value
            totals[third] = totals[third] + fold_rows(value.astype(F32))
        return tuple(totals)

    bias = loop(low // 2, high // 2, second, (zero,) * 3)
    put_rows(head_ref, [row_sum(total) for total in bias] + [sharp_sum])


def attention_back(
    images, image, extents, sharpness, query, key, value, inv, cov, attend, gbranch, wp, later=(),
):
    tokens, width = query.shape
    slots = tokens // images
    return call(
        functools.partial(attention_back_kernel, image), "attention_back",
        [SMEM] * 2 + [VMEM] * 8, [((slots, 3 * width), BF16), ((4, width), F32)],
        [
            pltpu.VMEM((slots, width), F32), pltpu.VMEM((width, width), F32),
            pltpu.VMEM((slots, width), F32), pltpu.VMEM((slots, width), F32),
        ], 8,
        (extents, sharpness, query, key, value, inv, cov, attend, gbranch, wp), 2e10, 2e7, later,
    )


def att_grads_kernel(
    bits_ref, norm_ref, mixing_ref, gbranch_ref, *refs
):
    *gjoined_refs, send_ref, keep_ref, matrix = refs
    slots = gjoined_refs[0].shape[0]
    width = norm_ref.shape[1]
    pairs = send_ref.shape[0]
    for image, gjoined_ref in enumerate(gjoined_refs):
        part = mul_tn(gjoined_ref[...], norm_ref[image * slots : (image + 1) * slots, :])
        rows = slice(0, 3 * width)
        matrix[rows, :] = part if image == 0 else matrix[rows, :] + part
    matrix[3 * width :, :] = mul_tn(mixing_ref[...], gbranch_ref[...])
    joined_rows, mixer_rows = 3 * width // (2 * pairs), width // (2 * pairs)
    for pair in range(pairs):
        for target, place in ((keep_ref, bits_ref[0]), (send_ref, 1 - bits_ref[0])):
            part = 2 * pair + place
            at = pl.ds(pl.multiple_of(part * joined_rows, 8), joined_rows)
            target[pair, 0:joined_rows, :] = matrix[at, :]
            at = pl.ds(pl.multiple_of(3 * width + part * mixer_rows, 8), mixer_rows)
            target[pair, joined_rows:, :] = matrix[at, :]


def att_grads(parts, bits, norm, mixing, gbranch, gjoined, later=()):
    width = norm.shape[1]
    share = ((parts // 2, 4 * width // parts, width), F32)
    return call(
        functools.partial(att_grads_kernel, bits), "att_grads", [VMEM] * (3 + len(gjoined)), [share, share],
        [pltpu.VMEM((4 * width, width), F32)], 8,
        (norm, mixing, gbranch, *gjoined), 2e9, 8e6, later,
    )


def outer_back_kernel(
    x_ref, gmix_ref, wq_ref, aff_ref, inner_ref, tail_ref, *refs
):
    *refs, incoming_ref, vector_ref, gnorm = refs
    images = len(refs) // 2
    gjoined_refs, head_refs = refs[:images], refs[images:]
    slots = gjoined_refs[0].shape[0]
    tokens, width = x_ref.shape
    zero = jnp.zeros((8, width), F32)
    for image, gjoined_ref in enumerate(gjoined_refs):
        gnorm[image * slots : (image + 1) * slots, :] = mul_nt(gjoined_ref[...], wq_ref[...])

    def body(step, carry):
        gain_sum, shift_sum = carry
        at = pl.ds(pl.multiple_of(step * 48, 16), 48)
        normal, inverse = norm_rows(x_ref[at, :].astype(F32))
        grad = gnorm[at, :]
        incoming_ref[at, :] = gmix_ref[at, :] + norm_back(grad, normal, inverse, aff_ref[0:1, :])
        return gain_sum + fold_rows(grad * normal), shift_sum + fold_rows(grad)

    gain_sum, shift_sum = loop(0, tokens // 48, body, (zero, zero), unroll=4)
    vector_ref[...] = jnp.zeros_like(vector_ref)
    vector_ref[0:1, :] = row_sum(gain_sum)
    vector_ref[1:2, :] = row_sum(shift_sum)
    head = sum(ref[...] for ref in head_refs[1:]) + head_refs[0][...]
    vector_ref[2:5, :] = head[0:3, :]
    vector_ref[5:19, :] = inner_ref[...]
    vector_ref[21:40, :] = tail_ref[...]
    vector_ref[40:41, :] = head[3:4, :]


def outer_back(source, gmix, wq, aff, inner, tail, gjoined, head, later=()):
    tokens, width = source.shape
    return call(
        outer_back_kernel, "outer_back", [VMEM] * (6 + 2 * len(head)),
        [((tokens, width), F32), ((SUM_ROWS, width), F32)], [pltpu.VMEM((tokens, width), F32)], 6,
        (source, gmix, wq, aff, inner, tail, *gjoined, *head), 5e9, 1e7, later,
    )


def row_blocks(rows):
    step = next(size for size in (32, 24, 16, 8, rows) if rows % size == 0)
    return rows // step, step


def blocks(rows, body):
    count, step = row_blocks(rows)

    def inner(index, carry):
        start = index * step
        body(pl.multiple_of(start, 8) if step % 8 == 0 else start, step)
        return carry

    loop(0, count, inner, 0)


def halve_first_kernel(
    high, side, bits_ref, held_ref, other_ref, send_high_ref, keep_high_ref, send_side_ref,
    keep_side_ref,
):
    half, quarter = send_high_ref.shape[0], send_side_ref.shape[1]
    high_bit, side_bit = bits_ref[high], bits_ref[side]

    def first(start, size):
        at = pl.ds(start, size)
        send_high_ref[at, :] = held_ref[1 - high_bit, at, :] + other_ref[1 - high_bit, at, :]
        keep_high_ref[at, :] = held_ref[high_bit, at, :] + other_ref[high_bit, at, :]

    def second(start, size):
        at = pl.ds(start, size)
        for target, bit in ((send_side_ref, 1 - side_bit), (keep_side_ref, side_bit)):
            here = pl.ds(pl.multiple_of(half + bit * quarter, 8) + start, size)
            for part in range(2):
                target[part, at, :] = held_ref[part, here, :] + other_ref[part, here, :]

    blocks(half, first)
    blocks(quarter, second)


def halve_first(bits, high, side, held, other, later=()):
    rows, width = held.shape[-2:]
    half, quarter = ((rows // 2, width), F32), ((2, rows // 4, width), F32)
    return call(
        functools.partial(halve_first_kernel, high, side, bits), "halve_first", [VMEM, VMEM],
        [half, half, quarter, quarter], [], 2, (held, other), held.size, 16 * held.size,
        later,
    )


def halve_second_kernel(
    high, side, bits_ref, one_ref, one_other_ref, two_ref, two_other_ref,
    send_one_ref, keep_one_ref, send_two_ref, keep_two_ref,
):
    quarter = send_one_ref.shape[0]
    high_bit, side_bit = bits_ref[high], bits_ref[side]

    def body(start, size):
        at = pl.ds(start, size)
        for target, bit in ((send_one_ref, 1 - side_bit), (keep_one_ref, side_bit)):
            here = pl.ds(pl.multiple_of(bit * quarter, 8) + start, size)
            target[at, :] = one_ref[here, :] + one_other_ref[here, :]
        for target, bit in ((send_two_ref, 1 - high_bit), (keep_two_ref, high_bit)):
            target[at, :] = two_ref[bit, at, :] + two_other_ref[bit, at, :]

    blocks(quarter, body)


def halve_second(bits, high, side, one, one_other, two, two_other, later=()):
    quarter = (two.shape[-2:], F32)
    return call(
        functools.partial(halve_second_kernel, high, side, bits), "halve_second", [VMEM] * 4,
         [quarter] * 4, [], 2,
        (one, one_other, two, two_other), one.size, 32 * one.size, later,
    )


def halve_third_kernel(
    place, bits_ref, one_ref, one_other_ref, two_ref, two_other_ref, send_ref, keep_ref
):
    bit = bits_ref[place]
    eighth = one_ref.shape[0] // 2

    def body(start, size):
        for target, half in ((send_ref, 1 - bit), (keep_ref, bit)):
            here = pl.ds(pl.multiple_of(half * eighth, 8) + start, size)
            target[pl.ds(start, size), :] = one_ref[here, :] + one_other_ref[here, :]
            target[pl.ds(eighth + start, size), :] = two_ref[here, :] + two_other_ref[here, :]

    blocks(eighth, body)


def halve_third(bits, place, one, one_other, two, two_other, later=()):
    return call(
        functools.partial(halve_third_kernel, place, bits), "halve_third", [VMEM] * 4,
        [(one.shape, F32)] * 2, [], 2, (one, one_other, two, two_other), one.size,
        32 * one.size, later,
    )


def split_add_kernel(place, bits_ref, held_ref, other_ref, send_ref, keep_ref):
    bit = bits_ref[place]

    def body(start, size):
        at = pl.ds(start, size)
        send_ref[at, :] = held_ref[1 - bit, at, :] + other_ref[1 - bit, at, :]
        keep_ref[at, :] = held_ref[bit, at, :] + other_ref[bit, at, :]

    blocks(send_ref.shape[0], body)


def split_add(bits, place, held, other, later=()):
    half = (held.shape[-2:], F32)
    return call(
        functools.partial(split_add_kernel, place, bits), "split_add", [VMEM, VMEM], [half, half],
        [], 2, (held, other), held.size, 16 * held.size, later,
    )


def add_kernel(held_ref, other_ref, out_ref):
    def body(start, size):
        at = pl.ds(start, size)
        out_ref[at, :] = held_ref[at, :] + other_ref[at, :]

    blocks(held_ref.shape[0], body)


def add(held, other, later=()):
    return call(
        add_kernel, "add_rows", [VMEM, VMEM], [(held.shape, F32)], [], 2, (held, other),
        held.size, 12 * held.size, later,
    )[0]


def append_kernel(held_ref, other_ref, rider_ref, rider_other_ref, out_ref):
    rows = held_ref.shape[0]

    def body(start, size):
        at = pl.ds(start, size)
        out_ref[at, :] = held_ref[at, :] + other_ref[at, :]

    blocks(rows, body)
    out_ref[rows:, :] = rider_ref[...] + rider_other_ref[...]


def append(held, other, rider, rider_other, later=()):
    rows, width = held.shape
    return call(
        append_kernel, "append_rows", [VMEM] * 4, [((rows + rider.shape[0], width), F32)], [], 2,
        (held, other, rider, rider_other), held.size, 12 * held.size, later,
    )[0]


def join_kernel(place, rider, bits_ref, held_ref, other_ref, out_ref):
    bit = bits_ref[place]
    rows = held_ref.shape[0] - rider

    def body(start, size):
        mine = pl.ds(pl.multiple_of(bit * rows, 8) + start, size)
        others = pl.ds(pl.multiple_of((1 - bit) * rows, 8) + start, size)
        out_ref[mine, :] = held_ref[pl.ds(start, size), :]
        out_ref[others, :] = other_ref[pl.ds(start, size), :]

    blocks(rows, body)
    if rider:
        out_ref[2 * rows :, :] = held_ref[rows:, :] + other_ref[rows:, :]


def join(bits, place, rider, held, other, later=()):
    rows, width = held.shape
    return call(
        functools.partial(join_kernel, place, rider, bits), "join_rows", [VMEM, VMEM],
        [((2 * rows - rider, width), F32)], [], 2, (held, other), held.size,
        16 * held.size, later,
    )[0]


def join_last_kernel(place, rider, bits_ref, held_ref, other_ref, out_ref, rider_ref):
    bit = bits_ref[place]
    rows = (held_ref.shape[0] - rider) // 4

    def body(start, size):
        for half in range(2):
            for following in range(2):
                source = pl.ds((2 * following + half) * rows + start, size)
                for side, ref in ((bit, held_ref), (1 - bit, other_ref)):
                    first = pl.multiple_of((4 * half + 2 * side + following) * rows, 8)
                    out_ref[pl.ds(first + start, size), :] = ref[source, :]

    blocks(rows, body)
    if rider:
        rider_ref[...] = held_ref[4 * rows :, :] + other_ref[4 * rows :, :]
    else:
        rider_ref[...] = jnp.zeros_like(rider_ref)


def join_last(bits, place, rider, held, other, later=()):
    rows, width = held.shape
    return call(
        functools.partial(join_last_kernel, place, rider, bits), "join_last", [VMEM, VMEM],
        [((2 * (rows - rider), width), F32), ((max(rider, 8), width), F32)], [], 2,
        (held, other), held.size, 16 * held.size, later,
    )


def upper_blocks(size):
    count = size // 128
    return [(row, column) for row in range(count) for column in range(row, count)]


def block(index):
    return slice(128 * index, 128 * index + 128)


def packed_rows(size, rider):
    return 128 * len(upper_blocks(size)) + rider * (size // 128)


def put_packed(target, source):
    for index, (row, column) in enumerate(upper_blocks(source.shape[0])):
        target[block(index), :] = source[block(row), block(column)]


def halves(source):
    high = source.astype(BF16)
    return high, (source - high.astype(F32)).astype(BF16)


def put_left(left, source):
    high, low = halves(source)
    size = source.shape[1]
    left[:, 0:size], left[:, size : 2 * size], left[:, 2 * size :] = high, high, low


def put_right(right, columns, source):
    high, low = halves(source)
    size = source.shape[0]
    right[0:size, columns], right[size : 2 * size, columns] = high, low
    right[2 * size :, columns] = high


def sweeps_kernel(mine_ref, other_ref, out_ref, now, total, left, right, step):
    size = out_ref.shape[0]
    for index, (row, column) in enumerate(upper_blocks(size)):
        part = mine_ref[block(index), :] + other_ref[block(index), :]
        now[block(row), block(column)] = part
        if row != column:
            now[block(column), block(row)] = part.T
    row = lax.broadcasted_iota(jnp.int32, (size, size), 0)
    diagonal = row == lax.broadcasted_iota(jnp.int32, (size, size), 1)
    trace = jnp.where(diagonal, now[...], 0.0)
    trace = jnp.sum(jnp.sum(trace, axis=0, keepdims=True), axis=1, keepdims=True)
    norm = jnp.sqrt(trace) + frob_eps
    now[...] = now[...] / (norm * norm)
    near, far = slice(0, size), slice(size, 2 * size)
    for sweep_index in range(NS_STEPS):
        last = sweep_index == NS_STEPS - 1
        put_left(left, now[...])
        put_right(right, near, now[...])
        square = mul_nn(left[...], right[:, near])
        step[...] = (
            jnp.where(diagonal, coef_first, 0.0) + coef_second * now[...] + coef_third * square
        )
        put_left(left, step[...])
        if sweep_index == 0:
            total[...] = step[...] / norm
            now[...] = mul_nn(left[...], right[:, near])
        elif last:
            put_right(right, near, total[...])
            out_ref[...] = mul_nn(left[...], right[:, near])
        else:
            put_right(right, far, total[...])
            both = mul_nn(left[...], right[...])
            now[...] = both[:, near]
            total[...] = both[:, far]
        if not last:
            put_right(right, near, now[...])
            now[...] = mul_nn(left[...], right[:, near])


def sweeps(width, mine, other, later=()):
    square = pltpu.VMEM((width, width), F32)
    return call(
        sweeps_kernel, "sweeps", [VMEM, VMEM], [((width, width), F32)],
        [
            square, square, pltpu.VMEM((width, 3 * width), BF16),
            pltpu.VMEM((3 * width, 2 * width), BF16), square,
        ], 9, (mine, other), 1e10, 4e6, later,
    )[0]


def prepare_kernel(
    turned, rider, bit_ref, share_ref, first_ref, second_ref, rider_ref,
    grad_one_ref, grad_two_ref, state_one_ref, state_two_ref, send_ref, keep_ref,
):
    split = first_ref.shape[0 if turned else 1]
    tall = second_ref.shape[0]
    grad_one = share_ref[0:split, :]
    grad_one_ref[...] = grad_one if turned else grad_one.T
    state_one_ref[...] = velocity_damping * first_ref[...] + grad_one_ref[...]
    grad_two_ref[...] = share_ref[split : split + tall, :]
    state_two_ref[...] = velocity_damping * second_ref[...] + grad_two_ref[...]
    gram = mul_tn if turned else mul_nt
    gram_one = gram(state_one_ref[...], state_one_ref[...], HIGH)
    gram_two = mul_tn(state_two_ref[...], state_two_ref[...], HIGH)
    even = bit_ref[0] == 0
    width = share_ref.shape[1]
    put_packed(keep_ref, jnp.where(even, gram_one, gram_two))
    put_packed(send_ref, jnp.where(even, gram_two, gram_one))
    if rider:
        for column in range(width // 128):
            first = packed_rows(width, 0) + column * rider
            keep_ref[first : first + rider, :] = rider_ref[:, block(column)]
            send_ref[first : first + rider, :] = rider_ref[:, block(column)]


def prepare(turned, rider, bit, share, first, second, rows, later=()):
    width = share.shape[1]
    upper = ((packed_rows(width, rider), 128), F32)
    one, two = (first.shape, F32), (second.shape, F32)
    return call(
        functools.partial(prepare_kernel, turned, rider, bit), "prepare", [VMEM] * 4,
        [one, two, one, two, upper, upper], [], 8, (share, first, second, rows), 2e9, 6e6, later,
    )


def renew_kernel(
    turned, factors, bit_ref, mine_ref, other_ref, state_one_ref, state_two_ref, one_ref, two_ref,
    new_one_ref, new_two_ref, low_one_ref, low_two_ref,
):
    even = bit_ref[0] == 0
    poly_one = jnp.where(even, mine_ref[...], other_ref[...])
    poly_two = jnp.where(even, other_ref[...], mine_ref[...])
    if turned:
        field_one = mul_nn(state_one_ref[...], poly_one, HIGH)
    else:
        field_one = mul_nn(poly_one, state_one_ref[...], HIGH)
    new_one = one_ref[...] - (rate_matrix * factors[0]) * field_one
    new_one_ref[...] = new_one
    low_one_ref[...] = new_one.astype(BF16)
    new_two = two_ref[...] - (rate_matrix * factors[1]) * mul_nn(
        state_two_ref[...], poly_two, HIGH
    )
    new_two_ref[...] = new_two
    low_two_ref[...] = new_two.astype(BF16)


def renew(
    turned, factors, bit, mine, other, state_one, state_two, one, two, later=(),
):
    outs = [(one.shape, F32), (two.shape, F32), (one.shape, BF16), (two.shape, BF16)]
    return call(
        functools.partial(renew_kernel, turned, factors, bit), "renew", [VMEM] * 6, outs, [],
        8, (mine, other, state_one, state_two, one, two), 2e9, 6e6, later,
    )


def vectors_kernel(
    start, rider, held_ref, other_ref, bn_ref, batch_ref, aff_ref, aff_velocity_ref, sharp_ref,
    sharp_velocity_ref, full_ref, sharp_sum_ref, new_aff_ref, aff_state_ref, new_sharp_ref,
    sharp_state_ref,
):
    rows, width = aff_ref.shape
    group = sharp_ref.shape[1]
    for column in range(width // 128):
        first = start + column * rider
        total = held_ref[first : first + rider, :] + other_ref[first : first + rider, :]
        full_ref[:, block(column)] = total[0:rows, :]
        if column == 0:
            sharp_sum_ref[...] = total[rows : rows + 1, 0:group]
    full_ref[rows // 2 - 1 : rows // 2, :] = bn_ref[1:2, :]
    full_ref[rows // 2 : rows // 2 + 1, :] = bn_ref[0:1, :]
    step_size = affine_step_size * lax.rsqrt(batch_ref[2:3, :])
    state = velocity_damping * aff_velocity_ref[...] + full_ref[...]
    aff_state_ref[...] = state
    new_aff_ref[...] = aff_ref[...] - step_size * state
    state = velocity_damping * sharp_velocity_ref[...] + sharp_sum_ref[...]
    sharp_state_ref[...] = state
    new_sharp_ref[...] = sharp_ref[...] - step_size[:, 0:group] * state


def vectors(
    width, rider, held, other, bn_totals, batch, aff, aff_velocity, sharp, sharp_velocity,
    later=(),
):
    start = packed_rows(width, 0)
    sharp, sharp_velocity = sharp[None], sharp_velocity[None]
    large, small = (aff.shape, F32), (sharp.shape, F32)
    return call(
        functools.partial(vectors_kernel, start, rider), "vectors", [VMEM] * 8,
        [large, small, large, large, small, small], [], 2,
        (held, other, bn_totals, batch, aff, aff_velocity, sharp, sharp_velocity), 0, 0, later,
    )


def bits_of(size):
    return [1 << place for place in range(size.bit_length() - 1)]


def swap(source, axis, bit):
    size = lax.axis_size(axis)
    return lax.ppermute(source, axis, [(member, member ^ bit) for member in range(size)])


def axis_steps(axis):
    base = 0 if axis == "narrow" else len(bits_of(lax.axis_size("narrow")))
    return [(axis, bit, base + place) for place, bit in enumerate(bits_of(lax.axis_size(axis)))]


def all_steps():
    return axis_steps("narrow") + axis_steps("wide")


class OwnBits:
    def __init__(self):
        self.steps = all_steps()

    def __getitem__(self, place):
        axis, bit, _ = self.steps[place]
        return lax.rem(lax.div(lax.axis_index(axis), bit), 2)


class Line:
    def __init__(self):
        self.last = ()

    def __call__(self, kernel, *args):
        out = kernel(*args, later=self.last)
        self.last = (out[-1] if isinstance(out, (list, tuple)) else out,)
        return out


def everyone(line, rows, combine, fillers=()):
    fillers = list(fillers)
    steps = all_steps()
    for axis, bit, _ in steps[:-1]:
        other = swap(rows, axis, bit)
        if axis != "narrow" or bit > 1:
            if fillers:
                fillers.pop(0)()
        rows = line(combine, rows, other)
    axis, bit, _ = steps[-1]
    other = swap(rows, axis, bit)
    for filler in fillers:
        filler()
    return rows, other


class Sum:
    def __init__(self, line, bits, send, keep):
        self.line, self.bits, self.keep = line, bits, keep
        (_, self.low, _), (_, self.high, self.high_place) = axis_steps("narrow")
        _, self.side, self.side_place = axis_steps("wide")[0]
        self.rest = axis_steps("wide")[1:]
        self.other = swap(send, "narrow", self.low)
        self.rider = 0

    def first(self):
        send, self.one, send_two, self.two = self.line(
            halve_first, self.bits, self.high_place, self.side_place, self.keep, self.other
        )
        self.one_other = swap(send, "narrow", self.high)
        self.two_other = swap(send_two, "wide", self.side)

    def second(self):
        send, self.one, send_two, self.two = self.line(
            halve_second, self.bits, self.high_place, self.side_place, self.one, self.one_other,
            self.two, self.two_other,
        )
        self.one_other = swap(send, "wide", self.side)
        self.two_other = swap(send_two, "narrow", self.high)

    def third(self):
        axis, bit, place = self.rest[0]
        send, self.keep = self.line(
            halve_third, self.bits, place, self.one, self.one_other, self.two, self.two_other
        )
        self.other = swap(send, axis, bit)
        self.done = 1

    def more(self):
        axis, bit, place = self.rest[self.done]
        shape = self.keep.shape
        self.done += 1
        if self.done < len(self.rest):
            keep, other = (array.reshape(2, -1, shape[1]) for array in (self.keep, self.other))
            send, self.keep = self.line(split_add, self.bits, place, keep, other)
            self.other = swap(send, axis, bit)
        else:
            self.keep = self.line(add, self.keep, self.other)
            self.other = swap(self.keep, axis, bit)

    def mores(self):
        while self.done < len(self.rest):
            self.more()

    def last_step(self):
        axis, bit, _ = self.rest[-1]
        return axis, bit

    def turn(self, rider=None):
        if rider is None:
            self.held = self.line(add, self.keep, self.other)
        else:
            self.held = self.line(append, self.keep, self.other, *rider)
            self.rider = rider[0].shape[0]
        self.place = len(self.rest) - 1
        self.back_move()

    def back_move(self):
        self.place -= 1
        axis, bit, _ = self.rest[self.place] if self.place >= 0 else axis_steps("wide")[0]
        self.other = swap(self.held, axis, bit)

    def back(self):
        _, _, place = self.rest[self.place]
        self.held = self.line(join, self.bits, place, self.rider, self.held, self.other)
        self.back_move()

    def backs(self):
        while self.place >= 0:
            self.back()

    def last(self):
        return self.line(
            join_last, self.bits, self.side_place, self.rider, self.held, self.other
        )


class Update:
    def __init__(self, line, turned, bits, gathered, states, rider=0):
        share, rows = gathered
        self.line, self.turned, self.bits = line, turned, bits
        self.width = share.shape[1]
        *self.grads, self.one, self.two, send, self.keep = line(
            prepare, turned, rider, bits, share, *states, rows
        )
        self.other = swap(send, "narrow", 1)

    def across(self):
        (axis, bit, _) = axis_steps("narrow")[1]
        self.keep = self.line(add, self.keep, self.other)
        self.other = swap(self.keep, axis, bit)
        self.sums = (self.keep, self.other)

    def sweep(self):
        self.keep = self.line(sweeps, self.width, self.keep, self.other)
        self.other = swap(self.keep, "narrow", 1)

    def renew(self, factors, masters):
        new = self.line(
            renew, self.turned, factors, self.bits, self.keep, self.other, self.one, self.two,
            *masters,
        )
        return self.grads + [self.one, self.two] + list(new)


def on_device(
    block_source,
    upstream_adjoint,
    picture_patch_extents,
    triple_matrix,
    mixer_matrix,
    expand_matrix,
    shrink_matrix,
    affine_entries,
    sharpness,
    triple_velocity,
    mixer_velocity,
    expand_velocity,
    shrink_velocity,
    affine_velocity,
    sharpness_velocity,
):
    images, slot_count, model_width = block_source.shape
    group_index = sharpness.shape[0]
    narrow_parts = lax.axis_size("narrow")
    narrow_pos = lax.axis_index("narrow")
    bits = OwnBits()
    source = block_source.reshape(-1, model_width)
    above = upstream_adjoint.reshape(-1, model_width)

    def own_part(full_matrix, along):
        part_size = full_matrix.shape[along] // narrow_parts
        return lax.dynamic_slice_in_dim(full_matrix, narrow_pos * part_size, part_size, along)

    (
        norm_one, query, key, value, inv, cov, attend, mixing, branch, after_mix, conv_one, act,
        stats,
    ) = front(
        images, picture_patch_extents, sharpness, source, triple_matrix, mixer_matrix,
        affine_entries,
    )
    line = Line()
    low_weights, backs = [], []

    def lower(matrix):
        low_weights.append(line(cast, matrix))

    def from_above():
        backs.append(
            line(
                upstream, images, len(backs), picture_patch_extents, above, low_weights[0],
                affine_entries,
            )
        )

    stats, stats_two = everyone(
        line, stats, merge,
        (lambda: lower(shrink_matrix), lambda: lower(expand_matrix))
        + (from_above,) * images,
    )
    shrink_low, expand_low = low_weights
    grad_branch3, grad_above, branch_sums = zip(*backs)
    (
        block_out, norm_three, hidden_low, grad_hidden, grad_local, grad_bn, batch, tail_sums,
        bn_sums,
    ) = line(
        middle, images, picture_patch_extents, stats, stats_two, after_mix, act, above,
        expand_low, shrink_low, affine_entries, grad_above, branch_sums,
    )
    fed_halves = []

    def fed_half():
        fed_halves.append(
            line(
                fed_grads, 1 - len(fed_halves), narrow_parts, bits, norm_three, hidden_low,
                grad_hidden, grad_branch3,
            )
        )

    bn_sums, bn_two = everyone(line, bn_sums, add, (fed_half, fed_half))
    fed = Sum(line, bits, *fed_halves)
    fed.first()
    grad_mix, grad_branch1, inner_sums, bn_totals = line(
        inner_back, images, picture_patch_extents, bn_sums, bn_two, batch, act, conv_one, grad_bn,
        grad_local, after_mix, branch, affine_entries,
    )
    fed.second()
    mixer_low = mixer_matrix.astype(BF16)
    backs = []
    for image in range(images):
        backs.append(
            line(
                attention_back, images, image, picture_patch_extents, sharpness, query, key,
                value, inv, cov, attend, grad_branch1, mixer_low,
            )
        )
        if image == 0:
            fed.third()
    grad_joined, head_sums = zip(*backs)
    att_send, att_keep = line(
        att_grads, narrow_parts, bits, norm_one, mixing, grad_branch1, grad_joined
    )
    att = Sum(line, bits, att_send, att_keep)
    incoming_adjoint, vector_sums = line(
        outer_back, source, grad_mix, triple_matrix.astype(BF16), affine_entries, inner_sums,
        tail_sums, grad_joined, head_sums,
    )
    rider = (vector_sums, swap(vector_sums, *fed.last_step()))
    full_weights = (triple_matrix, mixer_matrix, expand_matrix, shrink_matrix)
    factors = [math.sqrt(max(1.0, full.shape[0] / full.shape[1])) for full in full_weights]
    masters = (
        own_part(triple_matrix, 1).T, own_part(mixer_matrix, 0), own_part(expand_matrix, 1),
        own_part(shrink_matrix, 0),
    )
    att.first()
    fed.mores()
    att.second()
    fed.turn(rider)
    att.third()
    att.mores()
    fed.backs()
    att.turn()
    att.backs()
    fed = Update(line, False, bits, fed.last(), (expand_velocity, shrink_velocity), SUM_ROWS)
    att = Update(line, True, bits, att.last(), (triple_velocity.T, mixer_velocity))
    fed.across()
    att.across()
    fed.sweep()
    line.last += masters
    att.sweep()
    vector_outs = line(
        vectors, model_width, SUM_ROWS, *fed.sums, bn_totals, batch, affine_entries,
        affine_velocity, sharpness, sharpness_velocity,
    )
    fed = fed.renew(factors[2:], masters[2:])
    att = att.renew(factors[:2], masters[:2])
    vec_full, sharpness_sum, new_vec, vec_state, sharpness_following, sharpness_buffer = (
        vector_outs
    )
    sharpness_sum, sharpness_following, sharpness_buffer = (
        row.reshape(-1) for row in (sharpness_sum, sharpness_following, sharpness_buffer)
    )
    for member in (0, 2, 4, 6):
        att[member] = att[member].T
    return (
        block_out.reshape(block_source.shape),
        incoming_adjoint.reshape(block_source.shape),
        att[0],
        att[1],
        fed[0],
        fed[1],
        vec_full,
        sharpness_sum,
        att[4],
        att[5],
        fed[4],
        fed[5],
        att[2],
        att[3],
        fed[2],
        fed[3],
        att[6],
        att[7],
        fed[6],
        fed[7],
        new_vec,
        vec_state,
        sharpness_following,
        sharpness_buffer,
    )


def solution(mesh):
    return jax.shard_map(
        on_device,
        mesh=mesh,
        in_specs=(
            P(("wide", "narrow"), None, None),
            P(("wide", "narrow"), None, None),
            P(("wide", "narrow"), None),
            P(),
            P(),
            P(),
            P(),
            P(),
            P(),
            P(None, "narrow"),
            P("narrow", None),
            P(None, "narrow"),
            P("narrow", None),
            P(),
            P(),
        ),
        out_specs=(
            P(("wide", "narrow"), None, None),
            P(("wide", "narrow"), None, None),
            P(None, "narrow"),
            P("narrow", None),
            P(None, "narrow"),
            P("narrow", None),
            P(),
            P(),
            P(None, "narrow"),
            P("narrow", None),
            P(None, "narrow"),
            P("narrow", None),
            P(None, "narrow"),
            P("narrow", None),
            P(None, "narrow"),
            P("narrow", None),
            P(None, "narrow"),
            P("narrow", None),
            P(None, "narrow"),
            P("narrow", None),
            P(),
            P(),
            P(),
            P(),
        ),
        check_vma=False,
    )
```

```python
import functools
import math

import jax
import jax.numpy as jnp
from jax import lax
from jax.experimental import pallas as pl
from jax.experimental.pallas import tpu as pltpu
from jax.sharding import PartitionSpec as P

GRID = 24
NS_STEPS = 5
SUM_ROWS = 48

layer_eps = 1e-06
unit_eps = 1e-06
batch_eps = 1e-05
frob_eps = 1e-07
velocity_damping = 0.5
rate_matrix = 0.25
affine_step_size = 0.2
coef_first = 3.4445
coef_second = -4.775
coef_third = 2.0315
root_half = 0.7071067811865476
inverse_root_tau = 0.3989422804014327
HIGH = lax.Precision.HIGH
F32 = jnp.float32
BF16 = jnp.bfloat16


def mul_nn(left, right, precision=None):
    return lax.dot_general(
        left, right, (((1,), (0,)), ((), ())), precision=precision, preferred_element_type=F32
    )


def mul_nt(left, right, precision=None):
    return lax.dot_general(
        left, right, (((1,), (1,)), ((), ())), precision=precision, preferred_element_type=F32
    )


def mul_tn(left, right, precision=None):
    return lax.dot_general(
        left, right, (((0,), (0,)), ((), ())), precision=precision, preferred_element_type=F32
    )


def fold_rows(source):
    total = source[0:8]
    for start in range(8, source.shape[0], 8):
        total = total + source[start : start + 8]
    return total


def row_sum(total):
    return jnp.sum(total, axis=0, keepdims=True)


def norm_rows(source):
    centre = source - jnp.mean(source, axis=-1, keepdims=True)
    inverse = lax.rsqrt(jnp.mean(centre * centre, axis=-1, keepdims=True) + layer_eps)
    return centre * inverse, inverse


def norm_back(grad_norm, normal, inverse, gain):
    scaled = grad_norm * gain
    return inverse * (
        scaled
        - jnp.mean(scaled, axis=-1, keepdims=True)
        - normal * jnp.mean(scaled * normal, axis=-1, keepdims=True)
    )


def normal_cdf(source):
    return 0.5 * (1.0 + lax.erf(source * root_half))


def density(source):
    return jnp.exp(-0.5 * source * source) * inverse_root_tau


def loop(start, stop, body, carry, unroll=1):
    return lax.fori_loop(start, stop, body, carry, unroll=unroll)


def here(row):
    return pl.ds(pl.multiple_of(row * GRID, 8), GRID)


class Rows:
    def __init__(self, extent_ref, width):
        self.extent_ref = extent_ref
        self.column = lax.broadcasted_iota(jnp.int32, (GRID, width), 0)

    def inside(self, row):
        image = row // GRID
        limit = jnp.where(
            row - image * GRID < self.extent_ref[image, 0], self.extent_ref[image, 1], 0
        )
        return self.column < limit

    def after(self, value):
        return jnp.where(self.column == 0, 0.0, pltpu.roll(value, 1, 0))

    def before(self, value):
        return jnp.where(self.column == GRID - 1, 0.0, pltpu.roll(value, GRID - 1, 0))

    def convolve(self, plane, row, tap):
        columns = [None] * 3
        for down, source in enumerate(three_rows(plane, row)):
            for across in range(3):
                term = source * tap(3 * down + across)
                columns[across] = term if down == 0 else columns[across] + term
        return columns[1] + self.after(columns[0]) + self.before(columns[2])


def padded(row):
    return row + 2 * (row // GRID) + 1


def three_rows(plane, row):
    first = padded(row) - 1
    for down in range(3):
        yield plane[here(first + down), :]


def clear_edges(plane, images):
    edge = jnp.zeros((GRID, plane.shape[1]), F32)
    for image in range(images):
        base = image * (GRID + 2) * GRID
        plane[base : base + GRID, :] = edge
        plane[base + (GRID + 1) * GRID : base + (GRID + 2) * GRID, :] = edge


def plane_of(images, width):
    return pltpu.VMEM((images * (GRID + 2) * GRID, width), F32)


VMEM = pl.BlockSpec(memory_space=pltpu.VMEM)
SMEM = pl.BlockSpec(memory_space=pltpu.SMEM)


ANY = pl.BlockSpec(memory_space=pl.ANY)
FAR = pl.BlockSpec(memory_space=pltpu.HBM)
COST_UNIT = 3e9
KERNEL_COST = {
    "front": 15.0, "middle": 27.0, "fed_grads": 2.7, "inner_back": 13.0, "attention_back": 5.5,
    "att_grads": 3.0, "outer_back": 5.0, "sweeps": 9.5, "prepare": 6.0, "renew": 2.5,
}


def call(kernel, name, spaces, outs, scratch, limit, args, flops=0, size=0, later=()):
    del flops, size
    cost = KERNEL_COST.get(name, 1.0)
    inputs, extra = len(args), len(later)

    def body(*refs):
        kernel(*refs[:inputs], *refs[inputs + extra :])

    return pl.pallas_call(
        body,
        in_specs=list(spaces) + [ANY] * extra,
        out_specs=[VMEM] * len(outs),
        out_shape=[jax.ShapeDtypeStruct(shape, dtype) for shape, dtype in outs],
        scratch_shapes=scratch,
        compiler_params=pltpu.CompilerParams(vmem_limit_bytes=limit << 20),
        cost_estimate=pl.CostEstimate(
            flops=int(cost * COST_UNIT), bytes_accessed=1024, transcendentals=0
        ),
        name=name,
    )(*args, *later)


def merge_stats(one, two):
    shift = one[0] / one[2] - two[0] / two[2]
    count = one[2] + two[2]
    spread = one[1] + two[1] + shift * shift * (one[2] * two[2] / count)
    return one[0] + two[0], spread, count


def get_rows(ref):
    return [ref[row : row + 1, :] for row in range(ref.shape[0])]


def put_rows(ref, values):
    for row, value in enumerate(values):
        ref[row : row + 1, :] = value


def merge_kernel(held_ref, other_ref, out_ref):
    put_rows(out_ref, merge_stats(get_rows(held_ref), get_rows(other_ref)))


def merge(held, other, later=()):
    return call(
        merge_kernel, "merge_rows", [VMEM, VMEM], [(held.shape, F32)], [], 1, (held, other), 1e4,
        1e4, later,
    )[0]


def front_kernel(
    images, extent_ref, sharp_ref, x_far, wq_far, wp_far, aff_far,
    norm_ref, query_ref, key_ref, value_ref, inv_ref, cov_ref, attend_ref, mixing_ref,
    branch_ref, mix_ref, conv_ref, act_ref, stat_ref,
    joined, plane, x_ref, wq_ref, wp_ref, aff_ref, arrived,
):
    copies = [
        pltpu.make_async_copy(far, near, arrived.at[index])
        for index, (far, near) in enumerate(
            ((x_far, x_ref), (aff_far, aff_ref), (wq_far, wq_ref), (wp_far, wp_ref))
        )
    ]
    for copy in copies:
        copy.start()
    tokens, width = x_ref.shape
    slots = tokens // images
    heads = sharp_ref.shape[0]
    head = width // heads
    rows = Rows(extent_ref, width)
    clear_edges(plane, images)
    zero = jnp.zeros((8, width), F32)

    def aff(row):
        return aff_ref[row : row + 1, :]

    def first(step, carry):
        place = pl.ds(pl.multiple_of(step * 48, 16), 48)
        value = x_ref[place, :].astype(F32)
        mix_ref[place, :] = value
        normal, _ = norm_rows(value)
        norm_ref[place, :] = (normal * aff(0) + aff(1)).astype(BF16)
        return carry

    copies[0].wait()
    copies[1].wait()
    loop(0, tokens // 48, first, 0, unroll=4)
    copies[2].wait()
    joined[...] = mul_nn(norm_ref[...], wq_ref[...].astype(BF16))

    def second(row, carry):
        query_sum, key_sum = carry
        at = here(row)
        inside = rows.inside(row)
        query = jnp.where(inside, joined[at, :width] + aff(2), 0.0)
        key = jnp.where(inside, joined[at, width : 2 * width] + aff(3), 0.0)
        query_ref[at, :] = query
        key_ref[at, :] = key
        value_ref[at, :] = joined[at, 2 * width :] + aff(4)
        return query_sum + fold_rows(query * query), key_sum + fold_rows(key * key)

    for image in range(images):
        span = slice(image * slots, (image + 1) * slots)
        low, high = image * GRID, (image + 1) * GRID
        query_sum, key_sum = loop(low, high, second, (zero, zero), unroll=2)
        query_inv = lax.rsqrt(row_sum(query_sum) + unit_eps)
        key_inv = lax.rsqrt(row_sum(key_sum) + unit_eps)
        inv_ref[2 * image : 2 * image + 1, :] = query_inv
        inv_ref[2 * image + 1 : 2 * image + 2, :] = key_inv

        def third(row, carry):
            at = here(row)
            query_ref[at, :] = query_ref[at, :] * query_inv
            key_ref[at, :] = key_ref[at, :] * key_inv
            return carry

        loop(low, high, third, 0, unroll=2)
        cov_ref[image] = mul_tn(query_ref[span, :], key_ref[span, :], HIGH)
        lane = lax.broadcasted_iota(jnp.int32, (head, width), 1)
        for group in range(heads):
            part = slice(group * head, (group + 1) * head)
            own = (lane >= group * head) & (lane < (group + 1) * head)
            scores = jnp.where(own, cov_ref[image, part, :] * sharp_ref[group], -jnp.inf)
            raised = jnp.exp(scores - jnp.max(scores, axis=-1, keepdims=True))
            attend_ref[image, part, :] = raised / jnp.sum(raised, axis=-1, keepdims=True)
        mixing_ref[span, :] = mul_nt(value_ref[span, :], attend_ref[image], HIGH).astype(BF16)
    copies[3].wait()
    branch_ref[...] = mul_nn(mixing_ref[...], wp_ref[...].astype(BF16))

    def fourth(row, carry):
        at = here(row)
        inside = rows.inside(row)
        branch = branch_ref[at, :] + aff(5)
        branch_ref[at, :] = branch
        after = mix_ref[at, :] + jnp.where(inside, aff(6) * branch, 0.0)
        mix_ref[at, :] = after
        normal, _ = norm_rows(after)
        plane[here(padded(row)), :] = jnp.where(inside, normal * aff(7) + aff(8), 0.0)
        return carry

    loop(0, images * GRID, fourth, 0, unroll=8)

    def fifth(row, total):
        at = here(row)
        summed = rows.convolve(plane, row, lambda index: aff(9 + index)) + aff(18)
        conv_ref[at, :] = summed
        active = summed * normal_cdf(summed)
        act_ref[at, :] = active
        return total + fold_rows(jnp.where(rows.inside(row), active, 0.0))

    for image in range(images):
        low, high = image * GRID, (image + 1) * GRID
        act_sum = row_sum(loop(low, high, fifth, zero, unroll=2))
        count = (extent_ref[image, 0] * extent_ref[image, 1]).astype(F32)
        centre = act_sum / count

        def sixth(row, total):
            shifted = jnp.where(rows.inside(row), act_ref[here(row), :] - centre, 0.0)
            return total + fold_rows(shifted * shifted)

        spread = row_sum(loop(low, high, sixth, zero, unroll=4))
        own = (act_sum, spread, jnp.full_like(centre, count))
        stats = own if image == 0 else merge_stats(stats, own)
    put_rows(stat_ref, stats)


def front(images, extents, sharpness, source, wq, wp, aff, later=()):
    tokens, width = source.shape
    full, low, square = ((tokens, width), F32), ((tokens, width), BF16), ((images, width, width), F32)
    far = (extents, sharpness, source, wq, wp, aff)
    outs = [
        low, full, full, full, ((2 * images, width), F32), square, square, low,
        full, full, full, full, ((3, width), F32),
    ]
    return call(
        functools.partial(front_kernel, images), "front",
        [SMEM, SMEM, FAR, FAR, FAR, FAR], outs,
        [
            pltpu.VMEM((tokens, 3 * width), F32), plane_of(images, width),
            pltpu.VMEM(source.shape, source.dtype), pltpu.VMEM(wq.shape, F32),
            pltpu.VMEM(wp.shape, F32), pltpu.VMEM(aff.shape, F32), pltpu.SemaphoreType.DMA((4,)),
        ], 16,
        [pltpu.with_memory_space_constraint(array, pltpu.HBM) for array in far], 2e10, 3e7, later,
    )


def cast_kernel(source_ref, out_ref):
    out_ref[...] = source_ref[...].astype(BF16)


def cast(source, later=()):
    return call(
        cast_kernel, "cast", [VMEM], [(source.shape, BF16)], [], 2, (source,), later=later
    )[0]


def upstream_kernel(image, extent_ref, up_ref, w2_ref, aff_ref, gbranch_ref, dhidden_ref, sum_ref):
    slots, width = gbranch_ref.shape
    rows = Rows(extent_ref, width)
    low, high = image * GRID, (image + 1) * GRID

    def body(pair, total):
        grads = []
        for row in (2 * pair, 2 * pair + 1):
            value = up_ref[here(row), :].astype(F32) * aff_ref[39:40, :]
            grads.append(jnp.where(rows.inside(row), value, 0.0))
        grad = jnp.concatenate(grads, axis=0).astype(BF16)
        gbranch_ref[pl.ds(pl.multiple_of((2 * pair - low) * GRID, 16), 2 * GRID), :] = grad
        return total + fold_rows(grad.astype(F32))

    sum_ref[...] = loop(low // 2, high // 2, body, jnp.zeros((8, width), F32), unroll=2)
    dhidden_ref[...] = mul_nt(gbranch_ref[...], w2_ref[...])


def upstream(images, image, extents, up, w2, aff, later=()):
    tokens, width = up.shape
    slots, inner = tokens // images, w2.shape[0]
    return call(
        functools.partial(upstream_kernel, image), "upstream", [SMEM] + [VMEM] * 3,
        [((slots, width), BF16), ((slots, inner), F32), ((8, width), F32)], [], 2,
        (extents, up, w2, aff), later=later,
    )


def middle_kernel(
    images, extent_ref, stat_ref, stat_two_ref, mix_ref, act_ref, up_ref, w1_ref, w2_ref, aff_ref,
    *refs
):
    dhidden_refs, branch_sum_refs, refs = refs[:images], refs[images : 2 * images], refs[2 * images :]
    (
        out_ref, norm_ref, hidlow_ref, ghid_ref, glocal_ref, gbn_ref, batch_ref, sum_ref, bn_ref,
        hidden, conv_s, normal_s, inverse_s, branch_s, plane, grad_plane,
    ) = refs
    tokens, width = mix_ref.shape
    inner = w1_ref.shape[1]
    rows = Rows(extent_ref, width)
    clear_edges(plane, images)
    clear_edges(grad_plane, images)
    zero = jnp.zeros((8, width), F32)
    all_rows = images * GRID

    def aff(row):
        return aff_ref[row : row + 1, :]

    act_sum, spread, tally = merge_stats(get_rows(stat_ref), get_rows(stat_two_ref))
    centre = act_sum / tally
    inverse_std = lax.rsqrt(spread / tally + batch_eps)
    batch_ref[0:1, :] = centre
    batch_ref[1:2, :] = inverse_std
    batch_ref[2:3, :] = tally

    def first(row, carry):
        inside = rows.inside(row)
        unit = (act_ref[here(row), :] - centre) * inverse_std
        plane[here(padded(row)), :] = jnp.where(inside, unit * aff(19) + aff(20), 0.0)
        return carry

    loop(0, all_rows, first, 0, unroll=2)

    def second(row, carry):
        at = here(row)
        inside = rows.inside(row)
        summed = rows.convolve(plane, row, lambda index: aff(21 + index)) + aff(30)
        conv_s[at, :] = summed
        after = mix_ref[at, :] + jnp.where(inside, aff(31) * summed, 0.0)
        branch_s[at, :] = after
        return carry

    loop(0, all_rows, second, 0, unroll=2)

    def second_norm(step, carry):
        at = pl.ds(pl.multiple_of(step * 48, 16), 48)
        normal, inverse = norm_rows(branch_s[at, :])
        normal_s[at, :] = normal
        inverse_s[at, :] = inverse
        norm_ref[at, :] = (normal * aff(32) + aff(33)).astype(BF16)
        return carry

    loop(0, tokens // 48, second_norm, 0, unroll=4)

    sum_ref[17:18, :] = row_sum(sum(ref[...] for ref in branch_sum_refs))
    slots = tokens // images
    quarters = inner // width
    bias_sums = [zero] * quarters
    for image in range(images):
        span = slice(image * slots, (image + 1) * slots)
        hidden[...] = mul_nn(norm_ref[span, :], w1_ref[...])
        dhidden = dhidden_refs[image]
        for quarter in range(quarters):
            cols = slice(quarter * width, (quarter + 1) * width)
            bias = aff(34 + quarter)

            def fourth(step, total):
                at = pl.ds(pl.multiple_of(step * 16, 16), 16)
                to = pl.ds(pl.multiple_of(image * slots + step * 16, 16), 16)
                value = hidden[at, cols] + bias
                cdf = normal_cdf(value)
                hidlow_ref[to, cols] = (value * cdf).astype(BF16)
                grad = (dhidden[at, cols] * (cdf + value * density(value))).astype(BF16)
                ghid_ref[to, cols] = grad
                return total + fold_rows(grad.astype(F32))

            bias_sums[quarter] = loop(0, slots // 16, fourth, bias_sums[quarter], unroll=2)
        gbn_ref[span, :] = mul_nt(ghid_ref[span, :], w1_ref[...])
        glocal_ref[span, :] = mul_nn(hidlow_ref[span, :], w2_ref[...])
    for quarter in range(quarters):
        sum_ref[13 + quarter : 14 + quarter, :] = row_sum(bias_sums[quarter])

    def fifth(row, total):
        at = here(row)
        inside = rows.inside(row)
        branch = jnp.where(inside, glocal_ref[at, :] + aff(38), 0.0)
        out_ref[at, :] = (branch_s[at, :] + aff(39) * branch).astype(BF16)
        return total + fold_rows(up_ref[at, :].astype(F32) * branch)

    sum_ref[18:19, :] = row_sum(loop(0, all_rows, fifth, zero, unroll=2))

    def sixth(row, carry):
        gain_sum, shift_sum, scale_sum, bias_sum = carry
        at = here(row)
        inside = rows.inside(row)
        grad_norm = gbn_ref[at, :]
        normal = normal_s[at, :]
        grad = up_ref[at, :].astype(F32) + norm_back(grad_norm, normal, inverse_s[at, :], aff(32))
        glocal_ref[at, :] = grad
        kept = jnp.where(inside, grad, 0.0)
        scaled = kept * aff(31)
        grad_plane[here(padded(row)), :] = scaled
        return (
            gain_sum + fold_rows(grad_norm * normal), shift_sum + fold_rows(grad_norm),
            scale_sum + fold_rows(kept * conv_s[at, :]), bias_sum + fold_rows(scaled),
        )

    gain_sum, shift_sum, scale_sum, bias_sum = loop(0, all_rows, sixth, (zero,) * 4, unroll=6)
    sum_ref[11:12, :] = row_sum(gain_sum)
    sum_ref[12:13, :] = row_sum(shift_sum)
    sum_ref[10:11, :] = row_sum(scale_sum)
    sum_ref[9:10, :] = row_sum(bias_sum)

    def seventh(row, carry):
        bias_bn, gain_bn = carry
        at = here(row)
        summed = rows.convolve(grad_plane, row, lambda index: aff(29 - index))
        summed = jnp.where(rows.inside(row), summed, 0.0)
        gbn_ref[at, :] = summed
        unit = (act_ref[at, :] - centre) * inverse_std
        return bias_bn + fold_rows(summed), gain_bn + fold_rows(summed * unit)

    bias_bn, gain_bn = loop(0, all_rows, seventh, (zero, zero), unroll=2)
    bn_ref[0:1, :] = row_sum(bias_bn)
    bn_ref[1:2, :] = row_sum(gain_bn)
    kernel_sums(rows, plane, grad_plane, images, sum_ref, 0)


def kernel_sums(rows, plane, grad_plane, images, sum_ref, base):
    zero = jnp.zeros((8, plane.shape[1]), F32)

    def body(row, carry):
        grad = grad_plane[here(padded(row)), :]
        grads = (rows.before(grad), grad, rows.after(grad))
        totals = list(carry)
        for down, source in enumerate(three_rows(plane, row)):
            for across in range(3):
                index = 3 * down + across
                totals[index] = totals[index] + fold_rows(grads[across] * source)
        return tuple(totals)

    totals = loop(0, images * GRID, body, (zero,) * 9)
    for index, total in enumerate(totals):
        sum_ref[base + index : base + index + 1, :] = row_sum(total)


def middle(
    images, extents, stats, stats_two, after_mix, act, up, w1, w2, aff, dhidden, branch_sums,
    later=(),
):
    tokens, width = after_mix.shape
    inner = w1.shape[1]
    full, low, wide = ((tokens, width), F32), ((tokens, width), BF16), ((tokens, inner), BF16)
    outs = [
        low, low, wide, wide, full, full, ((3, width), F32), ((19, width), F32), ((2, width), F32),
    ]
    return call(
        functools.partial(middle_kernel, images), "middle",
        [SMEM] + [VMEM] * (8 + 2 * images), outs,
        [
            pltpu.VMEM((tokens // images, inner), F32),
            pltpu.VMEM((tokens, width), F32), pltpu.VMEM((tokens, width), F32),
            pltpu.VMEM((tokens, 1), F32), pltpu.VMEM((tokens, width), F32),
            plane_of(images, width), plane_of(images, width),
        ], 18,
        (extents, stats, stats_two, after_mix, act, up, w1, w2, aff, *dhidden, *branch_sums), 3e10,
        4e7, later,
    )


def fed_grads_kernel(shift, bit_ref, norm_ref, hidlow_ref, ghid_ref, *refs):
    *gbranch_refs, out_ref = refs
    slots = gbranch_refs[0].shape[0]
    width = norm_ref.shape[1]
    pairs = out_ref.shape[0]
    size = ghid_ref.shape[1] // (2 * pairs)
    low = bit_ref[0] if shift == 0 else 1 - bit_ref[0]
    for pair in range(pairs):
        cols = pl.ds(pl.multiple_of((2 * pair + low) * size, 128), size)
        out_ref[pair, 0:size, :] = mul_tn(ghid_ref[:, cols], norm_ref[...])
        total = None
        for image, gbranch_ref in enumerate(gbranch_refs):
            span = slice(image * slots, (image + 1) * slots)
            part = mul_tn(hidlow_ref[span, cols], gbranch_ref[...])
            total = part if image == 0 else total + part
        out_ref[pair, size : 2 * size, :] = total


def fed_grads(shift, parts, bit, norm, hidlow, ghid, gbranch, later=()):
    width, inner = norm.shape[1], ghid.shape[1]
    return call(
        functools.partial(fed_grads_kernel, shift, bit), "fed_grads", [VMEM] * (3 + len(gbranch)),
        [((parts // 2, 2 * inner // parts, width), F32)], [], 6,
        (norm, hidlow, ghid, *gbranch), 3e9, 1e7, later,
    )[0]


def inner_back_kernel(
    images, extent_ref, total_ref, total_two_ref, batch_ref, act_ref, conv_ref, gbn_ref, glocal_ref, mix_ref,
    branch_ref, aff_ref, gmix_ref, gbranch_ref, sum_ref, bn_ref,
    normal_s, inverse_s, plane, grad_plane,
):
    tokens, width = act_ref.shape
    rows = Rows(extent_ref, width)
    clear_edges(plane, images)
    clear_edges(grad_plane, images)
    zero = jnp.zeros((8, width), F32)
    all_rows = images * GRID

    def aff(row):
        return aff_ref[row : row + 1, :]

    totals = total_ref[...] + total_two_ref[...]
    bn_ref[...] = totals
    centre, inverse_std, tally = batch_ref[0:1, :], batch_ref[1:2, :], batch_ref[2:3, :]
    bias_mean, gain_mean = totals[0:1, :] / tally, totals[1:2, :] / tally
    factor = aff(19) * inverse_std

    def first(row, total):
        at = here(row)
        unit = (act_ref[at, :] - centre) * inverse_std
        value = conv_ref[at, :]
        slope = normal_cdf(value) + value * density(value)
        grad = factor * (gbn_ref[at, :] - (bias_mean + unit * gain_mean)) * slope
        grad = jnp.where(rows.inside(row), grad, 0.0)
        grad_plane[here(padded(row)), :] = grad
        return total + fold_rows(grad)

    sum_ref[13:14, :] = row_sum(loop(0, all_rows, first, zero, unroll=2))

    def second(row, carry):
        at = here(row)
        normal, inverse = norm_rows(mix_ref[at, :])
        normal_s[at, :] = normal
        inverse_s[at, :] = inverse
        plane[here(padded(row)), :] = jnp.where(rows.inside(row), normal * aff(7) + aff(8), 0.0)
        return carry

    loop(0, all_rows, second, 0, unroll=8)
    kernel_sums(rows, plane, grad_plane, images, sum_ref, 4)

    def third(row, carry):
        summed = rows.convolve(grad_plane, row, lambda index: aff(17 - index))
        gmix_ref[here(row), :] = jnp.where(rows.inside(row), summed, 0.0)
        return carry

    loop(0, all_rows, third, 0, unroll=2)

    def fourth(row, carry):
        gain_sum, shift_sum, scale_sum, bias_sum = carry
        at = here(row)
        grad_norm, normal = gmix_ref[at, :], normal_s[at, :]
        grad = glocal_ref[at, :] + norm_back(grad_norm, normal, inverse_s[at, :], aff(7))
        gmix_ref[at, :] = grad
        kept = jnp.where(rows.inside(row), grad, 0.0)
        low = (kept * aff(6)).astype(BF16)
        gbranch_ref[at, :] = low
        return (
            gain_sum + fold_rows(grad_norm * normal), shift_sum + fold_rows(grad_norm),
            scale_sum + fold_rows(kept * branch_ref[at, :]), bias_sum + fold_rows(low.astype(F32)),
        )

    gain_sum, shift_sum, scale_sum, bias_sum = loop(0, all_rows, fourth, (zero,) * 4, unroll=6)
    sum_ref[0:1, :] = row_sum(bias_sum)
    sum_ref[1:2, :] = row_sum(scale_sum)
    sum_ref[2:3, :] = row_sum(gain_sum)
    sum_ref[3:4, :] = row_sum(shift_sum)


def inner_back(
    images, extents, totals, totals_two, batch, act, conv, gbn, glocal, after_mix, branch, aff,
    later=(),
):
    tokens, width = act.shape
    outs = [((tokens, width), F32), ((tokens, width), BF16), ((14, width), F32), ((2, width), F32)]
    return call(
        functools.partial(inner_back_kernel, images), "inner_back",
        [SMEM] + [VMEM] * 10, outs,
        [
            pltpu.VMEM((tokens, width), F32), pltpu.VMEM((tokens, 1), F32),
            plane_of(images, width), plane_of(images, width),
        ], 10,
        (extents, totals, totals_two, batch, act, conv, gbn, glocal, after_mix, branch, aff), 2e10, 3e7,
        later,
    )


def attention_back_kernel(
    image, extent_ref, sharp_ref, query_ref, key_ref, value_ref, inv_ref, cov_ref, attend_ref,
    gbranch_ref, wp_ref, gjoined, head_ref,
    gmixing, gscore, gquery, gkey,
):
    slots, width = gmixing.shape
    heads = sharp_ref.shape[0]
    head = width // heads
    rows = Rows(extent_ref, width)
    zero = jnp.zeros((8, width), F32)
    span = slice(image * slots, (image + 1) * slots)
    low, high = image * GRID, (image + 1) * GRID
    gmixing[...] = mul_nt(gbranch_ref[span, :], wp_ref[...])
    lane = lax.broadcasted_iota(jnp.int32, (1, width), 1)
    sharp_sum = jnp.zeros((1, width), F32)
    gscore[...] = mul_tn(gmixing[...], value_ref[span, :], HIGH)
    for group in range(heads):
        part = slice(group * head, (group + 1) * head)
        attend = attend_ref[image, part, :]
        grad = gscore[part, :]
        grad = attend * (grad - jnp.sum(attend * grad, axis=-1, keepdims=True))
        gscore[part, :] = grad * sharp_ref[group]
        amount = jnp.sum(
            jnp.sum(grad * cov_ref[image, part, :], axis=0, keepdims=True), axis=1, keepdims=True
        )
        sharp_sum = sharp_sum + jnp.where(lane == group, amount, 0.0)
    gquery[...] = mul_nt(key_ref[span, :], gscore[...], HIGH)
    gkey[...] = mul_nn(query_ref[span, :], gscore[...], HIGH)
    gmixing[...] = mul_nn(gmixing[...], attend_ref[image], HIGH)

    def first(row, carry):
        query_dot, key_dot = carry
        at = here(row)
        to = here(row - low)
        return (
            query_dot + fold_rows(gquery[to, :] * query_ref[at, :]),
            key_dot + fold_rows(gkey[to, :] * key_ref[at, :]),
        )

    query_dot, key_dot = loop(low, high, first, (zero, zero), unroll=2)
    query_dot, key_dot = row_sum(query_dot), row_sum(key_dot)
    query_inv = inv_ref[2 * image : 2 * image + 1, :]
    key_inv = inv_ref[2 * image + 1 : 2 * image + 2, :]

    def second(pair, carry):
        totals = list(carry)
        thirds = ([], [], [])
        for row in (2 * pair, 2 * pair + 1):
            at = here(row)
            to = here(row - low)
            inside = rows.inside(row)
            grad = query_inv * (gquery[to, :] - query_ref[at, :] * query_dot)
            thirds[0].append(jnp.where(inside, grad, 0.0))
            grad = key_inv * (gkey[to, :] - key_ref[at, :] * key_dot)
            thirds[1].append(jnp.where(inside, grad, 0.0))
            thirds[2].append(gmixing[to, :])
        to = pl.ds(pl.multiple_of((2 * pair - low) * GRID, 16), 2 * GRID)
        for third in range(3):
            value = jnp.concatenate(thirds[third], axis=0).astype(BF16)
            gjoined[to, third * width : (third + 1) * width] = value
            totals[third] = totals[third] + fold_rows(value.astype(F32))
        return tuple(totals)

    bias = loop(low // 2, high // 2, second, (zero,) * 3)
    put_rows(head_ref, [row_sum(total) for total in bias] + [sharp_sum])


def attention_back(
    images, image, extents, sharpness, query, key, value, inv, cov, attend, gbranch, wp, later=(),
):
    tokens, width = query.shape
    slots = tokens // images
    return call(
        functools.partial(attention_back_kernel, image), "attention_back",
        [SMEM] * 2 + [VMEM] * 8, [((slots, 3 * width), BF16), ((4, width), F32)],
        [
            pltpu.VMEM((slots, width), F32), pltpu.VMEM((width, width), F32),
            pltpu.VMEM((slots, width), F32), pltpu.VMEM((slots, width), F32),
        ], 8,
        (extents, sharpness, query, key, value, inv, cov, attend, gbranch, wp), 2e10, 2e7, later,
    )


def att_grads_kernel(
    bits_ref, norm_ref, mixing_ref, gbranch_ref, *refs
):
    *gjoined_refs, send_ref, keep_ref, matrix = refs
    slots = gjoined_refs[0].shape[0]
    width = norm_ref.shape[1]
    pairs = send_ref.shape[0]
    for image, gjoined_ref in enumerate(gjoined_refs):
        part = mul_tn(gjoined_ref[...], norm_ref[image * slots : (image + 1) * slots, :])
        rows = slice(0, 3 * width)
        matrix[rows, :] = part if image == 0 else matrix[rows, :] + part
    matrix[3 * width :, :] = mul_tn(mixing_ref[...], gbranch_ref[...])
    joined_rows, mixer_rows = 3 * width // (2 * pairs), width // (2 * pairs)
    for pair in range(pairs):
        for target, place in ((keep_ref, bits_ref[0]), (send_ref, 1 - bits_ref[0])):
            part = 2 * pair + place
            at = pl.ds(pl.multiple_of(part * joined_rows, 8), joined_rows)
            target[pair, 0:joined_rows, :] = matrix[at, :]
            at = pl.ds(pl.multiple_of(3 * width + part * mixer_rows, 8), mixer_rows)
            target[pair, joined_rows:, :] = matrix[at, :]


def att_grads(parts, bits, norm, mixing, gbranch, gjoined, later=()):
    width = norm.shape[1]
    share = ((parts // 2, 4 * width // parts, width), F32)
    return call(
        functools.partial(att_grads_kernel, bits), "att_grads", [VMEM] * (3 + len(gjoined)), [share, share],
        [pltpu.VMEM((4 * width, width), F32)], 8,
        (norm, mixing, gbranch, *gjoined), 2e9, 8e6, later,
    )


def outer_back_kernel(
    x_ref, gmix_ref, wq_ref, aff_ref, inner_ref, tail_ref, *refs
):
    *refs, incoming_ref, vector_ref, gnorm = refs
    images = len(refs) // 2
    gjoined_refs, head_refs = refs[:images], refs[images:]
    slots = gjoined_refs[0].shape[0]
    tokens, width = x_ref.shape
    zero = jnp.zeros((8, width), F32)
    for image, gjoined_ref in enumerate(gjoined_refs):
        gnorm[image * slots : (image + 1) * slots, :] = mul_nt(gjoined_ref[...], wq_ref[...])

    def body(step, carry):
        gain_sum, shift_sum = carry
        at = pl.ds(pl.multiple_of(step * 48, 16), 48)
        normal, inverse = norm_rows(x_ref[at, :].astype(F32))
        grad = gnorm[at, :]
        incoming_ref[at, :] = gmix_ref[at, :] + norm_back(grad, normal, inverse, aff_ref[0:1, :])
        return gain_sum + fold_rows(grad * normal), shift_sum + fold_rows(grad)

    gain_sum, shift_sum = loop(0, tokens // 48, body, (zero, zero), unroll=4)
    vector_ref[...] = jnp.zeros_like(vector_ref)
    vector_ref[0:1, :] = row_sum(gain_sum)
    vector_ref[1:2, :] = row_sum(shift_sum)
    head = sum(ref[...] for ref in head_refs[1:]) + head_refs[0][...]
    vector_ref[2:5, :] = head[0:3, :]
    vector_ref[5:19, :] = inner_ref[...]
    vector_ref[21:40, :] = tail_ref[...]
    vector_ref[40:41, :] = head[3:4, :]


def outer_back(source, gmix, wq, aff, inner, tail, gjoined, head, later=()):
    tokens, width = source.shape
    return call(
        outer_back_kernel, "outer_back", [VMEM] * (6 + 2 * len(head)),
        [((tokens, width), F32), ((SUM_ROWS, width), F32)], [pltpu.VMEM((tokens, width), F32)], 6,
        (source, gmix, wq, aff, inner, tail, *gjoined, *head), 5e9, 1e7, later,
    )


def row_blocks(rows):
    step = next(size for size in (32, 24, 16, 8, rows) if rows % size == 0)
    return rows // step, step


def blocks(rows, body):
    count, step = row_blocks(rows)

    def inner(index, carry):
        start = index * step
        body(pl.multiple_of(start, 8) if step % 8 == 0 else start, step)
        return carry

    loop(0, count, inner, 0)


def halve_first_kernel(
    high, side, bits_ref, held_ref, other_ref, send_high_ref, keep_high_ref, send_side_ref,
    keep_side_ref,
):
    half, quarter = send_high_ref.shape[0], send_side_ref.shape[1]
    high_bit, side_bit = bits_ref[high], bits_ref[side]

    def first(start, size):
        at = pl.ds(start, size)
        send_high_ref[at, :] = held_ref[1 - high_bit, at, :] + other_ref[1 - high_bit, at, :]
        keep_high_ref[at, :] = held_ref[high_bit, at, :] + other_ref[high_bit, at, :]

    def second(start, size):
        at = pl.ds(start, size)
        for target, bit in ((send_side_ref, 1 - side_bit), (keep_side_ref, side_bit)):
            here = pl.ds(pl.multiple_of(half + bit * quarter, 8) + start, size)
            for part in range(2):
                target[part, at, :] = held_ref[part, here, :] + other_ref[part, here, :]

    blocks(half, first)
    blocks(quarter, second)


def halve_first(bits, high, side, held, other, later=()):
    rows, width = held.shape[-2:]
    half, quarter = ((rows // 2, width), F32), ((2, rows // 4, width), F32)
    return call(
        functools.partial(halve_first_kernel, high, side, bits), "halve_first", [VMEM, VMEM],
        [half, half, quarter, quarter], [], 2, (held, other), held.size, 16 * held.size,
        later,
    )


def halve_second_kernel(
    high, side, bits_ref, one_ref, one_other_ref, two_ref, two_other_ref,
    send_one_ref, keep_one_ref, send_two_ref, keep_two_ref,
):
    quarter = send_one_ref.shape[0]
    high_bit, side_bit = bits_ref[high], bits_ref[side]

    def body(start, size):
        at = pl.ds(start, size)
        for target, bit in ((send_one_ref, 1 - side_bit), (keep_one_ref, side_bit)):
            here = pl.ds(pl.multiple_of(bit * quarter, 8) + start, size)
            target[at, :] = one_ref[here, :] + one_other_ref[here, :]
        for target, bit in ((send_two_ref, 1 - high_bit), (keep_two_ref, high_bit)):
            target[at, :] = two_ref[bit, at, :] + two_other_ref[bit, at, :]

    blocks(quarter, body)


def halve_second(bits, high, side, one, one_other, two, two_other, later=()):
    quarter = (two.shape[-2:], F32)
    return call(
        functools.partial(halve_second_kernel, high, side, bits), "halve_second", [VMEM] * 4,
         [quarter] * 4, [], 2,
        (one, one_other, two, two_other), one.size, 32 * one.size, later,
    )


def halve_third_kernel(
    place, bits_ref, one_ref, one_other_ref, two_ref, two_other_ref, send_ref, keep_ref
):
    bit = bits_ref[place]
    eighth = one_ref.shape[0] // 2

    def body(start, size):
        for target, half in ((send_ref, 1 - bit), (keep_ref, bit)):
            here = pl.ds(pl.multiple_of(half * eighth, 8) + start, size)
            target[pl.ds(start, size), :] = one_ref[here, :] + one_other_ref[here, :]
            target[pl.ds(eighth + start, size), :] = two_ref[here, :] + two_other_ref[here, :]

    blocks(eighth, body)


def halve_third(bits, place, one, one_other, two, two_other, later=()):
    return call(
        functools.partial(halve_third_kernel, place, bits), "halve_third", [VMEM] * 4,
        [(one.shape, F32)] * 2, [], 2, (one, one_other, two, two_other), one.size,
        32 * one.size, later,
    )


def split_add_kernel(place, bits_ref, held_ref, other_ref, send_ref, keep_ref):
    bit = bits_ref[place]

    def body(start, size):
        at = pl.ds(start, size)
        send_ref[at, :] = held_ref[1 - bit, at, :] + other_ref[1 - bit, at, :]
        keep_ref[at, :] = held_ref[bit, at, :] + other_ref[bit, at, :]

    blocks(send_ref.shape[0], body)


def split_add(bits, place, held, other, later=()):
    half = (held.shape[-2:], F32)
    return call(
        functools.partial(split_add_kernel, place, bits), "split_add", [VMEM, VMEM], [half, half],
        [], 2, (held, other), held.size, 16 * held.size, later,
    )


def add_kernel(held_ref, other_ref, out_ref):
    def body(start, size):
        at = pl.ds(start, size)
        out_ref[at, :] = held_ref[at, :] + other_ref[at, :]

    blocks(held_ref.shape[0], body)


def add(held, other, later=()):
    return call(
        add_kernel, "add_rows", [VMEM, VMEM], [(held.shape, F32)], [], 2, (held, other),
        held.size, 12 * held.size, later,
    )[0]


def append_kernel(held_ref, other_ref, rider_ref, rider_other_ref, out_ref):
    rows = held_ref.shape[0]

    def body(start, size):
        at = pl.ds(start, size)
        out_ref[at, :] = held_ref[at, :] + other_ref[at, :]

    blocks(rows, body)
    out_ref[rows:, :] = rider_ref[...] + rider_other_ref[...]


def append(held, other, rider, rider_other, later=()):
    rows, width = held.shape
    return call(
        append_kernel, "append_rows", [VMEM] * 4, [((rows + rider.shape[0], width), F32)], [], 2,
        (held, other, rider, rider_other), held.size, 12 * held.size, later,
    )[0]


def join_kernel(place, rider, bits_ref, held_ref, other_ref, out_ref):
    bit = bits_ref[place]
    rows = held_ref.shape[0] - rider

    def body(start, size):
        mine = pl.ds(pl.multiple_of(bit * rows, 8) + start, size)
        others = pl.ds(pl.multiple_of((1 - bit) * rows, 8) + start, size)
        out_ref[mine, :] = held_ref[pl.ds(start, size), :]
        out_ref[others, :] = other_ref[pl.ds(start, size), :]

    blocks(rows, body)
    if rider:
        out_ref[2 * rows :, :] = held_ref[rows:, :] + other_ref[rows:, :]


def join(bits, place, rider, held, other, later=()):
    rows, width = held.shape
    return call(
        functools.partial(join_kernel, place, rider, bits), "join_rows", [VMEM, VMEM],
        [((2 * rows - rider, width), F32)], [], 2, (held, other), held.size,
        16 * held.size, later,
    )[0]


def join_last_kernel(place, rider, bits_ref, held_ref, other_ref, out_ref, rider_ref):
    bit = bits_ref[place]
    rows = (held_ref.shape[0] - rider) // 4

    def body(start, size):
        for half in range(2):
            for following in range(2):
                source = pl.ds((2 * following + half) * rows + start, size)
                for side, ref in ((bit, held_ref), (1 - bit, other_ref)):
                    first = pl.multiple_of((4 * half + 2 * side + following) * rows, 8)
                    out_ref[pl.ds(first + start, size), :] = ref[source, :]

    blocks(rows, body)
    if rider:
        rider_ref[...] = held_ref[4 * rows :, :] + other_ref[4 * rows :, :]
    else:
        rider_ref[...] = jnp.zeros_like(rider_ref)


def join_last(bits, place, rider, held, other, later=()):
    rows, width = held.shape
    return call(
        functools.partial(join_last_kernel, place, rider, bits), "join_last", [VMEM, VMEM],
        [((2 * (rows - rider), width), F32), ((max(rider, 8), width), F32)], [], 2,
        (held, other), held.size, 16 * held.size, later,
    )


def upper_blocks(size):
    count = size // 128
    return [(row, column) for row in range(count) for column in range(row, count)]


def block(index):
    return slice(128 * index, 128 * index + 128)


def packed_rows(size, rider):
    return 128 * len(upper_blocks(size)) + rider * (size // 128)


def put_packed(target, source):
    for index, (row, column) in enumerate(upper_blocks(source.shape[0])):
        target[block(index), :] = source[block(row), block(column)]


def halves(source):
    high = source.astype(BF16)
    return high, (source - high.astype(F32)).astype(BF16)


def put_left(left, source):
    high, low = halves(source)
    size = source.shape[1]
    left[:, 0:size], left[:, size : 2 * size], left[:, 2 * size :] = high, high, low


def put_right(right, columns, source):
    high, low = halves(source)
    size = source.shape[0]
    right[0:size, columns], right[size : 2 * size, columns] = high, low
    right[2 * size :, columns] = high


def sweeps_kernel(mine_ref, other_ref, out_ref, now, total, left, right, step):
    size = out_ref.shape[0]
    for index, (row, column) in enumerate(upper_blocks(size)):
        part = mine_ref[block(index), :] + other_ref[block(index), :]
        now[block(row), block(column)] = part
        if row != column:
            now[block(column), block(row)] = part.T
    row = lax.broadcasted_iota(jnp.int32, (size, size), 0)
    diagonal = row == lax.broadcasted_iota(jnp.int32, (size, size), 1)
    trace = jnp.where(diagonal, now[...], 0.0)
    trace = jnp.sum(jnp.sum(trace, axis=0, keepdims=True), axis=1, keepdims=True)
    norm = jnp.sqrt(trace) + frob_eps
    now[...] = now[...] / (norm * norm)
    near, far = slice(0, size), slice(size, 2 * size)
    for sweep_index in range(NS_STEPS):
        last = sweep_index == NS_STEPS - 1
        put_left(left, now[...])
        put_right(right, near, now[...])
        square = mul_nn(left[...], right[:, near])
        step[...] = (
            jnp.where(diagonal, coef_first, 0.0) + coef_second * now[...] + coef_third * square
        )
        put_left(left, step[...])
        if sweep_index == 0:
            total[...] = step[...] / norm
            now[...] = mul_nn(left[...], right[:, near])
        elif last:
            put_right(right, near, total[...])
            out_ref[...] = mul_nn(left[...], right[:, near])
        else:
            put_right(right, far, total[...])
            both = mul_nn(left[...], right[...])
            now[...] = both[:, near]
            total[...] = both[:, far]
        if not last:
            put_right(right, near, now[...])
            now[...] = mul_nn(left[...], right[:, near])


def sweeps(width, mine, other, later=()):
    square = pltpu.VMEM((width, width), F32)
    return call(
        sweeps_kernel, "sweeps", [VMEM, VMEM], [((width, width), F32)],
        [
            square, square, pltpu.VMEM((width, 3 * width), BF16),
            pltpu.VMEM((3 * width, 2 * width), BF16), square,
        ], 9, (mine, other), 1e10, 4e6, later,
    )[0]


def prepare_kernel(
    turned, rider, bit_ref, share_ref, first_ref, second_ref, rider_ref,
    grad_one_ref, grad_two_ref, state_one_ref, state_two_ref, send_ref, keep_ref,
):
    split = first_ref.shape[0 if turned else 1]
    tall = second_ref.shape[0]
    grad_one = share_ref[0:split, :]
    grad_one_ref[...] = grad_one if turned else grad_one.T
    state_one_ref[...] = velocity_damping * first_ref[...] + grad_one_ref[...]
    grad_two_ref[...] = share_ref[split : split + tall, :]
    state_two_ref[...] = velocity_damping * second_ref[...] + grad_two_ref[...]
    gram = mul_tn if turned else mul_nt
    gram_one = gram(state_one_ref[...], state_one_ref[...], HIGH)
    gram_two = mul_tn(state_two_ref[...], state_two_ref[...], HIGH)
    even = bit_ref[0] == 0
    width = share_ref.shape[1]
    put_packed(keep_ref, jnp.where(even, gram_one, gram_two))
    put_packed(send_ref, jnp.where(even, gram_two, gram_one))
    if rider:
        for column in range(width // 128):
            first = packed_rows(width, 0) + column * rider
            keep_ref[first : first + rider, :] = rider_ref[:, block(column)]
            send_ref[first : first + rider, :] = rider_ref[:, block(column)]


def prepare(turned, rider, bit, share, first, second, rows, later=()):
    width = share.shape[1]
    upper = ((packed_rows(width, rider), 128), F32)
    one, two = (first.shape, F32), (second.shape, F32)
    return call(
        functools.partial(prepare_kernel, turned, rider, bit), "prepare", [VMEM] * 4,
        [one, two, one, two, upper, upper], [], 8, (share, first, second, rows), 2e9, 6e6, later,
    )


def renew_kernel(
    turned, factors, bit_ref, mine_ref, other_ref, state_one_ref, state_two_ref, one_ref, two_ref,
    new_one_ref, new_two_ref, low_one_ref, low_two_ref,
):
    even = bit_ref[0] == 0
    poly_one = jnp.where(even, mine_ref[...], other_ref[...])
    poly_two = jnp.where(even, other_ref[...], mine_ref[...])
    if turned:
        field_one = mul_nn(state_one_ref[...], poly_one, HIGH)
    else:
        field_one = mul_nn(poly_one, state_one_ref[...], HIGH)
    new_one = one_ref[...] - (rate_matrix * factors[0]) * field_one
    new_one_ref[...] = new_one
    low_one_ref[...] = new_one.astype(BF16)
    new_two = two_ref[...] - (rate_matrix * factors[1]) * mul_nn(
        state_two_ref[...], poly_two, HIGH
    )
    new_two_ref[...] = new_two
    low_two_ref[...] = new_two.astype(BF16)


def renew(
    turned, factors, bit, mine, other, state_one, state_two, one, two, later=(),
):
    outs = [(one.shape, F32), (two.shape, F32), (one.shape, BF16), (two.shape, BF16)]
    return call(
        functools.partial(renew_kernel, turned, factors, bit), "renew", [VMEM] * 6, outs, [],
        8, (mine, other, state_one, state_two, one, two), 2e9, 6e6, later,
    )


def vectors_kernel(
    start, rider, held_ref, other_ref, bn_ref, batch_ref, aff_ref, aff_velocity_ref, sharp_ref,
    sharp_velocity_ref, full_ref, sharp_sum_ref, new_aff_ref, aff_state_ref, new_sharp_ref,
    sharp_state_ref,
):
    rows, width = aff_ref.shape
    group = sharp_ref.shape[1]
    for column in range(width // 128):
        first = start + column * rider
        total = held_ref[first : first + rider, :] + other_ref[first : first + rider, :]
        full_ref[:, block(column)] = total[0:rows, :]
        if column == 0:
            sharp_sum_ref[...] = total[rows : rows + 1, 0:group]
    full_ref[rows // 2 - 1 : rows // 2, :] = bn_ref[1:2, :]
    full_ref[rows // 2 : rows // 2 + 1, :] = bn_ref[0:1, :]
    step_size = affine_step_size * lax.rsqrt(batch_ref[2:3, :])
    state = velocity_damping * aff_velocity_ref[...] + full_ref[...]
    aff_state_ref[...] = state
    new_aff_ref[...] = aff_ref[...] - step_size * state
    state = velocity_damping * sharp_velocity_ref[...] + sharp_sum_ref[...]
    sharp_state_ref[...] = state
    new_sharp_ref[...] = sharp_ref[...] - step_size[:, 0:group] * state


def vectors(
    width, rider, held, other, bn_totals, batch, aff, aff_velocity, sharp, sharp_velocity,
    later=(),
):
    start = packed_rows(width, 0)
    sharp, sharp_velocity = sharp[None], sharp_velocity[None]
    large, small = (aff.shape, F32), (sharp.shape, F32)
    return call(
        functools.partial(vectors_kernel, start, rider), "vectors", [VMEM] * 8,
        [large, small, large, large, small, small], [], 2,
        (held, other, bn_totals, batch, aff, aff_velocity, sharp, sharp_velocity), 0, 0, later,
    )


def bits_of(size):
    return [1 << place for place in range(size.bit_length() - 1)]


def swap(source, axis, bit):
    size = lax.axis_size(axis)
    return lax.ppermute(source, axis, [(member, member ^ bit) for member in range(size)])


def axis_steps(axis):
    base = 0 if axis == "narrow" else len(bits_of(lax.axis_size("narrow")))
    return [(axis, bit, base + place) for place, bit in enumerate(bits_of(lax.axis_size(axis)))]


def all_steps():
    return axis_steps("narrow") + axis_steps("wide")


class OwnBits:
    def __init__(self):
        self.steps = all_steps()

    def __getitem__(self, place):
        axis, bit, _ = self.steps[place]
        return lax.rem(lax.div(lax.axis_index(axis), bit), 2)


class Line:
    def __init__(self):
        self.last = ()

    def __call__(self, kernel, *args):
        out = kernel(*args, later=self.last)
        self.last = (out[-1] if isinstance(out, (list, tuple)) else out,)
        return out


def everyone(line, rows, combine, fillers=()):
    fillers = list(fillers)
    steps = all_steps()
    for axis, bit, _ in steps[:-1]:
        other = swap(rows, axis, bit)
        if axis != "narrow" or bit > 1:
            if fillers:
                fillers.pop(0)()
        rows = line(combine, rows, other)
    axis, bit, _ = steps[-1]
    other = swap(rows, axis, bit)
    for filler in fillers:
        filler()
    return rows, other


class Sum:
    def __init__(self, line, bits, send, keep):
        self.line, self.bits, self.keep = line, bits, keep
        (_, self.low, _), (_, self.high, self.high_place) = axis_steps("narrow")
        _, self.side, self.side_place = axis_steps("wide")[0]
        self.rest = axis_steps("wide")[1:]
        self.other = swap(send, "narrow", self.low)
        self.rider = 0

    def first(self):
        send, self.one, send_two, self.two = self.line(
            halve_first, self.bits, self.high_place, self.side_place, self.keep, self.other
        )
        self.one_other = swap(send, "narrow", self.high)
        self.two_other = swap(send_two, "wide", self.side)

    def second(self):
        send, self.one, send_two, self.two = self.line(
            halve_second, self.bits, self.high_place, self.side_place, self.one, self.one_other,
            self.two, self.two_other,
        )
        self.one_other = swap(send, "wide", self.side)
        self.two_other = swap(send_two, "narrow", self.high)

    def third(self):
        axis, bit, place = self.rest[0]
        send, self.keep = self.line(
            halve_third, self.bits, place, self.one, self.one_other, self.two, self.two_other
        )
        self.other = swap(send, axis, bit)
        self.done = 1

    def more(self):
        axis, bit, place = self.rest[self.done]
        shape = self.keep.shape
        self.done += 1
        if self.done < len(self.rest):
            keep, other = (array.reshape(2, -1, shape[1]) for array in (self.keep, self.other))
            send, self.keep = self.line(split_add, self.bits, place, keep, other)
            self.other = swap(send, axis, bit)
        else:
            self.keep = self.line(add, self.keep, self.other)
            self.other = swap(self.keep, axis, bit)

    def mores(self):
        while self.done < len(self.rest):
            self.more()

    def last_step(self):
        axis, bit, _ = self.rest[-1]
        return axis, bit

    def turn(self, rider=None):
        if rider is None:
            self.held = self.line(add, self.keep, self.other)
        else:
            self.held = self.line(append, self.keep, self.other, *rider)
            self.rider = rider[0].shape[0]
        self.place = len(self.rest) - 1
        self.back_move()

    def back_move(self):
        self.place -= 1
        axis, bit, _ = self.rest[self.place] if self.place >= 0 else axis_steps("wide")[0]
        self.other = swap(self.held, axis, bit)

    def back(self):
        _, _, place = self.rest[self.place]
        self.held = self.line(join, self.bits, place, self.rider, self.held, self.other)
        self.back_move()

    def backs(self):
        while self.place >= 0:
            self.back()

    def last(self):
        return self.line(
            join_last, self.bits, self.side_place, self.rider, self.held, self.other
        )


class Update:
    def __init__(self, line, turned, bits, gathered, states, rider=0):
        share, rows = gathered
        self.line, self.turned, self.bits = line, turned, bits
        self.width = share.shape[1]
        *self.grads, self.one, self.two, send, self.keep = line(
            prepare, turned, rider, bits, share, *states, rows
        )
        self.other = swap(send, "narrow", 1)

    def across(self):
        (axis, bit, _) = axis_steps("narrow")[1]
        self.keep = self.line(add, self.keep, self.other)
        self.other = swap(self.keep, axis, bit)
        self.sums = (self.keep, self.other)

    def sweep(self):
        self.keep = self.line(sweeps, self.width, self.keep, self.other)
        self.other = swap(self.keep, "narrow", 1)

    def renew(self, factors, masters):
        new = self.line(
            renew, self.turned, factors, self.bits, self.keep, self.other, self.one, self.two,
            *masters,
        )
        return self.grads + [self.one, self.two] + list(new)


def on_device(
    block_source,
    upstream_adjoint,
    picture_patch_extents,
    triple_matrix,
    mixer_matrix,
    expand_matrix,
    shrink_matrix,
    affine_entries,
    sharpness,
    triple_velocity,
    mixer_velocity,
    expand_velocity,
    shrink_velocity,
    affine_velocity,
    sharpness_velocity,
):
    images, slot_count, model_width = block_source.shape
    group_index = sharpness.shape[0]
    narrow_parts = lax.axis_size("narrow")
    narrow_pos = lax.axis_index("narrow")
    bits = OwnBits()
    source = block_source.reshape(-1, model_width)
    above = upstream_adjoint.reshape(-1, model_width)

    def own_part(full_matrix, along):
        part_size = full_matrix.shape[along] // narrow_parts
        return lax.dynamic_slice_in_dim(full_matrix, narrow_pos * part_size, part_size, along)

    (
        norm_one, query, key, value, inv, cov, attend, mixing, branch, after_mix, conv_one, act,
        stats,
    ) = front(
        images, picture_patch_extents, sharpness, source, triple_matrix, mixer_matrix,
        affine_entries,
    )
    line = Line()
    low_weights, backs = [], []

    def lower(matrix):
        low_weights.append(line(cast, matrix))

    def from_above():
        backs.append(
            line(
                upstream, images, len(backs), picture_patch_extents, above, low_weights[0],
                affine_entries,
            )
        )

    stats, stats_two = everyone(
        line, stats, merge,
        (lambda: lower(shrink_matrix), lambda: lower(expand_matrix))
        + (from_above,) * images,
    )
    shrink_low, expand_low = low_weights
    grad_branch3, grad_above, branch_sums = zip(*backs)
    (
        block_out, norm_three, hidden_low, grad_hidden, grad_local, grad_bn, batch, tail_sums,
        bn_sums,
    ) = line(
        middle, images, picture_patch_extents, stats, stats_two, after_mix, act, above,
        expand_low, shrink_low, affine_entries, grad_above, branch_sums,
    )
    fed_halves = []

    def fed_half():
        fed_halves.append(
            line(
                fed_grads, 1 - len(fed_halves), narrow_parts, bits, norm_three, hidden_low,
                grad_hidden, grad_branch3,
            )
        )

    bn_sums, bn_two = everyone(line, bn_sums, add, (fed_half, fed_half))
    fed = Sum(line, bits, *fed_halves)
    fed.first()
    grad_mix, grad_branch1, inner_sums, bn_totals = line(
        inner_back, images, picture_patch_extents, bn_sums, bn_two, batch, act, conv_one, grad_bn,
        grad_local, after_mix, branch, affine_entries,
    )
    fed.second()
    mixer_low = mixer_matrix.astype(BF16)
    backs = []
    for image in range(images):
        backs.append(
            line(
                attention_back, images, image, picture_patch_extents, sharpness, query, key,
                value, inv, cov, attend, grad_branch1, mixer_low,
            )
        )
        if image == 0:
            fed.third()
    grad_joined, head_sums = zip(*backs)
    fed.mores()
    att_send, att_keep = line(
        att_grads, narrow_parts, bits, norm_one, mixing, grad_branch1, grad_joined
    )
    att = Sum(line, bits, att_send, att_keep)
    incoming_adjoint, vector_sums = line(
        outer_back, source, grad_mix, triple_matrix.astype(BF16), affine_entries, inner_sums,
        tail_sums, grad_joined, head_sums,
    )
    rider = (vector_sums, swap(vector_sums, *fed.last_step()))
    full_weights = (triple_matrix, mixer_matrix, expand_matrix, shrink_matrix)
    factors = [math.sqrt(max(1.0, full.shape[0] / full.shape[1])) for full in full_weights]
    masters = (
        own_part(triple_matrix, 1).T, own_part(mixer_matrix, 0), own_part(expand_matrix, 1),
        own_part(shrink_matrix, 0),
    )
    att.first()
    fed.turn(rider)
    att.second()
    att.third()
    fed.backs()
    att.mores()
    att.turn()
    att.backs()
    fed = Update(line, False, bits, fed.last(), (expand_velocity, shrink_velocity), SUM_ROWS)
    att = Update(line, True, bits, att.last(), (triple_velocity.T, mixer_velocity))
    fed.across()
    att.across()
    fed.sweep()
    line.last += masters
    att.sweep()
    vector_outs = line(
        vectors, model_width, SUM_ROWS, *fed.sums, bn_totals, batch, affine_entries,
        affine_velocity, sharpness, sharpness_velocity,
    )
    fed = fed.renew(factors[2:], masters[2:])
    att = att.renew(factors[:2], masters[:2])
    vec_full, sharpness_sum, new_vec, vec_state, sharpness_following, sharpness_buffer = (
        vector_outs
    )
    sharpness_sum, sharpness_following, sharpness_buffer = (
        row.reshape(-1) for row in (sharpness_sum, sharpness_following, sharpness_buffer)
    )
    for member in (0, 2, 4, 6):
        att[member] = att[member].T
    return (
        block_out.reshape(block_source.shape),
        incoming_adjoint.reshape(block_source.shape),
        att[0],
        att[1],
        fed[0],
        fed[1],
        vec_full,
        sharpness_sum,
        att[4],
        att[5],
        fed[4],
        fed[5],
        att[2],
        att[3],
        fed[2],
        fed[3],
        att[6],
        att[7],
        fed[6],
        fed[7],
        new_vec,
        vec_state,
        sharpness_following,
        sharpness_buffer,
    )


def solution(mesh):
    return jax.shard_map(
        on_device,
        mesh=mesh,
        in_specs=(
            P(("wide", "narrow"), None, None),
            P(("wide", "narrow"), None, None),
            P(("wide", "narrow"), None),
            P(),
            P(),
            P(),
            P(),
            P(),
            P(),
            P(None, "narrow"),
            P("narrow", None),
            P(None, "narrow"),
            P("narrow", None),
            P(),
            P(),
        ),
        out_specs=(
            P(("wide", "narrow"), None, None),
            P(("wide", "narrow"), None, None),
            P(None, "narrow"),
            P("narrow", None),
            P(None, "narrow"),
            P("narrow", None),
            P(),
            P(),
            P(None, "narrow"),
            P("narrow", None),
            P(None, "narrow"),
            P("narrow", None),
            P(None, "narrow"),
            P("narrow", None),
            P(None, "narrow"),
            P("narrow", None),
            P(None, "narrow"),
            P("narrow", None),
            P(None, "narrow"),
            P("narrow", None),
            P(),
            P(),
            P(),
            P(),
        ),
        check_vma=False,
    )
```

```python
import functools
import math

import jax
import jax.numpy as jnp
from jax import lax
from jax.experimental import pallas as pl
from jax.experimental.pallas import tpu as pltpu
from jax.sharding import PartitionSpec as P

GRID = 24
NS_STEPS = 5
SUM_ROWS = 48

layer_eps = 1e-06
unit_eps = 1e-06
batch_eps = 1e-05
frob_eps = 1e-07
velocity_damping = 0.5
rate_matrix = 0.25
affine_step_size = 0.2
coef_first = 3.4445
coef_second = -4.775
coef_third = 2.0315
root_half = 0.7071067811865476
inverse_root_tau = 0.3989422804014327
HIGH = lax.Precision.HIGH
F32 = jnp.float32
BF16 = jnp.bfloat16


def mul_nn(left, right, precision=None):
    return lax.dot_general(
        left, right, (((1,), (0,)), ((), ())), precision=precision, preferred_element_type=F32
    )


def mul_nt(left, right, precision=None):
    return lax.dot_general(
        left, right, (((1,), (1,)), ((), ())), precision=precision, preferred_element_type=F32
    )


def mul_tn(left, right, precision=None):
    return lax.dot_general(
        left, right, (((0,), (0,)), ((), ())), precision=precision, preferred_element_type=F32
    )


def fold_rows(source):
    total = source[0:8]
    for start in range(8, source.shape[0], 8):
        total = total + source[start : start + 8]
    return total


def row_sum(total):
    return jnp.sum(total, axis=0, keepdims=True)


def norm_rows(source):
    centre = source - jnp.mean(source, axis=-1, keepdims=True)
    inverse = lax.rsqrt(jnp.mean(centre * centre, axis=-1, keepdims=True) + layer_eps)
    return centre * inverse, inverse


def norm_back(grad_norm, normal, inverse, gain):
    scaled = grad_norm * gain
    return inverse * (
        scaled
        - jnp.mean(scaled, axis=-1, keepdims=True)
        - normal * jnp.mean(scaled * normal, axis=-1, keepdims=True)
    )


def normal_cdf(source):
    return 0.5 * (1.0 + lax.erf(source * root_half))


def density(source):
    return jnp.exp(-0.5 * source * source) * inverse_root_tau


def loop(start, stop, body, carry, unroll=1):
    return lax.fori_loop(start, stop, body, carry, unroll=unroll)


def here(row):
    return pl.ds(pl.multiple_of(row * GRID, 8), GRID)


class Rows:
    def __init__(self, extent_ref, width):
        self.extent_ref = extent_ref
        self.column = lax.broadcasted_iota(jnp.int32, (GRID, width), 0)

    def inside(self, row):
        image = row // GRID
        limit = jnp.where(
            row - image * GRID < self.extent_ref[image, 0], self.extent_ref[image, 1], 0
        )
        return self.column < limit

    def after(self, value):
        return jnp.where(self.column == 0, 0.0, pltpu.roll(value, 1, 0))

    def before(self, value):
        return jnp.where(self.column == GRID - 1, 0.0, pltpu.roll(value, GRID - 1, 0))

    def convolve(self, plane, row, tap):
        columns = [None] * 3
        for down, source in enumerate(three_rows(plane, row)):
            for across in range(3):
                term = source * tap(3 * down + across)
                columns[across] = term if down == 0 else columns[across] + term
        return columns[1] + self.after(columns[0]) + self.before(columns[2])


def padded(row):
    return row + 2 * (row // GRID) + 1


def three_rows(plane, row):
    first = padded(row) - 1
    for down in range(3):
        yield plane[here(first + down), :]


def clear_edges(plane, images):
    edge = jnp.zeros((GRID, plane.shape[1]), F32)
    for image in range(images):
        base = image * (GRID + 2) * GRID
        plane[base : base + GRID, :] = edge
        plane[base + (GRID + 1) * GRID : base + (GRID + 2) * GRID, :] = edge


def plane_of(images, width):
    return pltpu.VMEM((images * (GRID + 2) * GRID, width), F32)


VMEM = pl.BlockSpec(memory_space=pltpu.VMEM)
SMEM = pl.BlockSpec(memory_space=pltpu.SMEM)


ANY = pl.BlockSpec(memory_space=pl.ANY)
FAR = pl.BlockSpec(memory_space=pltpu.HBM)
COST_UNIT = 3e9
KERNEL_COST = {
    "front": 15.0, "middle": 27.0, "fed_grads": 2.7, "inner_back": 13.0, "attention_back": 5.5,
    "att_grads": 3.0, "outer_back": 5.0, "sweeps": 9.5, "prepare": 6.0, "renew": 2.5,
}


def call(kernel, name, spaces, outs, scratch, limit, args, flops=0, size=0, later=()):
    del flops, size
    cost = KERNEL_COST.get(name, 1.0)
    inputs, extra = len(args), len(later)

    def body(*refs):
        kernel(*refs[:inputs], *refs[inputs + extra :])

    return pl.pallas_call(
        body,
        in_specs=list(spaces) + [ANY] * extra,
        out_specs=[VMEM] * len(outs),
        out_shape=[jax.ShapeDtypeStruct(shape, dtype) for shape, dtype in outs],
        scratch_shapes=scratch,
        compiler_params=pltpu.CompilerParams(vmem_limit_bytes=limit << 20),
        cost_estimate=pl.CostEstimate(
            flops=int(cost * COST_UNIT), bytes_accessed=1024, transcendentals=0
        ),
        name=name,
    )(*args, *later)


def merge_stats(one, two):
    shift = one[0] / one[2] - two[0] / two[2]
    count = one[2] + two[2]
    spread = one[1] + two[1] + shift * shift * (one[2] * two[2] / count)
    return one[0] + two[0], spread, count


def get_rows(ref):
    return [ref[row : row + 1, :] for row in range(ref.shape[0])]


def put_rows(ref, values):
    for row, value in enumerate(values):
        ref[row : row + 1, :] = value


def merge_kernel(held_ref, other_ref, out_ref):
    put_rows(out_ref, merge_stats(get_rows(held_ref), get_rows(other_ref)))


def merge(held, other, later=()):
    return call(
        merge_kernel, "merge_rows", [VMEM, VMEM], [(held.shape, F32)], [], 1, (held, other), 1e4,
        1e4, later,
    )[0]


def front_kernel(
    images, extent_ref, sharp_ref, x_far, wq_far, wp_far, aff_far,
    norm_ref, query_ref, key_ref, value_ref, inv_ref, cov_ref, attend_ref, mixing_ref,
    branch_ref, mix_ref, conv_ref, act_ref, stat_ref,
    joined, plane, x_ref, wq_ref, wp_ref, aff_ref, arrived,
):
    copies = [
        pltpu.make_async_copy(far, near, arrived.at[index])
        for index, (far, near) in enumerate(
            ((x_far, x_ref), (aff_far, aff_ref), (wq_far, wq_ref), (wp_far, wp_ref))
        )
    ]
    for copy in copies:
        copy.start()
    tokens, width = x_ref.shape
    slots = tokens // images
    heads = sharp_ref.shape[0]
    head = width // heads
    rows = Rows(extent_ref, width)
    clear_edges(plane, images)
    zero = jnp.zeros((8, width), F32)

    def aff(row):
        return aff_ref[row : row + 1, :]

    def first(step, carry):
        place = pl.ds(pl.multiple_of(step * 48, 16), 48)
        value = x_ref[place, :].astype(F32)
        mix_ref[place, :] = value
        normal, _ = norm_rows(value)
        norm_ref[place, :] = (normal * aff(0) + aff(1)).astype(BF16)
        return carry

    copies[0].wait()
    copies[1].wait()
    loop(0, tokens // 48, first, 0, unroll=8)
    copies[2].wait()
    joined[...] = mul_nn(norm_ref[...], wq_ref[...].astype(BF16))

    def second(row, carry):
        query_sum, key_sum = carry
        at = here(row)
        inside = rows.inside(row)
        query = jnp.where(inside, joined[at, :width] + aff(2), 0.0)
        key = jnp.where(inside, joined[at, width : 2 * width] + aff(3), 0.0)
        query_ref[at, :] = query
        key_ref[at, :] = key
        value_ref[at, :] = joined[at, 2 * width :] + aff(4)
        return query_sum + fold_rows(query * query), key_sum + fold_rows(key * key)

    for image in range(images):
        span = slice(image * slots, (image + 1) * slots)
        low, high = image * GRID, (image + 1) * GRID
        query_sum, key_sum = loop(low, high, second, (zero, zero), unroll=2)
        query_inv = lax.rsqrt(row_sum(query_sum) + unit_eps)
        key_inv = lax.rsqrt(row_sum(key_sum) + unit_eps)
        inv_ref[2 * image : 2 * image + 1, :] = query_inv
        inv_ref[2 * image + 1 : 2 * image + 2, :] = key_inv

        def third(row, carry):
            at = here(row)
            query_ref[at, :] = query_ref[at, :] * query_inv
            key_ref[at, :] = key_ref[at, :] * key_inv
            return carry

        loop(low, high, third, 0, unroll=2)
        cov_ref[image] = mul_tn(query_ref[span, :], key_ref[span, :], HIGH)
        lane = lax.broadcasted_iota(jnp.int32, (head, width), 1)
        for group in range(heads):
            part = slice(group * head, (group + 1) * head)
            own = (lane >= group * head) & (lane < (group + 1) * head)
            scores = jnp.where(own, cov_ref[image, part, :] * sharp_ref[group], -jnp.inf)
            raised = jnp.exp(scores - jnp.max(scores, axis=-1, keepdims=True))
            attend_ref[image, part, :] = raised / jnp.sum(raised, axis=-1, keepdims=True)
        mixing_ref[span, :] = mul_nt(value_ref[span, :], attend_ref[image], HIGH).astype(BF16)
    copies[3].wait()
    branch_ref[...] = mul_nn(mixing_ref[...], wp_ref[...].astype(BF16))

    def fourth(row, carry):
        at = here(row)
        inside = rows.inside(row)
        branch = branch_ref[at, :] + aff(5)
        branch_ref[at, :] = branch
        after = mix_ref[at, :] + jnp.where(inside, aff(6) * branch, 0.0)
        mix_ref[at, :] = after
        normal, _ = norm_rows(after)
        plane[here(padded(row)), :] = jnp.where(inside, normal * aff(7) + aff(8), 0.0)
        return carry

    loop(0, images * GRID, fourth, 0, unroll=8)

    def fifth(row, total):
        at = here(row)
        summed = rows.convolve(plane, row, lambda index: aff(9 + index)) + aff(18)
        conv_ref[at, :] = summed
        active = summed * normal_cdf(summed)
        act_ref[at, :] = active
        return total + fold_rows(jnp.where(rows.inside(row), active, 0.0))

    for image in range(images):
        low, high = image * GRID, (image + 1) * GRID
        act_sum = row_sum(loop(low, high, fifth, zero, unroll=4))
        count = (extent_ref[image, 0] * extent_ref[image, 1]).astype(F32)
        centre = act_sum / count

        def sixth(row, total):
            shifted = jnp.where(rows.inside(row), act_ref[here(row), :] - centre, 0.0)
            return total + fold_rows(shifted * shifted)

        spread = row_sum(loop(low, high, sixth, zero, unroll=4))
        own = (act_sum, spread, jnp.full_like(centre, count))
        stats = own if image == 0 else merge_stats(stats, own)
    put_rows(stat_ref, stats)


def front(images, extents, sharpness, source, wq, wp, aff, later=()):
    tokens, width = source.shape
    full, low, square = ((tokens, width), F32), ((tokens, width), BF16), ((images, width, width), F32)
    far = (extents, sharpness, source, wq, wp, aff)
    outs = [
        low, full, full, full, ((2 * images, width), F32), square, square, low,
        full, full, full, full, ((3, width), F32),
    ]
    return call(
        functools.partial(front_kernel, images), "front",
        [SMEM, SMEM, FAR, FAR, FAR, FAR], outs,
        [
            pltpu.VMEM((tokens, 3 * width), F32), plane_of(images, width),
            pltpu.VMEM(source.shape, source.dtype), pltpu.VMEM(wq.shape, F32),
            pltpu.VMEM(wp.shape, F32), pltpu.VMEM(aff.shape, F32), pltpu.SemaphoreType.DMA((4,)),
        ], 16,
        [pltpu.with_memory_space_constraint(array, pltpu.HBM) for array in far], 2e10, 3e7, later,
    )


def cast_kernel(source_ref, out_ref):
    out_ref[...] = source_ref[...].astype(BF16)


def cast(source, later=()):
    return call(
        cast_kernel, "cast", [VMEM], [(source.shape, BF16)], [], 2, (source,), later=later
    )[0]


def upstream_kernel(image, extent_ref, up_ref, w2_ref, aff_ref, gbranch_ref, dhidden_ref, sum_ref):
    slots, width = gbranch_ref.shape
    rows = Rows(extent_ref, width)
    low, high = image * GRID, (image + 1) * GRID

    def body(pair, total):
        grads = []
        for row in (2 * pair, 2 * pair + 1):
            value = up_ref[here(row), :].astype(F32) * aff_ref[39:40, :]
            grads.append(jnp.where(rows.inside(row), value, 0.0))
        grad = jnp.concatenate(grads, axis=0).astype(BF16)
        gbranch_ref[pl.ds(pl.multiple_of((2 * pair - low) * GRID, 16), 2 * GRID), :] = grad
        return total + fold_rows(grad.astype(F32))

    sum_ref[...] = loop(low // 2, high // 2, body, jnp.zeros((8, width), F32), unroll=2)
    dhidden_ref[...] = mul_nt(gbranch_ref[...], w2_ref[...])


def upstream(images, image, extents, up, w2, aff, later=()):
    tokens, width = up.shape
    slots, inner = tokens // images, w2.shape[0]
    return call(
        functools.partial(upstream_kernel, image), "upstream", [SMEM] + [VMEM] * 3,
        [((slots, width), BF16), ((slots, inner), F32), ((8, width), F32)], [], 2,
        (extents, up, w2, aff), later=later,
    )


def middle_kernel(
    images, extent_ref, stat_ref, stat_two_ref, mix_ref, act_ref, up_ref, w1_ref, w2_ref, aff_ref,
    *refs
):
    dhidden_refs, branch_sum_refs, refs = refs[:images], refs[images : 2 * images], refs[2 * images :]
    (
        out_ref, norm_ref, hidlow_ref, ghid_ref, glocal_ref, gbn_ref, batch_ref, sum_ref, bn_ref,
        hidden, conv_s, normal_s, inverse_s, branch_s, plane, grad_plane,
    ) = refs
    tokens, width = mix_ref.shape
    inner = w1_ref.shape[1]
    rows = Rows(extent_ref, width)
    clear_edges(plane, images)
    clear_edges(grad_plane, images)
    zero = jnp.zeros((8, width), F32)
    all_rows = images * GRID

    def aff(row):
        return aff_ref[row : row + 1, :]

    act_sum, spread, tally = merge_stats(get_rows(stat_ref), get_rows(stat_two_ref))
    centre = act_sum / tally
    inverse_std = lax.rsqrt(spread / tally + batch_eps)
    batch_ref[0:1, :] = centre
    batch_ref[1:2, :] = inverse_std
    batch_ref[2:3, :] = tally

    def first(row, carry):
        inside = rows.inside(row)
        unit = (act_ref[here(row), :] - centre) * inverse_std
        plane[here(padded(row)), :] = jnp.where(inside, unit * aff(19) + aff(20), 0.0)
        return carry

    loop(0, all_rows, first, 0, unroll=2)

    def second(row, carry):
        at = here(row)
        inside = rows.inside(row)
        summed = rows.convolve(plane, row, lambda index: aff(21 + index)) + aff(30)
        conv_s[at, :] = summed
        after = mix_ref[at, :] + jnp.where(inside, aff(31) * summed, 0.0)
        branch_s[at, :] = after
        return carry

    loop(0, all_rows, second, 0, unroll=2)

    def second_norm(step, carry):
        at = pl.ds(pl.multiple_of(step * 48, 16), 48)
        normal, inverse = norm_rows(branch_s[at, :])
        normal_s[at, :] = normal
        inverse_s[at, :] = inverse
        norm_ref[at, :] = (normal * aff(32) + aff(33)).astype(BF16)
        return carry

    loop(0, tokens // 48, second_norm, 0, unroll=4)

    sum_ref[17:18, :] = row_sum(sum(ref[...] for ref in branch_sum_refs))
    slots = tokens // images
    quarters = inner // width
    bias_sums = [zero] * quarters
    for image in range(images):
        span = slice(image * slots, (image + 1) * slots)
        hidden[...] = mul_nn(norm_ref[span, :], w1_ref[...])
        dhidden = dhidden_refs[image]
        for quarter in range(quarters):
            cols = slice(quarter * width, (quarter + 1) * width)
            bias = aff(34 + quarter)

            def fourth(step, total):
                at = pl.ds(pl.multiple_of(step * 16, 16), 16)
                to = pl.ds(pl.multiple_of(image * slots + step * 16, 16), 16)
                value = hidden[at, cols] + bias
                cdf = normal_cdf(value)
                hidlow_ref[to, cols] = (value * cdf).astype(BF16)
                grad = (dhidden[at, cols] * (cdf + value * density(value))).astype(BF16)
                ghid_ref[to, cols] = grad
                return total + fold_rows(grad.astype(F32))

            bias_sums[quarter] = loop(0, slots // 16, fourth, bias_sums[quarter], unroll=4)
        gbn_ref[span, :] = mul_nt(ghid_ref[span, :], w1_ref[...])
        glocal_ref[span, :] = mul_nn(hidlow_ref[span, :], w2_ref[...])
    for quarter in range(quarters):
        sum_ref[13 + quarter : 14 + quarter, :] = row_sum(bias_sums[quarter])

    def fifth(row, total):
        at = here(row)
        inside = rows.inside(row)
        branch = jnp.where(inside, glocal_ref[at, :] + aff(38), 0.0)
        out_ref[at, :] = (branch_s[at, :] + aff(39) * branch).astype(BF16)
        return total + fold_rows(up_ref[at, :].astype(F32) * branch)

    sum_ref[18:19, :] = row_sum(loop(0, all_rows, fifth, zero, unroll=2))

    def sixth(row, carry):
        gain_sum, shift_sum, scale_sum, bias_sum = carry
        at = here(row)
        inside = rows.inside(row)
        grad_norm = gbn_ref[at, :]
        normal = normal_s[at, :]
        grad = up_ref[at, :].astype(F32) + norm_back(grad_norm, normal, inverse_s[at, :], aff(32))
        glocal_ref[at, :] = grad
        kept = jnp.where(inside, grad, 0.0)
        scaled = kept * aff(31)
        grad_plane[here(padded(row)), :] = scaled
        return (
            gain_sum + fold_rows(grad_norm * normal), shift_sum + fold_rows(grad_norm),
            scale_sum + fold_rows(kept * conv_s[at, :]), bias_sum + fold_rows(scaled),
        )

    gain_sum, shift_sum, scale_sum, bias_sum = loop(0, all_rows, sixth, (zero,) * 4, unroll=6)
    sum_ref[11:12, :] = row_sum(gain_sum)
    sum_ref[12:13, :] = row_sum(shift_sum)
    sum_ref[10:11, :] = row_sum(scale_sum)
    sum_ref[9:10, :] = row_sum(bias_sum)

    def seventh(row, carry):
        bias_bn, gain_bn = carry
        at = here(row)
        summed = rows.convolve(grad_plane, row, lambda index: aff(29 - index))
        summed = jnp.where(rows.inside(row), summed, 0.0)
        gbn_ref[at, :] = summed
        unit = (act_ref[at, :] - centre) * inverse_std
        return bias_bn + fold_rows(summed), gain_bn + fold_rows(summed * unit)

    bias_bn, gain_bn = loop(0, all_rows, seventh, (zero, zero), unroll=2)
    bn_ref[0:1, :] = row_sum(bias_bn)
    bn_ref[1:2, :] = row_sum(gain_bn)
    kernel_sums(rows, plane, grad_plane, images, sum_ref, 0)


def kernel_sums(rows, plane, grad_plane, images, sum_ref, base):
    zero = jnp.zeros((8, plane.shape[1]), F32)

    def body(row, carry):
        grad = grad_plane[here(padded(row)), :]
        grads = (rows.before(grad), grad, rows.after(grad))
        totals = list(carry)
        for down, source in enumerate(three_rows(plane, row)):
            for across in range(3):
                index = 3 * down + across
                totals[index] = totals[index] + fold_rows(grads[across] * source)
        return tuple(totals)

    totals = loop(0, images * GRID, body, (zero,) * 9)
    for index, total in enumerate(totals):
        sum_ref[base + index : base + index + 1, :] = row_sum(total)


def middle(
    images, extents, stats, stats_two, after_mix, act, up, w1, w2, aff, dhidden, branch_sums,
    later=(),
):
    tokens, width = after_mix.shape
    inner = w1.shape[1]
    full, low, wide = ((tokens, width), F32), ((tokens, width), BF16), ((tokens, inner), BF16)
    outs = [
        low, low, wide, wide, full, full, ((3, width), F32), ((19, width), F32), ((2, width), F32),
    ]
    return call(
        functools.partial(middle_kernel, images), "middle",
        [SMEM] + [VMEM] * (8 + 2 * images), outs,
        [
            pltpu.VMEM((tokens // images, inner), F32),
            pltpu.VMEM((tokens, width), F32), pltpu.VMEM((tokens, width), F32),
            pltpu.VMEM((tokens, 1), F32), pltpu.VMEM((tokens, width), F32),
            plane_of(images, width), plane_of(images, width),
        ], 18,
        (extents, stats, stats_two, after_mix, act, up, w1, w2, aff, *dhidden, *branch_sums), 3e10,
        4e7, later,
    )


def fed_grads_kernel(shift, bit_ref, norm_ref, hidlow_ref, ghid_ref, *refs):
    *gbranch_refs, out_ref = refs
    slots = gbranch_refs[0].shape[0]
    width = norm_ref.shape[1]
    pairs = out_ref.shape[0]
    size = ghid_ref.shape[1] // (2 * pairs)
    low = bit_ref[0] if shift == 0 else 1 - bit_ref[0]
    for pair in range(pairs):
        cols = pl.ds(pl.multiple_of((2 * pair + low) * size, 128), size)
        out_ref[pair, 0:size, :] = mul_tn(ghid_ref[:, cols], norm_ref[...])
        total = None
        for image, gbranch_ref in enumerate(gbranch_refs):
            span = slice(image * slots, (image + 1) * slots)
            part = mul_tn(hidlow_ref[span, cols], gbranch_ref[...])
            total = part if image == 0 else total + part
        out_ref[pair, size : 2 * size, :] = total


def fed_grads(shift, parts, bit, norm, hidlow, ghid, gbranch, later=()):
    width, inner = norm.shape[1], ghid.shape[1]
    return call(
        functools.partial(fed_grads_kernel, shift, bit), "fed_grads", [VMEM] * (3 + len(gbranch)),
        [((parts // 2, 2 * inner // parts, width), F32)], [], 6,
        (norm, hidlow, ghid, *gbranch), 3e9, 1e7, later,
    )[0]


def inner_back_kernel(
    images, extent_ref, total_ref, total_two_ref, batch_ref, act_ref, conv_ref, gbn_ref, glocal_ref, mix_ref,
    branch_ref, aff_ref, gmix_ref, gbranch_ref, sum_ref, bn_ref,
    normal_s, inverse_s, plane, grad_plane,
):
    tokens, width = act_ref.shape
    rows = Rows(extent_ref, width)
    clear_edges(plane, images)
    clear_edges(grad_plane, images)
    zero = jnp.zeros((8, width), F32)
    all_rows = images * GRID

    def aff(row):
        return aff_ref[row : row + 1, :]

    totals = total_ref[...] + total_two_ref[...]
    bn_ref[...] = totals
    centre, inverse_std, tally = batch_ref[0:1, :], batch_ref[1:2, :], batch_ref[2:3, :]
    bias_mean, gain_mean = totals[0:1, :] / tally, totals[1:2, :] / tally
    factor = aff(19) * inverse_std

    def first(row, total):
        at = here(row)
        unit = (act_ref[at, :] - centre) * inverse_std
        value = conv_ref[at, :]
        slope = normal_cdf(value) + value * density(value)
        grad = factor * (gbn_ref[at, :] - (bias_mean + unit * gain_mean)) * slope
        grad = jnp.where(rows.inside(row), grad, 0.0)
        grad_plane[here(padded(row)), :] = grad
        return total + fold_rows(grad)

    sum_ref[13:14, :] = row_sum(loop(0, all_rows, first, zero, unroll=4))

    def second(row, carry):
        at = here(row)
        normal, inverse = norm_rows(mix_ref[at, :])
        normal_s[at, :] = normal
        inverse_s[at, :] = inverse
        plane[here(padded(row)), :] = jnp.where(rows.inside(row), normal * aff(7) + aff(8), 0.0)
        return carry

    loop(0, all_rows, second, 0, unroll=8)
    kernel_sums(rows, plane, grad_plane, images, sum_ref, 4)

    def third(row, carry):
        summed = rows.convolve(grad_plane, row, lambda index: aff(17 - index))
        gmix_ref[here(row), :] = jnp.where(rows.inside(row), summed, 0.0)
        return carry

    loop(0, all_rows, third, 0, unroll=2)

    def fourth(row, carry):
        gain_sum, shift_sum, scale_sum, bias_sum = carry
        at = here(row)
        grad_norm, normal = gmix_ref[at, :], normal_s[at, :]
        grad = glocal_ref[at, :] + norm_back(grad_norm, normal, inverse_s[at, :], aff(7))
        gmix_ref[at, :] = grad
        kept = jnp.where(rows.inside(row), grad, 0.0)
        low = (kept * aff(6)).astype(BF16)
        gbranch_ref[at, :] = low
        return (
            gain_sum + fold_rows(grad_norm * normal), shift_sum + fold_rows(grad_norm),
            scale_sum + fold_rows(kept * branch_ref[at, :]), bias_sum + fold_rows(low.astype(F32)),
        )

    gain_sum, shift_sum, scale_sum, bias_sum = loop(0, all_rows, fourth, (zero,) * 4, unroll=6)
    sum_ref[0:1, :] = row_sum(bias_sum)
    sum_ref[1:2, :] = row_sum(scale_sum)
    sum_ref[2:3, :] = row_sum(gain_sum)
    sum_ref[3:4, :] = row_sum(shift_sum)


def inner_back(
    images, extents, totals, totals_two, batch, act, conv, gbn, glocal, after_mix, branch, aff,
    later=(),
):
    tokens, width = act.shape
    outs = [((tokens, width), F32), ((tokens, width), BF16), ((14, width), F32), ((2, width), F32)]
    return call(
        functools.partial(inner_back_kernel, images), "inner_back",
        [SMEM] + [VMEM] * 10, outs,
        [
            pltpu.VMEM((tokens, width), F32), pltpu.VMEM((tokens, 1), F32),
            plane_of(images, width), plane_of(images, width),
        ], 10,
        (extents, totals, totals_two, batch, act, conv, gbn, glocal, after_mix, branch, aff), 2e10, 3e7,
        later,
    )


def attention_back_kernel(
    image, extent_ref, sharp_ref, query_ref, key_ref, value_ref, inv_ref, cov_ref, attend_ref,
    gbranch_ref, wp_ref, gjoined, head_ref,
    gmixing, gscore, gquery, gkey,
):
    slots, width = gmixing.shape
    heads = sharp_ref.shape[0]
    head = width // heads
    rows = Rows(extent_ref, width)
    zero = jnp.zeros((8, width), F32)
    span = slice(image * slots, (image + 1) * slots)
    low, high = image * GRID, (image + 1) * GRID
    gmixing[...] = mul_nt(gbranch_ref[span, :], wp_ref[...])
    lane = lax.broadcasted_iota(jnp.int32, (1, width), 1)
    sharp_sum = jnp.zeros((1, width), F32)
    gscore[...] = mul_tn(gmixing[...], value_ref[span, :], HIGH)
    for group in range(heads):
        part = slice(group * head, (group + 1) * head)
        attend = attend_ref[image, part, :]
        grad = gscore[part, :]
        grad = attend * (grad - jnp.sum(attend * grad, axis=-1, keepdims=True))
        gscore[part, :] = grad * sharp_ref[group]
        amount = jnp.sum(
            jnp.sum(grad * cov_ref[image, part, :], axis=0, keepdims=True), axis=1, keepdims=True
        )
        sharp_sum = sharp_sum + jnp.where(lane == group, amount, 0.0)
    gquery[...] = mul_nt(key_ref[span, :], gscore[...], HIGH)
    gkey[...] = mul_nn(query_ref[span, :], gscore[...], HIGH)
    gmixing[...] = mul_nn(gmixing[...], attend_ref[image], HIGH)

    def first(row, carry):
        query_dot, key_dot = carry
        at = here(row)
        to = here(row - low)
        return (
            query_dot + fold_rows(gquery[to, :] * query_ref[at, :]),
            key_dot + fold_rows(gkey[to, :] * key_ref[at, :]),
        )

    query_dot, key_dot = loop(low, high, first, (zero, zero), unroll=2)
    query_dot, key_dot = row_sum(query_dot), row_sum(key_dot)
    query_inv = inv_ref[2 * image : 2 * image + 1, :]
    key_inv = inv_ref[2 * image + 1 : 2 * image + 2, :]

    def second(pair, carry):
        totals = list(carry)
        thirds = ([], [], [])
        for row in (2 * pair, 2 * pair + 1):
            at = here(row)
            to = here(row - low)
            inside = rows.inside(row)
            grad = query_inv * (gquery[to, :] - query_ref[at, :] * query_dot)
            thirds[0].append(jnp.where(inside, grad, 0.0))
            grad = key_inv * (gkey[to, :] - key_ref[at, :] * key_dot)
            thirds[1].append(jnp.where(inside, grad, 0.0))
            thirds[2].append(gmixing[to, :])
        to = pl.ds(pl.multiple_of((2 * pair - low) * GRID, 16), 2 * GRID)
        for third in range(3):
            value = jnp.concatenate(thirds[third], axis=0).astype(BF16)
            gjoined[to, third * width : (third + 1) * width] = value
            totals[third] = totals[third] + fold_rows(value.astype(F32))
        return tuple(totals)

    bias = loop(low // 2, high // 2, second, (zero,) * 3, unroll=2)
    put_rows(head_ref, [row_sum(total) for total in bias] + [sharp_sum])


def attention_back(
    images, image, extents, sharpness, query, key, value, inv, cov, attend, gbranch, wp, later=(),
):
    tokens, width = query.shape
    slots = tokens // images
    return call(
        functools.partial(attention_back_kernel, image), "attention_back",
        [SMEM] * 2 + [VMEM] * 8, [((slots, 3 * width), BF16), ((4, width), F32)],
        [
            pltpu.VMEM((slots, width), F32), pltpu.VMEM((width, width), F32),
            pltpu.VMEM((slots, width), F32), pltpu.VMEM((slots, width), F32),
        ], 8,
        (extents, sharpness, query, key, value, inv, cov, attend, gbranch, wp), 2e10, 2e7, later,
    )


def att_grads_kernel(
    bits_ref, norm_ref, mixing_ref, gbranch_ref, *refs
):
    *gjoined_refs, send_ref, keep_ref, matrix = refs
    slots = gjoined_refs[0].shape[0]
    width = norm_ref.shape[1]
    pairs = send_ref.shape[0]
    for image, gjoined_ref in enumerate(gjoined_refs):
        part = mul_tn(gjoined_ref[...], norm_ref[image * slots : (image + 1) * slots, :])
        rows = slice(0, 3 * width)
        matrix[rows, :] = part if image == 0 else matrix[rows, :] + part
    matrix[3 * width :, :] = mul_tn(mixing_ref[...], gbranch_ref[...])
    joined_rows, mixer_rows = 3 * width // (2 * pairs), width // (2 * pairs)
    for pair in range(pairs):
        for target, place in ((keep_ref, bits_ref[0]), (send_ref, 1 - bits_ref[0])):
            part = 2 * pair + place
            at = pl.ds(pl.multiple_of(part * joined_rows, 8), joined_rows)
            target[pair, 0:joined_rows, :] = matrix[at, :]
            at = pl.ds(pl.multiple_of(3 * width + part * mixer_rows, 8), mixer_rows)
            target[pair, joined_rows:, :] = matrix[at, :]


def att_grads(parts, bits, norm, mixing, gbranch, gjoined, later=()):
    width = norm.shape[1]
    share = ((parts // 2, 4 * width // parts, width), F32)
    return call(
        functools.partial(att_grads_kernel, bits), "att_grads", [VMEM] * (3 + len(gjoined)), [share, share],
        [pltpu.VMEM((4 * width, width), F32)], 8,
        (norm, mixing, gbranch, *gjoined), 2e9, 8e6, later,
    )


def outer_back_kernel(
    x_ref, gmix_ref, wq_ref, aff_ref, inner_ref, tail_ref, *refs
):
    *refs, incoming_ref, vector_ref, gnorm = refs
    images = len(refs) // 2
    gjoined_refs, head_refs = refs[:images], refs[images:]
    slots = gjoined_refs[0].shape[0]
    tokens, width = x_ref.shape
    zero = jnp.zeros((8, width), F32)
    for image, gjoined_ref in enumerate(gjoined_refs):
        gnorm[image * slots : (image + 1) * slots, :] = mul_nt(gjoined_ref[...], wq_ref[...])

    def body(step, carry):
        gain_sum, shift_sum = carry
        at = pl.ds(pl.multiple_of(step * 48, 16), 48)
        normal, inverse = norm_rows(x_ref[at, :].astype(F32))
        grad = gnorm[at, :]
        incoming_ref[at, :] = gmix_ref[at, :] + norm_back(grad, normal, inverse, aff_ref[0:1, :])
        return gain_sum + fold_rows(grad * normal), shift_sum + fold_rows(grad)

    gain_sum, shift_sum = loop(0, tokens // 48, body, (zero, zero), unroll=4)
    vector_ref[...] = jnp.zeros_like(vector_ref)
    vector_ref[0:1, :] = row_sum(gain_sum)
    vector_ref[1:2, :] = row_sum(shift_sum)
    head = sum(ref[...] for ref in head_refs[1:]) + head_refs[0][...]
    vector_ref[2:5, :] = head[0:3, :]
    vector_ref[5:19, :] = inner_ref[...]
    vector_ref[21:40, :] = tail_ref[...]
    vector_ref[40:41, :] = head[3:4, :]


def outer_back(source, gmix, wq, aff, inner, tail, gjoined, head, later=()):
    tokens, width = source.shape
    return call(
        outer_back_kernel, "outer_back", [VMEM] * (6 + 2 * len(head)),
        [((tokens, width), F32), ((SUM_ROWS, width), F32)], [pltpu.VMEM((tokens, width), F32)], 6,
        (source, gmix, wq, aff, inner, tail, *gjoined, *head), 5e9, 1e7, later,
    )


def row_blocks(rows):
    step = next(size for size in (32, 24, 16, 8, rows) if rows % size == 0)
    return rows // step, step


def blocks(rows, body):
    count, step = row_blocks(rows)

    def inner(index, carry):
        start = index * step
        body(pl.multiple_of(start, 8) if step % 8 == 0 else start, step)
        return carry

    loop(0, count, inner, 0)


def halve_first_kernel(
    high, side, bits_ref, held_ref, other_ref, send_high_ref, keep_high_ref, send_side_ref,
    keep_side_ref,
):
    half, quarter = send_high_ref.shape[0], send_side_ref.shape[1]
    high_bit, side_bit = bits_ref[high], bits_ref[side]

    def first(start, size):
        at = pl.ds(start, size)
        send_high_ref[at, :] = held_ref[1 - high_bit, at, :] + other_ref[1 - high_bit, at, :]
        keep_high_ref[at, :] = held_ref[high_bit, at, :] + other_ref[high_bit, at, :]

    def second(start, size):
        at = pl.ds(start, size)
        for target, bit in ((send_side_ref, 1 - side_bit), (keep_side_ref, side_bit)):
            here = pl.ds(pl.multiple_of(half + bit * quarter, 8) + start, size)
            for part in range(2):
                target[part, at, :] = held_ref[part, here, :] + other_ref[part, here, :]

    blocks(half, first)
    blocks(quarter, second)


def halve_first(bits, high, side, held, other, later=()):
    rows, width = held.shape[-2:]
    half, quarter = ((rows // 2, width), F32), ((2, rows // 4, width), F32)
    return call(
        functools.partial(halve_first_kernel, high, side, bits), "halve_first", [VMEM, VMEM],
        [half, half, quarter, quarter], [], 2, (held, other), held.size, 16 * held.size,
        later,
    )


def halve_second_kernel(
    high, side, bits_ref, one_ref, one_other_ref, two_ref, two_other_ref,
    send_one_ref, keep_one_ref, send_two_ref, keep_two_ref,
):
    quarter = send_one_ref.shape[0]
    high_bit, side_bit = bits_ref[high], bits_ref[side]

    def body(start, size):
        at = pl.ds(start, size)
        for target, bit in ((send_one_ref, 1 - side_bit), (keep_one_ref, side_bit)):
            here = pl.ds(pl.multiple_of(bit * quarter, 8) + start, size)
            target[at, :] = one_ref[here, :] + one_other_ref[here, :]
        for target, bit in ((send_two_ref, 1 - high_bit), (keep_two_ref, high_bit)):
            target[at, :] = two_ref[bit, at, :] + two_other_ref[bit, at, :]

    blocks(quarter, body)


def halve_second(bits, high, side, one, one_other, two, two_other, later=()):
    quarter = (two.shape[-2:], F32)
    return call(
        functools.partial(halve_second_kernel, high, side, bits), "halve_second", [VMEM] * 4,
         [quarter] * 4, [], 2,
        (one, one_other, two, two_other), one.size, 32 * one.size, later,
    )


def halve_third_kernel(
    place, bits_ref, one_ref, one_other_ref, two_ref, two_other_ref, send_ref, keep_ref
):
    bit = bits_ref[place]
    eighth = one_ref.shape[0] // 2

    def body(start, size):
        for target, half in ((send_ref, 1 - bit), (keep_ref, bit)):
            here = pl.ds(pl.multiple_of(half * eighth, 8) + start, size)
            target[pl.ds(start, size), :] = one_ref[here, :] + one_other_ref[here, :]
            target[pl.ds(eighth + start, size), :] = two_ref[here, :] + two_other_ref[here, :]

    blocks(eighth, body)


def halve_third(bits, place, one, one_other, two, two_other, later=()):
    return call(
        functools.partial(halve_third_kernel, place, bits), "halve_third", [VMEM] * 4,
        [(one.shape, F32)] * 2, [], 2, (one, one_other, two, two_other), one.size,
        32 * one.size, later,
    )


def split_add_kernel(place, bits_ref, held_ref, other_ref, send_ref, keep_ref):
    bit = bits_ref[place]

    def body(start, size):
        at = pl.ds(start, size)
        send_ref[at, :] = held_ref[1 - bit, at, :] + other_ref[1 - bit, at, :]
        keep_ref[at, :] = held_ref[bit, at, :] + other_ref[bit, at, :]

    blocks(send_ref.shape[0], body)


def split_add(bits, place, held, other, later=()):
    half = (held.shape[-2:], F32)
    return call(
        functools.partial(split_add_kernel, place, bits), "split_add", [VMEM, VMEM], [half, half],
        [], 2, (held, other), held.size, 16 * held.size, later,
    )


def add_kernel(held_ref, other_ref, out_ref):
    def body(start, size):
        at = pl.ds(start, size)
        out_ref[at, :] = held_ref[at, :] + other_ref[at, :]

    blocks(held_ref.shape[0], body)


def add(held, other, later=()):
    return call(
        add_kernel, "add_rows", [VMEM, VMEM], [(held.shape, F32)], [], 2, (held, other),
        held.size, 12 * held.size, later,
    )[0]


def append_kernel(held_ref, other_ref, rider_ref, rider_other_ref, out_ref):
    rows = held_ref.shape[0]

    def body(start, size):
        at = pl.ds(start, size)
        out_ref[at, :] = held_ref[at, :] + other_ref[at, :]

    blocks(rows, body)
    out_ref[rows:, :] = rider_ref[...] + rider_other_ref[...]


def append(held, other, rider, rider_other, later=()):
    rows, width = held.shape
    return call(
        append_kernel, "append_rows", [VMEM] * 4, [((rows + rider.shape[0], width), F32)], [], 2,
        (held, other, rider, rider_other), held.size, 12 * held.size, later,
    )[0]


def join_kernel(place, rider, bits_ref, held_ref, other_ref, out_ref):
    bit = bits_ref[place]
    rows = held_ref.shape[0] - rider

    def body(start, size):
        mine = pl.ds(pl.multiple_of(bit * rows, 8) + start, size)
        others = pl.ds(pl.multiple_of((1 - bit) * rows, 8) + start, size)
        out_ref[mine, :] = held_ref[pl.ds(start, size), :]
        out_ref[others, :] = other_ref[pl.ds(start, size), :]

    blocks(rows, body)
    if rider:
        out_ref[2 * rows :, :] = held_ref[rows:, :] + other_ref[rows:, :]


def join(bits, place, rider, held, other, later=()):
    rows, width = held.shape
    return call(
        functools.partial(join_kernel, place, rider, bits), "join_rows", [VMEM, VMEM],
        [((2 * rows - rider, width), F32)], [], 2, (held, other), held.size,
        16 * held.size, later,
    )[0]


def join_last_kernel(place, rider, bits_ref, held_ref, other_ref, out_ref, rider_ref):
    bit = bits_ref[place]
    rows = (held_ref.shape[0] - rider) // 4

    def body(start, size):
        for half in range(2):
            for following in range(2):
                source = pl.ds((2 * following + half) * rows + start, size)
                for side, ref in ((bit, held_ref), (1 - bit, other_ref)):
                    first = pl.multiple_of((4 * half + 2 * side + following) * rows, 8)
                    out_ref[pl.ds(first + start, size), :] = ref[source, :]

    blocks(rows, body)
    if rider:
        rider_ref[...] = held_ref[4 * rows :, :] + other_ref[4 * rows :, :]
    else:
        rider_ref[...] = jnp.zeros_like(rider_ref)


def join_last(bits, place, rider, held, other, later=()):
    rows, width = held.shape
    return call(
        functools.partial(join_last_kernel, place, rider, bits), "join_last", [VMEM, VMEM],
        [((2 * (rows - rider), width), F32), ((max(rider, 8), width), F32)], [], 2,
        (held, other), held.size, 16 * held.size, later,
    )


def upper_blocks(size):
    count = size // 128
    return [(row, column) for row in range(count) for column in range(row, count)]


def block(index):
    return slice(128 * index, 128 * index + 128)


def packed_rows(size, rider):
    return 128 * len(upper_blocks(size)) + rider * (size // 128)


def put_packed(target, source):
    for index, (row, column) in enumerate(upper_blocks(source.shape[0])):
        target[block(index), :] = source[block(row), block(column)]


def halves(source):
    high = source.astype(BF16)
    return high, (source - high.astype(F32)).astype(BF16)


def put_left(left, source):
    high, low = halves(source)
    size = source.shape[1]
    left[:, 0:size], left[:, size : 2 * size], left[:, 2 * size :] = high, high, low


def put_right(right, columns, source):
    high, low = halves(source)
    size = source.shape[0]
    right[0:size, columns], right[size : 2 * size, columns] = high, low
    right[2 * size :, columns] = high


def sweeps_kernel(mine_ref, other_ref, out_ref, now, total, left, right, step):
    size = out_ref.shape[0]
    for index, (row, column) in enumerate(upper_blocks(size)):
        part = mine_ref[block(index), :] + other_ref[block(index), :]
        now[block(row), block(column)] = part
        if row != column:
            now[block(column), block(row)] = part.T
    row = lax.broadcasted_iota(jnp.int32, (size, size), 0)
    diagonal = row == lax.broadcasted_iota(jnp.int32, (size, size), 1)
    trace = jnp.where(diagonal, now[...], 0.0)
    trace = jnp.sum(jnp.sum(trace, axis=0, keepdims=True), axis=1, keepdims=True)
    norm = jnp.sqrt(trace) + frob_eps
    now[...] = now[...] / (norm * norm)
    near, far = slice(0, size), slice(size, 2 * size)
    for sweep_index in range(NS_STEPS):
        last = sweep_index == NS_STEPS - 1
        put_left(left, now[...])
        put_right(right, near, now[...])
        square = mul_nn(left[...], right[:, near])
        step[...] = (
            jnp.where(diagonal, coef_first, 0.0) + coef_second * now[...] + coef_third * square
        )
        put_left(left, step[...])
        if sweep_index == 0:
            total[...] = step[...] / norm
            now[...] = mul_nn(left[...], right[:, near])
        elif last:
            put_right(right, near, total[...])
            out_ref[...] = mul_nn(left[...], right[:, near])
        else:
            put_right(right, far, total[...])
            both = mul_nn(left[...], right[...])
            now[...] = both[:, near]
            total[...] = both[:, far]
        if not last:
            put_right(right, near, now[...])
            now[...] = mul_nn(left[...], right[:, near])


def sweeps(width, mine, other, later=()):
    square = pltpu.VMEM((width, width), F32)
    return call(
        sweeps_kernel, "sweeps", [VMEM, VMEM], [((width, width), F32)],
        [
            square, square, pltpu.VMEM((width, 3 * width), BF16),
            pltpu.VMEM((3 * width, 2 * width), BF16), square,
        ], 9, (mine, other), 1e10, 4e6, later,
    )[0]


def prepare_kernel(
    turned, rider, bit_ref, share_ref, first_ref, second_ref, rider_ref,
    grad_one_ref, grad_two_ref, state_one_ref, state_two_ref, send_ref, keep_ref,
):
    split = first_ref.shape[0 if turned else 1]
    tall = second_ref.shape[0]
    grad_one = share_ref[0:split, :]
    grad_one_ref[...] = grad_one if turned else grad_one.T
    state_one_ref[...] = velocity_damping * first_ref[...] + grad_one_ref[...]
    grad_two_ref[...] = share_ref[split : split + tall, :]
    state_two_ref[...] = velocity_damping * second_ref[...] + grad_two_ref[...]
    gram = mul_tn if turned else mul_nt
    gram_one = gram(state_one_ref[...], state_one_ref[...], HIGH)
    gram_two = mul_tn(state_two_ref[...], state_two_ref[...], HIGH)
    even = bit_ref[0] == 0
    width = share_ref.shape[1]
    put_packed(keep_ref, jnp.where(even, gram_one, gram_two))
    put_packed(send_ref, jnp.where(even, gram_two, gram_one))
    if rider:
        for column in range(width // 128):
            first = packed_rows(width, 0) + column * rider
            keep_ref[first : first + rider, :] = rider_ref[:, block(column)]
            send_ref[first : first + rider, :] = rider_ref[:, block(column)]


def prepare(turned, rider, bit, share, first, second, rows, later=()):
    width = share.shape[1]
    upper = ((packed_rows(width, rider), 128), F32)
    one, two = (first.shape, F32), (second.shape, F32)
    return call(
        functools.partial(prepare_kernel, turned, rider, bit), "prepare", [VMEM] * 4,
        [one, two, one, two, upper, upper], [], 8, (share, first, second, rows), 2e9, 6e6, later,
    )


def renew_kernel(
    turned, factors, bit_ref, mine_ref, other_ref, state_one_ref, state_two_ref, one_ref, two_ref,
    new_one_ref, new_two_ref, low_one_ref, low_two_ref,
):
    even = bit_ref[0] == 0
    poly_one = jnp.where(even, mine_ref[...], other_ref[...])
    poly_two = jnp.where(even, other_ref[...], mine_ref[...])
    if turned:
        field_one = mul_nn(state_one_ref[...], poly_one, HIGH)
    else:
        field_one = mul_nn(poly_one, state_one_ref[...], HIGH)
    new_one = one_ref[...] - (rate_matrix * factors[0]) * field_one
    new_one_ref[...] = new_one
    low_one_ref[...] = new_one.astype(BF16)
    new_two = two_ref[...] - (rate_matrix * factors[1]) * mul_nn(
        state_two_ref[...], poly_two, HIGH
    )
    new_two_ref[...] = new_two
    low_two_ref[...] = new_two.astype(BF16)


def renew(
    turned, factors, bit, mine, other, state_one, state_two, one, two, later=(),
):
    outs = [(one.shape, F32), (two.shape, F32), (one.shape, BF16), (two.shape, BF16)]
    return call(
        functools.partial(renew_kernel, turned, factors, bit), "renew", [VMEM] * 6, outs, [],
        8, (mine, other, state_one, state_two, one, two), 2e9, 6e6, later,
    )


def vectors_kernel(
    start, rider, held_ref, other_ref, bn_ref, batch_ref, aff_ref, aff_velocity_ref, sharp_ref,
    sharp_velocity_ref, full_ref, sharp_sum_ref, new_aff_ref, aff_state_ref, new_sharp_ref,
    sharp_state_ref,
):
    rows, width = aff_ref.shape
    group = sharp_ref.shape[1]
    for column in range(width // 128):
        first = start + column * rider
        total = held_ref[first : first + rider, :] + other_ref[first : first + rider, :]
        full_ref[:, block(column)] = total[0:rows, :]
        if column == 0:
            sharp_sum_ref[...] = total[rows : rows + 1, 0:group]
    full_ref[rows // 2 - 1 : rows // 2, :] = bn_ref[1:2, :]
    full_ref[rows // 2 : rows // 2 + 1, :] = bn_ref[0:1, :]
    step_size = affine_step_size * lax.rsqrt(batch_ref[2:3, :])
    state = velocity_damping * aff_velocity_ref[...] + full_ref[...]
    aff_state_ref[...] = state
    new_aff_ref[...] = aff_ref[...] - step_size * state
    state = velocity_damping * sharp_velocity_ref[...] + sharp_sum_ref[...]
    sharp_state_ref[...] = state
    new_sharp_ref[...] = sharp_ref[...] - step_size[:, 0:group] * state


def vectors(
    width, rider, held, other, bn_totals, batch, aff, aff_velocity, sharp, sharp_velocity,
    later=(),
):
    start = packed_rows(width, 0)
    sharp, sharp_velocity = sharp[None], sharp_velocity[None]
    large, small = (aff.shape, F32), (sharp.shape, F32)
    return call(
        functools.partial(vectors_kernel, start, rider), "vectors", [VMEM] * 8,
        [large, small, large, large, small, small], [], 2,
        (held, other, bn_totals, batch, aff, aff_velocity, sharp, sharp_velocity), 0, 0, later,
    )


def bits_of(size):
    return [1 << place for place in range(size.bit_length() - 1)]


def swap(source, axis, bit):
    size = lax.axis_size(axis)
    return lax.ppermute(source, axis, [(member, member ^ bit) for member in range(size)])


def axis_steps(axis):
    base = 0 if axis == "narrow" else len(bits_of(lax.axis_size("narrow")))
    return [(axis, bit, base + place) for place, bit in enumerate(bits_of(lax.axis_size(axis)))]


def all_steps():
    return axis_steps("narrow") + axis_steps("wide")


class OwnBits:
    def __init__(self):
        self.steps = all_steps()

    def __getitem__(self, place):
        axis, bit, _ = self.steps[place]
        return lax.rem(lax.div(lax.axis_index(axis), bit), 2)


class Line:
    def __init__(self):
        self.last = ()

    def __call__(self, kernel, *args):
        out = kernel(*args, later=self.last)
        self.last = (out[-1] if isinstance(out, (list, tuple)) else out,)
        return out


def everyone(line, rows, combine, fillers=()):
    fillers = list(fillers)
    steps = all_steps()
    for axis, bit, _ in steps[:-1]:
        other = swap(rows, axis, bit)
        if axis != "narrow" or bit > 1:
            if fillers:
                fillers.pop(0)()
        rows = line(combine, rows, other)
    axis, bit, _ = steps[-1]
    other = swap(rows, axis, bit)
    for filler in fillers:
        filler()
    return rows, other


class Sum:
    def __init__(self, line, bits, send, keep):
        self.line, self.bits, self.keep = line, bits, keep
        (_, self.low, _), (_, self.high, self.high_place) = axis_steps("narrow")
        _, self.side, self.side_place = axis_steps("wide")[0]
        self.rest = axis_steps("wide")[1:]
        self.other = swap(send, "narrow", self.low)
        self.rider = 0

    def first(self):
        send, self.one, send_two, self.two = self.line(
            halve_first, self.bits, self.high_place, self.side_place, self.keep, self.other
        )
        self.one_other = swap(send, "narrow", self.high)
        self.two_other = swap(send_two, "wide", self.side)

    def second(self):
        send, self.one, send_two, self.two = self.line(
            halve_second, self.bits, self.high_place, self.side_place, self.one, self.one_other,
            self.two, self.two_other,
        )
        self.one_other = swap(send, "wide", self.side)
        self.two_other = swap(send_two, "narrow", self.high)

    def third(self):
        axis, bit, place = self.rest[0]
        send, self.keep = self.line(
            halve_third, self.bits, place, self.one, self.one_other, self.two, self.two_other
        )
        self.other = swap(send, axis, bit)
        self.done = 1

    def more(self):
        axis, bit, place = self.rest[self.done]
        shape = self.keep.shape
        self.done += 1
        if self.done < len(self.rest):
            keep, other = (array.reshape(2, -1, shape[1]) for array in (self.keep, self.other))
            send, self.keep = self.line(split_add, self.bits, place, keep, other)
            self.other = swap(send, axis, bit)
        else:
            self.keep = self.line(add, self.keep, self.other)
            self.other = swap(self.keep, axis, bit)

    def mores(self):
        while self.done < len(self.rest):
            self.more()

    def last_step(self):
        axis, bit, _ = self.rest[-1]
        return axis, bit

    def turn(self, rider=None):
        if rider is None:
            self.held = self.line(add, self.keep, self.other)
        else:
            self.held = self.line(append, self.keep, self.other, *rider)
            self.rider = rider[0].shape[0]
        self.place = len(self.rest) - 1
        self.back_move()

    def back_move(self):
        self.place -= 1
        axis, bit, _ = self.rest[self.place] if self.place >= 0 else axis_steps("wide")[0]
        self.other = swap(self.held, axis, bit)

    def back(self):
        _, _, place = self.rest[self.place]
        self.held = self.line(join, self.bits, place, self.rider, self.held, self.other)
        self.back_move()

    def backs(self):
        while self.place >= 0:
            self.back()

    def last(self):
        return self.line(
            join_last, self.bits, self.side_place, self.rider, self.held, self.other
        )


class Update:
    def __init__(self, line, turned, bits, gathered, states, rider=0):
        share, rows = gathered
        self.line, self.turned, self.bits = line, turned, bits
        self.width = share.shape[1]
        *self.grads, self.one, self.two, send, self.keep = line(
            prepare, turned, rider, bits, share, *states, rows
        )
        self.other = swap(send, "narrow", 1)

    def across(self):
        (axis, bit, _) = axis_steps("narrow")[1]
        self.keep = self.line(add, self.keep, self.other)
        self.other = swap(self.keep, axis, bit)
        self.sums = (self.keep, self.other)

    def sweep(self):
        self.keep = self.line(sweeps, self.width, self.keep, self.other)
        self.other = swap(self.keep, "narrow", 1)

    def renew(self, factors, masters):
        new = self.line(
            renew, self.turned, factors, self.bits, self.keep, self.other, self.one, self.two,
            *masters,
        )
        return self.grads + [self.one, self.two] + list(new)


def on_device(
    block_source,
    upstream_adjoint,
    picture_patch_extents,
    triple_matrix,
    mixer_matrix,
    expand_matrix,
    shrink_matrix,
    affine_entries,
    sharpness,
    triple_velocity,
    mixer_velocity,
    expand_velocity,
    shrink_velocity,
    affine_velocity,
    sharpness_velocity,
):
    images, slot_count, model_width = block_source.shape
    group_index = sharpness.shape[0]
    narrow_parts = lax.axis_size("narrow")
    narrow_pos = lax.axis_index("narrow")
    bits = OwnBits()
    source = block_source.reshape(-1, model_width)
    above = upstream_adjoint.reshape(-1, model_width)

    def own_part(full_matrix, along):
        part_size = full_matrix.shape[along] // narrow_parts
        return lax.dynamic_slice_in_dim(full_matrix, narrow_pos * part_size, part_size, along)

    (
        norm_one, query, key, value, inv, cov, attend, mixing, branch, after_mix, conv_one, act,
        stats,
    ) = front(
        images, picture_patch_extents, sharpness, source, triple_matrix, mixer_matrix,
        affine_entries,
    )
    line = Line()
    low_weights, backs = [], []

    def lower(matrix):
        low_weights.append(line(cast, matrix))

    def from_above():
        backs.append(
            line(
                upstream, images, len(backs), picture_patch_extents, above, low_weights[0],
                affine_entries,
            )
        )

    stats, stats_two = everyone(
        line, stats, merge,
        (lambda: lower(shrink_matrix), lambda: lower(expand_matrix))
        + (from_above,) * images,
    )
    shrink_low, expand_low = low_weights
    grad_branch3, grad_above, branch_sums = zip(*backs)
    (
        block_out, norm_three, hidden_low, grad_hidden, grad_local, grad_bn, batch, tail_sums,
        bn_sums,
    ) = line(
        middle, images, picture_patch_extents, stats, stats_two, after_mix, act, above,
        expand_low, shrink_low, affine_entries, grad_above, branch_sums,
    )
    fed_halves = []

    def fed_half():
        fed_halves.append(
            line(
                fed_grads, 1 - len(fed_halves), narrow_parts, bits, norm_three, hidden_low,
                grad_hidden, grad_branch3,
            )
        )

    bn_sums, bn_two = everyone(line, bn_sums, add, (fed_half, fed_half))
    fed = Sum(line, bits, *fed_halves)
    fed.first()
    grad_mix, grad_branch1, inner_sums, bn_totals = line(
        inner_back, images, picture_patch_extents, bn_sums, bn_two, batch, act, conv_one, grad_bn,
        grad_local, after_mix, branch, affine_entries,
    )
    fed.second()
    mixer_low = mixer_matrix.astype(BF16)
    backs = []
    for image in range(images):
        backs.append(
            line(
                attention_back, images, image, picture_patch_extents, sharpness, query, key,
                value, inv, cov, attend, grad_branch1, mixer_low,
            )
        )
        if image == 0:
            fed.third()
    grad_joined, head_sums = zip(*backs)
    fed.mores()
    att_send, att_keep = line(
        att_grads, narrow_parts, bits, norm_one, mixing, grad_branch1, grad_joined
    )
    att = Sum(line, bits, att_send, att_keep)
    incoming_adjoint, vector_sums = line(
        outer_back, source, grad_mix, triple_matrix.astype(BF16), affine_entries, inner_sums,
        tail_sums, grad_joined, head_sums,
    )
    rider = (vector_sums, swap(vector_sums, *fed.last_step()))
    full_weights = (triple_matrix, mixer_matrix, expand_matrix, shrink_matrix)
    factors = [math.sqrt(max(1.0, full.shape[0] / full.shape[1])) for full in full_weights]
    masters = (
        own_part(triple_matrix, 1).T, own_part(mixer_matrix, 0), own_part(expand_matrix, 1),
        own_part(shrink_matrix, 0),
    )
    att.first()
    fed.turn(rider)
    att.second()
    att.third()
    fed.backs()
    att.mores()
    att.turn()
    att.backs()
    fed = Update(line, False, bits, fed.last(), (expand_velocity, shrink_velocity), SUM_ROWS)
    att = Update(line, True, bits, att.last(), (triple_velocity.T, mixer_velocity))
    fed.across()
    att.across()
    fed.sweep()
    line.last += masters
    att.sweep()
    vector_outs = line(
        vectors, model_width, SUM_ROWS, *fed.sums, bn_totals, batch, affine_entries,
        affine_velocity, sharpness, sharpness_velocity,
    )
    fed = fed.renew(factors[2:], masters[2:])
    att = att.renew(factors[:2], masters[:2])
    vec_full, sharpness_sum, new_vec, vec_state, sharpness_following, sharpness_buffer = (
        vector_outs
    )
    sharpness_sum, sharpness_following, sharpness_buffer = (
        row.reshape(-1) for row in (sharpness_sum, sharpness_following, sharpness_buffer)
    )
    for member in (0, 2, 4, 6):
        att[member] = att[member].T
    return (
        block_out.reshape(block_source.shape),
        incoming_adjoint.reshape(block_source.shape),
        att[0],
        att[1],
        fed[0],
        fed[1],
        vec_full,
        sharpness_sum,
        att[4],
        att[5],
        fed[4],
        fed[5],
        att[2],
        att[3],
        fed[2],
        fed[3],
        att[6],
        att[7],
        fed[6],
        fed[7],
        new_vec,
        vec_state,
        sharpness_following,
        sharpness_buffer,
    )


def solution(mesh):
    return jax.shard_map(
        on_device,
        mesh=mesh,
        in_specs=(
            P(("wide", "narrow"), None, None),
            P(("wide", "narrow"), None, None),
            P(("wide", "narrow"), None),
            P(),
            P(),
            P(),
            P(),
            P(),
            P(),
            P(None, "narrow"),
            P("narrow", None),
            P(None, "narrow"),
            P("narrow", None),
            P(),
            P(),
        ),
        out_specs=(
            P(("wide", "narrow"), None, None),
            P(("wide", "narrow"), None, None),
            P(None, "narrow"),
            P("narrow", None),
            P(None, "narrow"),
            P("narrow", None),
            P(),
            P(),
            P(None, "narrow"),
            P("narrow", None),
            P(None, "narrow"),
            P("narrow", None),
            P(None, "narrow"),
            P("narrow", None),
            P(None, "narrow"),
            P("narrow", None),
            P(None, "narrow"),
            P("narrow", None),
            P(None, "narrow"),
            P("narrow", None),
            P(),
            P(),
            P(),
            P(),
        ),
        check_vma=False,
    )
```
